32 devices in a mesh: dp: 8 (over z, y), head: 2 (over core), sub: 2 (over x).
Axes of the slice: x: 2, y: 2, z: 4, core: 2. Of those that a mesh axis runs over, the one named last changes fastest.
Arguments:
- queries: bfloat16 [2, 4096, 4096], P('sub', 'dp', 'head'), may hold values from -6 to 6
- key_states: bfloat16 [4096, 1024], P('dp', 'head'), may hold values from -6 to 6
- value_states: bfloat16 [4096, 1024], P('dp', 'head'), may hold values from -6 to 6
- out_grad: bfloat16 [2, 4096, 4096], P('sub', 'dp', 'head'), may hold values from -6 to 6
- seg_ids: int32 [4096], P('dp'), may hold values from -1 to 7, as said below
- handed: int32 [8], replicated, may hold values from 0 to 256, as said below
Outputs:
- attended: bfloat16 [2, 4096, 4096], P('sub', 'dp', 'head')
- query_grad: bfloat16 [2, 4096, 4096], P('sub', 'dp', 'head')
- key_grad: bfloat16 [4096, 1024], P('dp', ('head', 'sub'))
- value_grad: bfloat16 [4096, 1024], P('dp', ('head', 'sub'))
The draws below stay inside these ranges and needn't reach their ends.
Inputs may be any that keep to these rules, and one draw needn't show every extreme that they name: `seg_ids`: within a block of 512 slots, live slots come first and numbers never fall; slots of one sequence are contiguous; the first 4 blocks are full, and block 0 holds eight sequences. handed[i] for i < 4 is at least 1 and starts a sequence of block i at slot 512 - handed[i]; it is 0 for the other half. Block i + 4 has at most 512 - handed[i] live slots. handed[0] is 256, and block 4 is exactly full after receiving.
All inputs are finite; a program needn't handle non-finite values.
Results may differ from the reference program's by a relative error of at most 0.022.
Values may be sent and summed in bfloat16 or wider, within the bound.
No kernel may reach another device: no remote copies, remote signals or barrier semaphores. Data moves between devices by JAX's collectives and lax.ppermute only.
A program may use at most 64 MiB of HBM per device.

```python
import jax
import jax.numpy as jnp
from jax import lax

HQ = 64
KVH = 8
HD = 128
TOK_DEV = 512
TOKENS = 4096
N_DP = 8


def sequence_layout(key):
    folded_key = jax.random.fold_in(key, 7)
    key_parts = jax.random.split(folded_key, 4)
    halfway = N_DP // 2
    capacity = TOK_DEV // 2
    boundary = jax.random.randint(key_parts[0], (halfway,), capacity, TOK_DEV)
    boundary = boundary.at[0].set(capacity)
    moved_rows = TOK_DEV - boundary
    filled = jax.random.randint(key_parts[1], (halfway,), 1, TOK_DEV - moved_rows + 1)
    filled = filled.at[0].set(TOK_DEV - moved_rows[0])
    live_rows = jnp.concatenate([jnp.full((halfway,), TOK_DEV, jnp.int32), filled.astype(jnp.int32)])
    forced = jnp.concatenate([boundary.astype(jnp.int32), jnp.full((halfway,), TOK_DEV, jnp.int32)])
    cut_rows = jax.random.randint(key_parts[2], (N_DP, 6), 1, TOK_DEV)
    leading = jax.random.permutation(key_parts[3], capacity - 1)[:6] + 1
    cut_rows = cut_rows.at[0].set(leading.astype(cut_rows.dtype))
    row_index = jnp.arange(TOK_DEV, dtype=jnp.int32)
    starts = jnp.any(row_index[None, :, None] == cut_rows[:, None, :], axis=-1) | (row_index[None, :] == 0) | (row_index[None, :] == forced[:, None])
    numbers = jnp.cumsum(starts.astype(jnp.int32), axis=1) - 1
    numbers = jnp.where(row_index[None, :] < live_rows[:, None], numbers, -1)
    handed = jnp.concatenate([moved_rows.astype(jnp.int32), jnp.zeros((halfway,), jnp.int32)])
    return (numbers.astype(jnp.int32), handed)


def draw_seg_ids(key, part):
    return sequence_layout(key)[0].reshape(TOKENS)


def draw_handed(key, part):
    return sequence_layout(key)[1]


def draw_queries(key, part):
    drawn = jnp.clip(jax.random.normal(jax.random.fold_in(key, 41), (2, TOKENS, HQ // 2 * HD), jnp.float32), -6.0, 6.0)
    return drawn.astype(jnp.bfloat16)


def draw_key_states(key, part):
    drawn = jnp.clip(jax.random.normal(jax.random.fold_in(key, 43), (TOKENS, KVH, HD), jnp.float32), -6.0, 6.0)
    return drawn.reshape(TOKENS, KVH * HD).astype(jnp.bfloat16)


def block_levels(key, shape, cuts, low, top_value):
    def one(dim, shards_of):
        heights = jax.random.uniform(jax.random.fold_in(jax.random.fold_in(key, 6), dim), (shards_of,), jnp.float32, low / len(cuts), top_value / len(cuts))
        return jnp.repeat(jnp.exp(heights), shape[dim] // shards_of).reshape((-1,) + (1,) * (len(shape) - dim - 1))

    factor_of = one(*cuts[0])
    for cut in cuts[1:]:
        factor_of = factor_of * one(*cut)
    return factor_of


def noise(key, dims, scale, reach, shards=(), kind=jnp.bfloat16):
    result = jax.random.normal(key, dims, jnp.float32) * scale
    if len(shards) > 0:
        result = block_levels(key, dims, shards, -0.22, 0.18) * result
    return jnp.clip(result, min=-reach, max=reach).astype(kind)


def setup_inputs(seed: int = 0) -> dict:
    key_list = jax.random.split(jax.random.key(seed), 7)
    queries = draw_queries(jax.random.fold_in(key_list[6], 71), 0)
    key_states = draw_key_states(jax.random.fold_in(key_list[6], 71), 0)
    value_states = noise(key_list[2], (TOKENS, KVH * HD), 1.0, 6.0, ((0, 8), (1, 2)))
    out_grad = noise(key_list[3], (2, TOKENS, HQ // 2 * HD), 1.0, 6.0, ((0, 2), (1, 8), (2, 2)))
    seg_ids = draw_seg_ids(jax.random.fold_in(key_list[6], 71), 0)
    handed = draw_handed(jax.random.fold_in(key_list[6], 71), 0)
    return dict(queries=queries, key_states=key_states, value_states=value_states, out_grad=out_grad, seg_ids=seg_ids, handed=handed)


masked_value = -1e30


def through_bf16(values):
    return lax.optimization_barrier(values.astype(jnp.bfloat16)).astype(jnp.float32)


def one_device(pieces):
    query_block, key_block, value_block, grad_block, segment = pieces
    length = segment.shape[0]
    scaling = HD ** -0.5
    precise = lax.Precision.HIGHEST
    query_f = query_block.astype(jnp.float32)
    key_f = key_block.astype(jnp.float32)
    value_f = value_block.astype(jnp.float32)
    grad_f = grad_block.astype(jnp.float32)
    scores = jnp.einsum("stgjd,ugd->sgjtu", query_f, key_f, precision=precise) * scaling
    row_index = jnp.arange(length, dtype=jnp.int32)
    allowed = (segment[:, None] == segment[None, :]) & (row_index[None, :] <= row_index[:, None]) & (segment[:, None] >= 0)
    scores = jnp.where(allowed, scores, masked_value)
    row_top = jnp.max(scores, axis=-1, keepdims=True)
    log_total = row_top + jnp.log(jnp.sum(jnp.exp(scores - row_top), axis=-1, keepdims=True))
    probabilities = jnp.where(allowed, jnp.exp(scores - log_total), 0.0)
    weights = through_bf16(probabilities)
    attended = jnp.einsum("sgjtu,ugd->stgjd", weights, value_f, precision=precise).astype(jnp.bfloat16)
    row_delta = jnp.einsum("stgjd,stgjd->sgjt", grad_f, attended.astype(jnp.float32), precision=precise)
    prob_grad = jnp.einsum("stgjd,ugd->sgjtu", grad_f, value_f, precision=precise)
    score_grad = through_bf16(probabilities * (prob_grad - row_delta[..., None]))
    query_grad = (jnp.einsum("sgjtu,ugd->stgjd", score_grad, key_f, precision=precise) * scaling).astype(jnp.bfloat16)
    key_grad = (jnp.einsum("sgjtu,stgjd->ugd", score_grad, query_f, precision=precise) * scaling).astype(jnp.bfloat16)
    value_grad = jnp.einsum("sgjtu,stgjd->ugd", weights, grad_f, precision=precise).astype(jnp.bfloat16)
    return attended, query_grad, key_grad, value_grad


def relayout(before, segment_rows, handed):
    devices = segment_rows.shape[0]
    length = segment_rows.shape[1]
    halfway = devices // 2
    device_index = jnp.arange(devices, dtype=jnp.int32)
    sender = device_index < halfway
    partner = jnp.where(sender, device_index, device_index - halfway).astype(jnp.int32)
    live_rows = jnp.sum((segment_rows >= 0).astype(jnp.int32), axis=1)
    kept_count = jnp.where(sender, length - handed, live_rows)
    added_count = jnp.where(sender, 0, handed[partner])
    row_index = jnp.arange(length, dtype=jnp.int32)
    source_row = jnp.clip(length - added_count[:, None] + row_index[None, :] - kept_count[:, None], 0, length - 1).astype(jnp.int32)
    moved_rows = before[partner[:, None], source_row]
    extra_dims = (1,) * (before.ndim - 2)
    own_mask = (row_index[None, :] < kept_count[:, None]).reshape((devices, length) + extra_dims)
    new_mask = (row_index[None, :] < (kept_count + added_count)[:, None]).reshape((devices, length) + extra_dims)
    return jnp.where(own_mask, before, jnp.where(new_mask, moved_rows, jnp.zeros((), before.dtype)))


def reference(queries, key_states, value_states, out_grad, seg_ids, handed):
    per_group = HQ // KVH // 2
    query_split = jnp.moveaxis(queries.reshape(2, N_DP, TOK_DEV, KVH, per_group, HD), 1, 0)
    grad_split = jnp.moveaxis(out_grad.reshape(2, N_DP, TOK_DEV, KVH, per_group, HD), 1, 0)
    key_split = key_states.reshape(N_DP, TOK_DEV, KVH, HD)
    value_split = value_states.reshape(N_DP, TOK_DEV, KVH, HD)
    segment_rows = seg_ids.reshape(N_DP, TOK_DEV)
    attended, query_grad, key_grad, value_grad = lax.map(one_device, (query_split, key_split, value_split, grad_split, segment_rows))
    attended = relayout(jnp.moveaxis(attended, 1, 2), segment_rows, handed)
    query_grad = relayout(jnp.moveaxis(query_grad, 1, 2), segment_rows, handed)
    key_grad = relayout(key_grad, segment_rows, handed)
    value_grad = relayout(value_grad, segment_rows, handed)
    attended = jnp.moveaxis(attended, 2, 0).reshape(2, TOKENS, HQ // 2 * HD)
    query_grad = jnp.moveaxis(query_grad, 2, 0).reshape(2, TOKENS, HQ // 2 * HD)
    return attended, query_grad, key_grad.reshape(TOKENS, KVH * HD), value_grad.reshape(TOKENS, KVH * HD)
```

```python
import functools

import jax
import jax.numpy as jnp
from jax import lax
from jax.experimental import pallas as pl
from jax.experimental.pallas import tpu as pltpu
from jax.sharding import PartitionSpec as P

HD = 128
LOG2E = 1.4426950408889634
MASKED = -1e30
NT = (((1,), (1,)), ((), ()))
NN = (((1,), (0,)), ((), ()))


def dot(a, b, dims):
    return lax.dot_general(a, b, dims, preferred_element_type=jnp.float32)


def fill_bias(seg_ref, bias_ref, keys, first_row, rows):
    seg_keys = seg_ref[0:1, 0:keys].astype(jnp.float32)
    key_seg = jnp.transpose(jnp.broadcast_to(seg_keys, (HD, keys)))
    for begin in range(0, rows, HD):
        row_seg = seg_ref[0:1, first_row + begin : first_row + begin + HD].astype(jnp.float32)
        key_index = lax.broadcasted_iota(jnp.int32, (keys, HD), 0)
        row_index = lax.broadcasted_iota(jnp.int32, (keys, HD), 1) + (first_row + begin)
        allowed = (key_seg == row_seg) & (key_index <= row_index)
        bias_ref[:, begin : begin + HD] = jnp.where(allowed, 0.0, MASKED)


def attend_group(q_ref, do_ref, k, v, bias_ref, live, per_group, emit):
    scale = HD**-0.5
    k_t = jnp.transpose(k)
    v_t = jnp.transpose(v)
    dk = None
    dv = None
    for j in range(per_group):
        q = q_ref[:, j * HD : (j + 1) * HD]
        do = do_ref[:, j * HD : (j + 1) * HD]
        x = dot(k, q, NT) * (scale * LOG2E) + bias_ref[...]
        p = jnp.exp2(x - jnp.max(x, axis=0, keepdims=True))
        inverse = jnp.where(live, 1.0 / jnp.sum(p, axis=0, keepdims=True), 0.0)
        w = p * inverse
        wb = w.astype(jnp.bfloat16)
        dp = dot(v, do, NT)
        delta = jnp.sum(w * dp, axis=0, keepdims=True)
        ds = (w * (dp - delta)).astype(jnp.bfloat16)
        out = jnp.transpose(dot(v_t, wb, NN)).astype(jnp.bfloat16)
        dq = jnp.transpose(dot(k_t, ds, NN) * scale).astype(jnp.bfloat16)
        emit(j, out, dq)
        dv_j = dot(wb, do, NN)
        dk_j = dot(ds, q, NN)
        dv = dv_j if dv is None else dv + dv_j
        dk = dk_j if dk is None else dk + dk_j
    return dk * scale, dv


def kept_limit(handed_ref, length):
    return length - handed_ref[lax.axis_index("dp")]


def tail_kernel(length, per_group, aliased, handed_ref, side_ref, q_ref, do_ref, k_ref, v_ref, seg_ref, *refs):
    refs = refs[aliased:]
    out_ref, dq_ref, send_ref, tail_ref, head_ref, bias_ref = refs
    half = length // 2
    width = per_group * HD

    @pl.when(pl.program_id(0) == 0)
    def _():
        fill_bias(seg_ref, bias_ref, length, half, half)

    live = seg_ref[0:1, half:length] >= 0
    keep = lax.broadcasted_iota(jnp.int32, (half, HD), 0) + half < kept_limit(handed_ref, length)

    def emit(j, out, dq):
        columns = slice(j * HD, (j + 1) * HD)
        zero = jnp.zeros_like(out)
        send_ref[:, columns] = out
        send_ref[:, width + j * HD : width + (j + 1) * HD] = dq
        out_ref[:, columns] = jnp.where(keep, out, zero)
        dq_ref[:, columns] = jnp.where(keep, dq, zero)

    dk, dv = attend_group(q_ref, do_ref, k_ref[...], v_ref[...], bias_ref, live, per_group, emit)
    head_ref[0, 0] = dk[:half]
    head_ref[0, 1] = dv[:half]
    tail_ref[0, 0] = dk[half:]
    tail_ref[0, 1] = dv[half:]


def head_kernel(length, per_group, side_ref, q_ref, do_ref, k_ref, v_ref, seg_ref, part_ref, old_out, old_dq, out_ref, dq_ref, head_ref, bias_ref):
    half = length // 2

    @pl.when(pl.program_id(0) == 0)
    def _():
        fill_bias(seg_ref, bias_ref, half, 0, half)

    live = seg_ref[0:1, 0:half] >= 0

    def emit(j, out, dq):
        columns = slice(j * HD, (j + 1) * HD)
        out_ref[:, columns] = out
        dq_ref[:, columns] = dq

    dk, dv = attend_group(q_ref, do_ref, k_ref[...], v_ref[...], bias_ref, live, per_group, emit)
    head_ref[0, 0] = part_ref[0, 0] + dk
    head_ref[0, 1] = part_ref[0, 1] + dv


def any_spec():
    return pl.BlockSpec(memory_space=pl.ANY)


def attention_cost(rows, keys, heads):
    return pl.CostEstimate(
        flops=12 * rows * keys * HD * heads,
        transcendentals=rows * keys * heads,
        bytes_accessed=heads * (rows + keys) * HD * 8,
    )


def tail_call(handed, side, q, do, k, v, seg, groups, first, count, previous):
    length, row_width = q.shape
    half = length // 2
    width = row_width // groups
    per_group = width // HD
    split = groups // 2
    aliased = 0 if previous is None else 4

    def side_of(g, side_ref):
        group = g + first
        return (group // split) ^ side_ref[0], group % split

    def key_block(g, handed_ref, side_ref):
        plane, place = side_of(g, side_ref)
        return plane, 0, 0, place

    row_spec = pl.BlockSpec((half, width), lambda g, *_: (1, g + first))
    key_spec = pl.BlockSpec((length, HD), lambda g, *_: (0, g + first))
    part_spec = pl.BlockSpec((1, 2, half, HD), key_block)
    part_shape = jax.ShapeDtypeStruct((2, 2, half, split * HD), jnp.float32)
    grid_spec = pltpu.PrefetchScalarGridSpec(
        num_scalar_prefetch=2,
        grid=(count,),
        in_specs=[row_spec, row_spec, key_spec, key_spec, pl.BlockSpec((1, length), lambda g, *_: (0, 0))]
        + [any_spec()] * aliased,
        out_specs=[
            row_spec,
            row_spec,
            pl.BlockSpec((half, 2 * width), lambda g, *_: (0, g)),
            part_spec,
            part_spec,
        ],
        scratch_shapes=[pltpu.VMEM((length, half), jnp.float32)],
    )
    return pl.pallas_call(
        functools.partial(tail_kernel, length, per_group, aliased),
        grid_spec=grid_spec,
        out_shape=[
            jax.ShapeDtypeStruct(q.shape, jnp.bfloat16),
            jax.ShapeDtypeStruct(q.shape, jnp.bfloat16),
            jax.ShapeDtypeStruct((half, 2 * width * count), jnp.bfloat16),
            part_shape,
            part_shape,
        ],
        input_output_aliases={7: 0, 8: 1, 9: 3, 10: 4} if aliased else {},
        cost_estimate=attention_cost(half, length, per_group * count),
        name="tail_rows",
    )(handed, side, q, do, k, v, seg, *(previous or ()))


def head_call(side, q, do, k, v, seg, groups, part, out, dq):
    length, row_width = q.shape
    half = length // 2
    width = row_width // groups
    per_group = width // HD
    split = groups // 2

    def key_block(g, side_ref):
        return (g // split) ^ side_ref[0], 0, 0, g % split

    row_spec = pl.BlockSpec((half, width), lambda g, *_: (0, g))
    key_spec = pl.BlockSpec((half, HD), lambda g, *_: (0, g))
    part_spec = pl.BlockSpec((1, 2, half, HD), key_block)
    grid_spec = pltpu.PrefetchScalarGridSpec(
        num_scalar_prefetch=1,
        grid=(groups,),
        in_specs=[row_spec, row_spec, key_spec, key_spec, pl.BlockSpec((1, length), lambda g, *_: (0, 0)), part_spec]
        + [any_spec()] * 2,
        out_specs=[row_spec, row_spec, part_spec],
        scratch_shapes=[pltpu.VMEM((half, half), jnp.float32)],
    )
    return pl.pallas_call(
        functools.partial(head_kernel, length, per_group),
        grid_spec=grid_spec,
        out_shape=[
            jax.ShapeDtypeStruct(q.shape, jnp.bfloat16),
            jax.ShapeDtypeStruct(q.shape, jnp.bfloat16),
            jax.ShapeDtypeStruct(part.shape, jnp.float32),
        ],
        input_output_aliases={7: 0, 8: 1, 6: 2},
        cost_estimate=attention_cost(half, half, per_group * groups),
        name="head_rows",
    )(side, q, do, k, v, seg, part, out, dq)


def moved_rows(place_ref, arrived, length):
    capacity = arrived.shape[0]
    kept = place_ref[0]
    added = place_ref[1]
    row = lax.broadcasted_iota(jnp.int32, (length, capacity), 0)
    source = lax.broadcasted_iota(jnp.int32, (length, capacity), 1)
    chosen = (source - (capacity - added) == row - kept) & (source >= capacity - added)
    pick = jnp.where(chosen, 1.0, 0.0).astype(jnp.bfloat16)
    return dot(pick, arrived, NN).astype(jnp.bfloat16)


def place_kernel(place_ref, arrived_ref, old_out_ref, old_dq_ref, out_ref, dq_ref):
    length, width = out_ref.shape
    moved = moved_rows(place_ref, arrived_ref[...], length)
    out_ref[...] = old_out_ref[...] + moved[:, :width]
    dq_ref[...] = old_dq_ref[...] + moved[:, width:]


def place_call(place, arrived, out, dq, width, first):
    length = out.shape[0]
    capacity = arrived.shape[0]
    count = arrived.shape[1] // (2 * width)
    row_spec = pl.BlockSpec((length, width), lambda g, *_: (0, g + first))
    grid_spec = pltpu.PrefetchScalarGridSpec(
        num_scalar_prefetch=1,
        grid=(count,),
        in_specs=[pl.BlockSpec((capacity, 2 * width), lambda g, *_: (0, g)), row_spec, row_spec],
        out_specs=[row_spec, row_spec],
    )
    return pl.pallas_call(
        place_kernel,
        grid_spec=grid_spec,
        out_shape=[jax.ShapeDtypeStruct(out.shape, out.dtype)] * 2,
        input_output_aliases={2: 0, 3: 1},
        cost_estimate=pl.CostEstimate(
            flops=4 * length * capacity * width * count,
            transcendentals=0,
            bytes_accessed=8 * length * width * count,
        ),
        name="place_rows",
    )(place, arrived, out, dq)


def place_keys_kernel(place_ref, arrived_ref, head_ref, tail_ref, dk_ref, dv_ref):
    length, width = dk_ref.shape
    half = length // 2
    moved = moved_rows(place_ref, arrived_ref[...], length)
    limit = place_ref[2]
    row = lax.broadcasted_iota(jnp.int32, (half, width), 0)
    for part, ref in ((0, dk_ref), (1, dv_ref)):
        columns = slice(part * width, (part + 1) * width)
        ref[:half] = head_ref[:, columns] + moved[:half, columns]
        tail = tail_ref[:, columns]
        ref[half:] = jnp.where(row + half < limit, tail, jnp.zeros_like(tail)) + moved[half:, columns]


def place_keys_call(place, arrived, head, tail):
    half, width = head.shape
    shape = jax.ShapeDtypeStruct((2 * half, width // 2), jnp.bfloat16)
    return pl.pallas_call(
        place_keys_kernel,
        in_specs=[pl.BlockSpec(memory_space=pltpu.SMEM)] + [pl.BlockSpec(memory_space=pltpu.VMEM)] * 3,
        out_specs=[pl.BlockSpec(memory_space=pltpu.VMEM)] * 2,
        out_shape=[shape, shape],
        name="place_keys",
    )(place, arrived, head, tail)


def sum_kernel(own_ref, other_ref, out_ref):
    width = own_ref.shape[-1]
    for part in range(2):
        out_ref[:, part * width : (part + 1) * width] = (own_ref[0, part] + other_ref[part]).astype(jnp.bfloat16)


def sum_call(own, other):
    _, parts, rows, width = own.shape
    return pl.pallas_call(
        sum_kernel,
        grid=(1,),
        in_specs=[
            pl.BlockSpec((1, parts, rows, width), lambda i: (0, 0, 0, 0)),
            pl.BlockSpec((parts, rows, width), lambda i: (0, 0, 0)),
        ],
        out_specs=pl.BlockSpec((rows, parts * width), lambda i: (0, 0)),
        out_shape=jax.ShapeDtypeStruct((rows, parts * width), jnp.bfloat16),
        name="sum_keys",
    )(own, other)


def on_device(queries, key_states, value_states, out_grad, seg_ids, handed):
    length = seg_ids.shape[0]
    groups = key_states.shape[1] // HD
    q = queries[0]
    do = out_grad[0]
    width = q.shape[1] // groups
    position = lax.axis_index("dp")
    devices = lax.axis_size("dp")
    halfway = devices // 2
    seg = seg_ids.reshape(1, length)
    side = lax.axis_index("sub").astype(jnp.int32).reshape(1)
    onward = [(i, i + halfway) for i in range(halfway)]
    across = [(0, 1), (1, 0)]

    first = 1 if groups > 1 else groups
    out, dq, send_a, tail, head = tail_call(handed, side, q, do, key_states, value_states, seg, groups, 0, first, None)
    arrived_a = lax.ppermute(send_a, "dp", onward)
    arrived_b = None
    if groups > first:
        out, dq, send_b, tail, head = tail_call(
            handed, side, q, do, key_states, value_states, seg, groups, first, groups - first, (out, dq, tail, head)
        )
        arrived_b = lax.ppermute(send_b, "dp", onward)
    tail_sum = sum_call(tail, lax.ppermute(tail[1], "sub", across))
    arrived_keys = lax.ppermute(tail_sum, "dp", onward)
    out, dq, head = head_call(side, q, do, key_states, value_states, seg, groups, head, out, dq)
    head_sum = sum_call(head, lax.ppermute(head[1], "sub", across))

    live_rows = jnp.sum((seg_ids >= 0).astype(jnp.int32))
    partner_moved = lax.dynamic_index_in_dim(handed, jnp.maximum(position - halfway, 0), 0, keepdims=False)
    own_moved = lax.dynamic_index_in_dim(handed, position, 0, keepdims=False)
    added = jnp.where(position < halfway, 0, partner_moved)
    place = jnp.stack([live_rows, added, length - own_moved]).astype(jnp.int32)

    out, dq = place_call(place, arrived_a, out, dq, width, 0)
    if arrived_b is not None:
        out, dq = place_call(place, arrived_b, out, dq, width, first)
    dk, dv = place_keys_call(place, arrived_keys, head_sum, tail_sum)
    return out[None], dq[None], dk, dv


def solution(mesh):
    return jax.shard_map(
        on_device,
        mesh=mesh,
        in_specs=(
            P("sub", "dp", "head"),
            P("dp", "head"),
            P("dp", "head"),
            P("sub", "dp", "head"),
            P("dp"),
            P(),
        ),
        out_specs=(
            P("sub", "dp", "head"),
            P("sub", "dp", "head"),
            P("dp", ("head", "sub")),
            P("dp", ("head", "sub")),
        ),
        check_vma=False,
    )
```

```python
import functools

import jax
import jax.numpy as jnp
from jax import lax
from jax.experimental import pallas as pl
from jax.experimental.pallas import tpu as pltpu
from jax.sharding import PartitionSpec as P


HD = 128
PAD = 16
LOG2E = 1.4426950408889634
MASKED = -1e30
NT = (((1,), (1,)), ((), ()))
NN = (((1,), (0,)), ((), ()))


def dot(a, b, dims):
    return lax.dot_general(a, b, dims, preferred_element_type=jnp.float32)


def any_spec():
    return pl.BlockSpec(memory_space=pl.ANY)


def attention_cost(rows, keys, heads):
    return pl.CostEstimate(
        flops=12 * rows * keys * HD * heads,
        transcendentals=rows * keys * heads,
        bytes_accessed=heads * (rows + keys) * HD * 8,
    )


def fill_bias(key_seg, row_seg, bias_ref, row_offset):
    keys = key_seg.shape[1]
    rows = row_seg.shape[1]
    column = jnp.transpose(jnp.broadcast_to(key_seg.astype(jnp.float32), (HD, keys)))
    for begin in range(0, rows, HD):
        row = row_seg[:, begin : begin + HD].astype(jnp.float32)
        key_index = lax.broadcasted_iota(jnp.int32, (keys, HD), 0)
        row_index = lax.broadcasted_iota(jnp.int32, (keys, HD), 1) + (row_offset + begin)
        allowed = (column == row) & (key_index <= row_index)
        bias_ref[:, begin : begin + HD] = jnp.where(allowed, 0.0, MASKED)


def head_scores(q, do, k, v, bias_ref, live):
    scale = HD**-0.5
    x = dot(k, q, NT) * (scale * LOG2E) + bias_ref[...]
    p = jnp.exp2(x - jnp.max(x, axis=0, keepdims=True))
    inverse = jnp.where(live, 1.0 / jnp.sum(p, axis=0, keepdims=True), 0.0)
    w = p * inverse
    dp = dot(v, do, NT)
    delta = jnp.sum(w * dp, axis=0, keepdims=True)
    return w, w * (dp - delta)


def row_outputs(w, ds, k_t, v_t):
    out = jnp.transpose(dot(v_t, w, NN)).astype(jnp.bfloat16)
    dq = jnp.transpose(dot(k_t, ds, NN) * HD**-0.5).astype(jnp.bfloat16)
    return out, dq


def heads_of(ref, j):
    return ref[:, j * HD : (j + 1) * HD]


def packed_kernel(per_group, handed_ref, position_ref, side_ref, q_ref, do_ref, k_ref, v_ref, seg_ref, pack_ref, key_ref, bias_ref):
    window = q_ref.shape[0]

    @pl.when(pl.program_id(0) == 0)
    def _():
        fill_bias(seg_ref[...], seg_ref[...], bias_ref, 0)

    live = seg_ref[...] >= 0
    k = k_ref[...]
    v = v_ref[...]
    key_index = lax.broadcasted_iota(jnp.int32, (window, window), 0)
    row_index = lax.broadcasted_iota(jnp.int32, (window, window), 1)
    for j in range(per_group):
        w, ds = head_scores(heads_of(q_ref, j), heads_of(do_ref, j), k, v, bias_ref, live)
        packed = jnp.where(key_index <= row_index, w, jnp.transpose(ds))
        pack_ref[:, j * window : (j + 1) * window] = packed.astype(jnp.bfloat16)
    key_ref[...] = jnp.where(side_ref[0] == 0, k, v)


def packed_call(handed, position, side, q, do, k, v, seg, groups):
    length, row_width = q.shape
    window = length // 4
    width = row_width // groups
    per_group = width // HD

    def place(handed_ref, position_ref):
        return jnp.where(handed_ref[position_ref[0]] > window, 2, 3)

    row_spec = pl.BlockSpec((window, width), lambda g, h, p, s: (place(h, p), g))
    key_spec = pl.BlockSpec((window, HD), lambda g, h, p, s: (place(h, p), g))
    grid_spec = pltpu.PrefetchScalarGridSpec(
        num_scalar_prefetch=3,
        grid=(groups,),
        in_specs=[row_spec, row_spec, key_spec, key_spec, pl.BlockSpec((1, window), lambda g, h, p, s: (0, place(h, p)))],
        out_specs=[
            pl.BlockSpec((window, per_group * window), lambda g, *_: (0, g)),
            pl.BlockSpec((window, HD), lambda g, *_: (0, g)),
        ],
        scratch_shapes=[pltpu.VMEM((window, window), jnp.float32)],
    )
    return pl.pallas_call(
        functools.partial(packed_kernel, per_group),
        grid_spec=grid_spec,
        out_shape=[
            jax.ShapeDtypeStruct((window, groups * per_group * window), jnp.bfloat16),
            jax.ShapeDtypeStruct((window, groups * HD), jnp.bfloat16),
        ],
        cost_estimate=attention_cost(window, window, per_group * groups),
        name="packed_window",
    )(handed, position, side, q, do, k, v, seg)


def last_rows_kernel(per_group, q_ref, do_ref, k_ref, v_ref, seg_ref, send_ref, bias_ref):
    window, width = q_ref.shape

    @pl.when(pl.program_id(0) == 0)
    def _():
        fill_bias(seg_ref[...], seg_ref[:, window:], bias_ref, window)

    live = seg_ref[:, window:] >= 0
    k = k_ref[...]
    v = v_ref[...]
    k_t = jnp.transpose(k)
    v_t = jnp.transpose(v)
    for j in range(per_group):
        w, ds = head_scores(heads_of(q_ref, j), heads_of(do_ref, j), k, v, bias_ref, live)
        out, dq = row_outputs(w.astype(jnp.bfloat16), ds.astype(jnp.bfloat16), k_t, v_t)
        send_ref[:, j * HD : (j + 1) * HD] = out
        send_ref[:, width + j * HD : width + (j + 1) * HD] = dq


def last_rows_call(q, do, k, v, seg, groups):
    length, row_width = q.shape
    window = length // 4
    width = row_width // groups
    per_group = width // HD
    row_spec = pl.BlockSpec((window, width), lambda g: (3, g))
    key_spec = pl.BlockSpec((2 * window, HD), lambda g: (1, g))
    return pl.pallas_call(
        functools.partial(last_rows_kernel, per_group),
        grid=(groups,),
        in_specs=[row_spec, row_spec, key_spec, key_spec, pl.BlockSpec((1, 2 * window), lambda g: (0, 1))],
        out_specs=pl.BlockSpec((window, 2 * width), lambda g: (0, g)),
        out_shape=jax.ShapeDtypeStruct((window, 2 * row_width), jnp.bfloat16),
        scratch_shapes=[pltpu.VMEM((2 * window, window), jnp.float32)],
        cost_estimate=attention_cost(window, 2 * window, per_group * groups),
        name="last_rows",
    )(q, do, k, v, seg)


def attend_group(q_ref, do_ref, k, v, bias_ref, live, per_group, emit):
    k_t = jnp.transpose(k)
    v_t = jnp.transpose(v)
    dk = None
    dv = None
    for j in range(per_group):
        q = heads_of(q_ref, j)
        do = heads_of(do_ref, j)
        w, ds = head_scores(q, do, k, v, bias_ref, live)
        w = w.astype(jnp.bfloat16)
        ds = ds.astype(jnp.bfloat16)
        emit(j, *row_outputs(w, ds, k_t, v_t))
        dv_j = dot(w, do, NN)
        dk_j = dot(ds, q, NN)
        dv = dv_j if dv is None else dv + dv_j
        dk = dk_j if dk is None else dk + dk_j
    return dk * HD**-0.5, dv


def tail_kernel(split, per_group, handed_ref, position_ref, side_ref, q_ref, do_ref, k_ref, v_ref, seg_ref, out_ref, dq_ref, give_tail, give_head, keep_tail, keep_head, bias_ref):
    length = k_ref.shape[0]
    half = length // 2

    @pl.when(pl.program_id(0) == 0)
    def _():
        fill_bias(seg_ref[...], seg_ref[:, half:], bias_ref, half)

    live = seg_ref[:, half:] >= 0
    limit = length - handed_ref[position_ref[0]]
    keep = lax.broadcasted_iota(jnp.int32, (half, HD), 0) + half < limit

    def emit(j, out, dq):
        zero = jnp.zeros_like(out)
        out_ref[:, j * HD : (j + 1) * HD] = jnp.where(keep, out, zero)
        dq_ref[:, j * HD : (j + 1) * HD] = jnp.where(keep, dq, zero)

    dk, dv = attend_group(q_ref, do_ref, k_ref[...], v_ref[...], bias_ref, live, per_group, emit)

    def store(head_ref, tail_ref):
        head_ref[0] = dk[:half]
        head_ref[1] = dv[:half]
        tail_ref[0] = dk[half:]
        tail_ref[1] = dv[half:]

    pl.when(pl.program_id(0) < split)(lambda: store(give_head, give_tail))
    pl.when(pl.program_id(0) >= split)(lambda: store(keep_head, keep_tail))


def head_kernel(split, per_group, side_ref, q_ref, do_ref, k_ref, v_ref, seg_ref, give_part, keep_part, old_out, old_dq, out_ref, dq_ref, give_ref, keep_ref, bias_ref):
    @pl.when(pl.program_id(0) == 0)
    def _():
        fill_bias(seg_ref[...], seg_ref[...], bias_ref, 0)

    live = seg_ref[...] >= 0

    def emit(j, out, dq):
        out_ref[:, j * HD : (j + 1) * HD] = out
        dq_ref[:, j * HD : (j + 1) * HD] = dq

    dk, dv = attend_group(q_ref, do_ref, k_ref[...], v_ref[...], bias_ref, live, per_group, emit)

    def store(ref, part_ref):
        ref[0] = part_ref[0] + dk
        ref[1] = part_ref[1] + dv

    pl.when(pl.program_id(0) < split)(lambda: store(give_ref, give_part))
    pl.when(pl.program_id(0) >= split)(lambda: store(keep_ref, keep_part))


def key_places(split):
    def group(t, side_ref):
        return ((t // split) ^ (1 - side_ref[0])) * split + t % split

    def give(t):
        return jnp.minimum(t, split - 1)

    def keep(t):
        return jnp.maximum(t - split, 0)

    return group, give, keep


def tail_call(handed, position, side, q, do, k, v, seg, groups):
    length, row_width = q.shape
    half = length // 2
    width = row_width // groups
    per_group = width // HD
    split = groups // 2
    group, give, keep = key_places(split)
    row_spec = pl.BlockSpec((half, width), lambda t, h, p, s: (1, group(t, s)))
    key_spec = pl.BlockSpec((length, HD), lambda t, h, p, s: (0, group(t, s)))
    give_spec = pl.BlockSpec((2, half, HD), lambda t, *_: (0, 0, give(t)))
    keep_spec = pl.BlockSpec((2, half, HD), lambda t, *_: (0, 0, keep(t)))
    part_shape = jax.ShapeDtypeStruct((2, half, split * HD), jnp.float32)
    grid_spec = pltpu.PrefetchScalarGridSpec(
        num_scalar_prefetch=3,
        grid=(groups,),
        in_specs=[row_spec, row_spec, key_spec, key_spec, pl.BlockSpec((1, length), lambda t, *_: (0, 0))],
        out_specs=[row_spec, row_spec, give_spec, give_spec, keep_spec, keep_spec],
        scratch_shapes=[pltpu.VMEM((length, half), jnp.float32)],
    )
    return pl.pallas_call(
        functools.partial(tail_kernel, split, per_group),
        grid_spec=grid_spec,
        out_shape=[jax.ShapeDtypeStruct(q.shape, jnp.bfloat16)] * 2 + [part_shape] * 4,
        cost_estimate=attention_cost(half, length, per_group * groups),
        name="tail_rows",
    )(handed, position, side, q, do, k, v, seg)


def head_call(side, q, do, k, v, seg, groups, give_part, keep_part, out, dq):
    length, row_width = q.shape
    half = length // 2
    width = row_width // groups
    per_group = width // HD
    split = groups // 2
    group, give, keep = key_places(split)
    row_spec = pl.BlockSpec((half, width), lambda t, s: (0, group(t, s)))
    key_spec = pl.BlockSpec((half, HD), lambda t, s: (0, group(t, s)))
    give_spec = pl.BlockSpec((2, half, HD), lambda t, *_: (0, 0, give(t)))
    keep_spec = pl.BlockSpec((2, half, HD), lambda t, *_: (0, 0, keep(t)))
    grid_spec = pltpu.PrefetchScalarGridSpec(
        num_scalar_prefetch=1,
        grid=(groups,),
        in_specs=[row_spec, row_spec, key_spec, key_spec, pl.BlockSpec((1, half), lambda t, *_: (0, 0)), give_spec, keep_spec]
        + [any_spec()] * 2,
        out_specs=[row_spec, row_spec, give_spec, keep_spec],
        scratch_shapes=[pltpu.VMEM((half, half), jnp.float32)],
    )
    return pl.pallas_call(
        functools.partial(head_kernel, split, per_group),
        grid_spec=grid_spec,
        out_shape=[jax.ShapeDtypeStruct(q.shape, jnp.bfloat16)] * 2 + [jax.ShapeDtypeStruct(give_part.shape, jnp.float32)] * 2,
        input_output_aliases={8: 0, 9: 1},
        cost_estimate=attention_cost(half, half, per_group * groups),
        name="head_rows",
    )(side, q, do, k, v, seg, give_part, keep_part, out, dq)


def sum_kernel(own_ref, other_ref, out_ref):
    width = own_ref.shape[-1]
    for part in range(2):
        out_ref[:, part * width : (part + 1) * width] = (own_ref[part] + other_ref[part]).astype(jnp.bfloat16)


def sum_call(own, other):
    parts, rows, width = own.shape
    return pl.pallas_call(
        sum_kernel,
        in_specs=[pl.BlockSpec(memory_space=pltpu.VMEM)] * 2,
        out_specs=pl.BlockSpec(memory_space=pltpu.VMEM),
        out_shape=jax.ShapeDtypeStruct((rows, parts * width), jnp.bfloat16),
        name="sum_keys",
    )(own, other)


ACTIVE, START, FIRST, SKIP = range(4)


def place_numbers(seg_ids, handed, position, halfway):
    length = seg_ids.shape[0]
    window = length // 4
    live = jnp.sum((seg_ids >= 0).astype(jnp.int32))
    partner_moved = lax.dynamic_index_in_dim(handed, jnp.maximum(position - halfway, 0), 0, keepdims=False)
    own_moved = lax.dynamic_index_in_dim(handed, position, 0, keepdims=False)
    receiver = position >= halfway
    added = jnp.where(receiver, partner_moved, 0)
    large = receiver & (added > window)
    last = length - window - PAD
    skip = jnp.where(large, 2 * window - added, window - added)
    late = jnp.maximum(live + added - window, 0)

    def start(first):
        return jnp.minimum(first // PAD, last // PAD)

    return jnp.stack(
        [receiver.astype(jnp.int32), start(live), live, skip]
        + [large.astype(jnp.int32), start(late), late, jnp.zeros_like(late)]
        + [live, added, length - own_moved]
    ).astype(jnp.int32)


def pick_matrix(place_ref, base, rows, window):
    row = lax.broadcasted_iota(jnp.int32, (rows, window), 0)
    source = lax.broadcasted_iota(jnp.int32, (rows, window), 1)
    skip = place_ref[base + SKIP]
    offset = place_ref[base + FIRST] - place_ref[base + START] * PAD - skip
    chosen = (row - source == offset) & (source >= skip)
    return jnp.where(chosen, 1.0, 0.0).astype(jnp.bfloat16)


def with_rows(place_ref, base, refs, bufs, sems, rows, add):
    @pl.when(place_ref[base + ACTIVE] == 1)
    def _():
        begin = pl.multiple_of(place_ref[base + START] * PAD, PAD)
        reads = [
            pltpu.make_async_copy(ref.at[pl.ds(begin, rows), :], buf, sems.at[i]) for i, (ref, buf) in enumerate(zip(refs, bufs))
        ]
        for copy in reads:
            copy.start()
        for copy in reads:
            copy.wait()
        add()
        writes = [
            pltpu.make_async_copy(buf, ref.at[pl.ds(begin, rows), :], sems.at[i]) for i, (ref, buf) in enumerate(zip(refs, bufs))
        ]
        for copy in writes:
            copy.start()
        for copy in writes:
            copy.wait()


def place_packed_kernel(groups, per_group, place_ref, side_ref, pack_ref, mine_ref, other_ref, old_out, old_dq, out_ref, dq_ref, out_buf, dq_buf, sems):
    window = pack_ref.shape[0]
    rows = out_buf.shape[0]

    def add():
        pick = pick_matrix(place_ref, 0, rows, window)
        first = lax.broadcasted_iota(jnp.int32, (window, window), 0)
        second = lax.broadcasted_iota(jnp.int32, (window, window), 1)
        for g in range(groups):
            mine = heads_of(mine_ref, g)
            other = heads_of(other_ref, g)
            k = jnp.where(side_ref[0] == 0, mine, other)
            v = jnp.where(side_ref[0] == 0, other, mine)
            k_f = k.astype(jnp.float32)
            v_t = jnp.transpose(v)
            for j in range(per_group):
                head = g * per_group + j
                packed = pack_ref[:, head * window : (head + 1) * window].astype(jnp.float32)
                w = jnp.where(first <= second, packed, 0.0).astype(jnp.bfloat16)
                ds = jnp.where(first > second, packed, 0.0)
                out = jnp.transpose(dot(v_t, w, NN)).astype(jnp.bfloat16)
                total = jnp.sum(ds, axis=1, keepdims=True)
                dq = (dot(ds.astype(jnp.bfloat16), k, NN) - total * k_f) * HD**-0.5
                columns = slice(head * HD, (head + 1) * HD)
                out_buf[:, columns] += dot(pick, out, NN).astype(jnp.bfloat16)
                dq_buf[:, columns] += dot(pick, dq.astype(jnp.bfloat16), NN).astype(jnp.bfloat16)

    with_rows(place_ref, 0, (out_ref, dq_ref), (out_buf, dq_buf), sems, rows, add)


def place_last_kernel(groups, width, place_ref, arrived_ref, old_out, old_dq, out_ref, dq_ref, out_buf, dq_buf, sems):
    window = arrived_ref.shape[0]
    rows = out_buf.shape[0]

    def add():
        pick = pick_matrix(place_ref, 4, rows, window)
        for g in range(groups):
            columns = slice(g * width, (g + 1) * width)
            moved = dot(pick, arrived_ref[:, 2 * g * width : 2 * (g + 1) * width], NN).astype(jnp.bfloat16)
            out_buf[:, columns] += moved[:, :width]
            dq_buf[:, columns] += moved[:, width:]

    with_rows(place_ref, 4, (out_ref, dq_ref), (out_buf, dq_buf), sems, rows, add)


def place_call(kernel, scalars, arrays, out, dq):
    window = arrays[0].shape[0]
    rows = window + PAD
    count = len(scalars) + len(arrays)
    return pl.pallas_call(
        kernel,
        in_specs=[pl.BlockSpec(memory_space=pltpu.SMEM)] * len(scalars)
        + [pl.BlockSpec(memory_space=pltpu.VMEM)] * len(arrays)
        + [any_spec()] * 2,
        out_specs=[any_spec()] * 2,
        out_shape=[jax.ShapeDtypeStruct(out.shape, out.dtype)] * 2,
        scratch_shapes=[pltpu.VMEM((rows, out.shape[1]), jnp.bfloat16)] * 2 + [pltpu.SemaphoreType.DMA((2,))],
        input_output_aliases={count: 0, count + 1: 1},
        cost_estimate=pl.CostEstimate(
            flops=8 * rows * window * out.shape[1], transcendentals=0, bytes_accessed=12 * rows * out.shape[1]
        ),
    )(*scalars, *arrays, out, dq)


def place_keys_kernel(base, place_ref, arrived_ref, head_ref, tail_ref, dk_ref, dv_ref):
    length, width = dk_ref.shape
    half = length // 2
    kept = place_ref[base]
    added = place_ref[base + 1]
    limit = place_ref[base + 2]
    row = lax.broadcasted_iota(jnp.int32, (length, half), 0)
    source = lax.broadcasted_iota(jnp.int32, (length, half), 1)
    chosen = (row - source == kept - half + added) & (source >= half - added)
    pick = jnp.where(chosen, 1.0, 0.0).astype(jnp.bfloat16)
    moved = dot(pick, arrived_ref[...], NN).astype(jnp.bfloat16)
    own_row = lax.broadcasted_iota(jnp.int32, (half, width), 0) + half
    for part, ref in ((0, dk_ref), (1, dv_ref)):
        columns = slice(part * width, (part + 1) * width)
        ref[:half] = head_ref[:, columns] + moved[:half, columns]
        tail = tail_ref[:, columns]
        ref[half:] = jnp.where(own_row < limit, tail, jnp.zeros_like(tail)) + moved[half:, columns]


def place_keys_call(base, place, arrived, head, tail):
    half, width = head.shape
    shape = jax.ShapeDtypeStruct((2 * half, width // 2), jnp.bfloat16)
    return pl.pallas_call(
        functools.partial(place_keys_kernel, base),
        in_specs=[pl.BlockSpec(memory_space=pltpu.SMEM)] + [pl.BlockSpec(memory_space=pltpu.VMEM)] * 3,
        out_specs=[pl.BlockSpec(memory_space=pltpu.VMEM)] * 2,
        out_shape=[shape, shape],
        name="place_keys",
    )(place, arrived, head, tail)


def program(queries, key_states, value_states, out_grad, seg_ids, handed):
    length = seg_ids.shape[0]
    groups = key_states.shape[1] // HD
    q = queries[0]
    do = out_grad[0]
    width = q.shape[1] // groups
    per_group = width // HD
    index = lax.axis_index("dp").astype(jnp.int32)
    devices = lax.axis_size("dp")
    halfway = devices // 2
    seg = seg_ids.reshape(1, length)
    position = index.reshape(1)
    side = lax.axis_index("sub").astype(jnp.int32).reshape(1)
    onward = [(i, i + halfway) for i in range(halfway)]
    across = [(0, 1), (1, 0)]

    def moved(block, axis, route):
        return lax.ppermute(block, axis, route)

    own = (q, do, key_states, value_states, seg, groups)
    packed, window_keys = packed_call(handed, position, side, *own)
    packed_in = moved(packed, "dp", onward)
    mine = moved(window_keys, "dp", onward)
    last = last_rows_call(*own)
    last_in = moved(last, "dp", onward)

    out, dq, give_tail, give_head, keep_tail, keep_head = tail_call(handed, position, side, *own)
    other_tail = moved(give_tail, "sub", across)
    other = moved(mine, "sub", across)
    out, dq, give_head, keep_head = head_call(side, *own, give_head, keep_head, out, dq)
    other_head = moved(give_head, "sub", across)
    tail_sum = sum_call(keep_tail, other_tail)
    keys_in = moved(tail_sum, "dp", onward)
    head_sum = sum_call(keep_head, other_head)

    place = place_numbers(seg_ids, handed, index, halfway)
    out, dq = place_call(
        functools.partial(place_packed_kernel, groups, per_group), (place, side), (packed_in, mine, other), out, dq
    )
    dk, dv = place_keys_call(8, place, keys_in, head_sum, tail_sum)
    out, dq = place_call(functools.partial(place_last_kernel, groups, width), (place,), (last_in,), out, dq)
    return out[None], dq[None], dk, dv


def solution(mesh):
    return jax.shard_map(
        program,
        mesh=mesh,
        in_specs=(
            P("sub", "dp", "head"),
            P("dp", "head"),
            P("dp", "head"),
            P("sub", "dp", "head"),
            P("dp"),
            P(),
        ),
        out_specs=(
            P("sub", "dp", "head"),
            P("sub", "dp", "head"),
            P("dp", ("head", "sub")),
            P("dp", ("head", "sub")),
        ),
        check_vma=False,
    )
```

```python
import functools
import itertools

import jax
import jax.numpy as jnp
from jax import lax
from jax.experimental import pallas as pl
from jax.experimental.pallas import tpu as pltpu
from jax.sharding import PartitionSpec as P


HD = 128
PAD = 16
LOG2E = 1.4426950408889634
MASKED = -1e30
NT = (((1,), (1,)), ((), ()))
NN = (((1,), (0,)), ((), ()))


def dot(a, b, dims):
    return lax.dot_general(a, b, dims, preferred_element_type=jnp.float32)


def any_spec():
    return pl.BlockSpec(memory_space=pl.ANY)


def attention_cost(rows, keys, heads):
    return pl.CostEstimate(
        flops=12 * rows * keys * HD * heads,
        transcendentals=rows * keys * heads,
        bytes_accessed=heads * (rows + keys) * HD * 8,
    )


def fill_bias(key_seg, row_seg, bias_ref, row_offset):
    keys = key_seg.shape[1]
    rows = row_seg.shape[1]
    column = jnp.transpose(jnp.broadcast_to(key_seg.astype(jnp.float32), (HD, keys)))
    for begin in range(0, rows, HD):
        row = row_seg[:, begin : begin + HD].astype(jnp.float32)
        key_index = lax.broadcasted_iota(jnp.int32, (keys, HD), 0)
        row_index = lax.broadcasted_iota(jnp.int32, (keys, HD), 1) + (row_offset + begin)
        allowed = (column == row) & (key_index <= row_index)
        bias_ref[:, begin : begin + HD] = jnp.where(allowed, 0.0, MASKED)


def head_scores(q, do, k, v, bias_ref, live):
    scale = HD**-0.5
    x = dot(k, q, NT) * (scale * LOG2E) + bias_ref[...]
    p = jnp.exp2(x - jnp.max(x, axis=0, keepdims=True))
    inverse = jnp.where(live, 1.0 / jnp.sum(p, axis=0, keepdims=True), 0.0)
    w = p * inverse
    dp = dot(v, do, NT)
    delta = jnp.sum(w * dp, axis=0, keepdims=True)
    return w, w * (dp - delta)


def row_outputs(w, ds, k_t, v_t):
    out = jnp.transpose(dot(v_t, w, NN)).astype(jnp.bfloat16)
    dq = jnp.transpose(dot(k_t, ds, NN) * HD**-0.5).astype(jnp.bfloat16)
    return out, dq


def heads_of(ref, j):
    return ref[:, j * HD : (j + 1) * HD]


def packed_offset(moved, window):
    return jnp.minimum((2 * window - moved) // PAD, window // PAD) * PAD


def stacked(block, per_group):
    return jnp.concatenate([block[:, j * HD : (j + 1) * HD] for j in range(per_group)], axis=0)


def packed_kernel(per_group, handed_ref, position_ref, side_ref, q_ref, do_ref, k_ref, v_ref, seg_ref, pack_ref, key_ref, bias_ref, live_ref):
    window = q_ref.shape[0] // 2
    offset = pl.multiple_of(packed_offset(handed_ref[position_ref[0]], window), PAD)
    slots = pl.ds(offset, window)

    @pl.when(pl.program_id(0) == 0)
    def _():
        seg = jnp.broadcast_to(seg_ref[...].astype(jnp.float32), (8, 2 * window))
        seg = pltpu.roll(seg, 2 * window - offset, 1)[0:1, :window]
        fill_bias(seg, seg, bias_ref, 0)
        live_ref[...] = jnp.broadcast_to(seg, (8, window))
        for j in range(1, per_group):
            bias_ref[:, j * window : (j + 1) * window] = bias_ref[:, :window]

    live = jnp.concatenate([live_ref[0:1, :]] * per_group, axis=1) >= 0
    k = k_ref[slots, :]
    v = v_ref[slots, :]
    q = stacked(q_ref[slots, :], per_group)
    do = stacked(do_ref[slots, :], per_group)
    w, ds = head_scores(q, do, k, v, bias_ref, live)
    key_index = lax.broadcasted_iota(jnp.int32, (window, window), 0)
    row_index = lax.broadcasted_iota(jnp.int32, (window, window), 1)
    for j in range(per_group):
        columns = slice(j * window, (j + 1) * window)
        packed = jnp.where(key_index <= row_index, w[:, columns], jnp.transpose(ds[:, columns]))
        pack_ref[:, columns] = packed.astype(jnp.bfloat16)
    key_ref[...] = jnp.where(side_ref[0] == 0, k, v)


def packed_call(handed, position, side, q, do, k, v, seg, groups):
    length, row_width = q.shape
    half = length // 2
    window = half // 2
    width = row_width // groups
    per_group = width // HD
    row_spec = pl.BlockSpec((half, width), lambda g, *_: (1, g))
    key_spec = pl.BlockSpec((half, HD), lambda g, *_: (1, g))
    grid_spec = pltpu.PrefetchScalarGridSpec(
        num_scalar_prefetch=3,
        grid=(groups,),
        in_specs=[row_spec, row_spec, key_spec, key_spec, pl.BlockSpec((1, half), lambda g, *_: (0, 1))],
        out_specs=[
            pl.BlockSpec((window, per_group * window), lambda g, *_: (0, g)),
            pl.BlockSpec((window, HD), lambda g, *_: (0, g)),
        ],
        scratch_shapes=[pltpu.VMEM((window, per_group * window), jnp.float32), pltpu.VMEM((8, window), jnp.float32)],
    )
    return pl.pallas_call(
        functools.partial(packed_kernel, per_group),
        grid_spec=grid_spec,
        out_shape=[
            jax.ShapeDtypeStruct((window, groups * per_group * window), jnp.bfloat16),
            jax.ShapeDtypeStruct((window, groups * HD), jnp.bfloat16),
        ],
        cost_estimate=attention_cost(window, window, per_group * groups),
        name="packed_window",
    )(handed, position, side, q, do, k, v, seg)


def last_rows_kernel(per_group, q_ref, do_ref, k_ref, v_ref, seg_ref, send_ref, bias_ref):
    window, width = q_ref.shape

    @pl.when(pl.program_id(0) == 0)
    def _():
        fill_bias(seg_ref[...], seg_ref[:, window:], bias_ref, window)
        for j in range(1, per_group):
            bias_ref[:, j * window : (j + 1) * window] = bias_ref[:, :window]

    live = jnp.concatenate([seg_ref[:, window:]] * per_group, axis=1) >= 0
    k = k_ref[...]
    v = v_ref[...]
    q = stacked(q_ref[...], per_group)
    do = stacked(do_ref[...], per_group)
    w, ds = head_scores(q, do, k, v, bias_ref, live)
    out = dot(jnp.transpose(v), w.astype(jnp.bfloat16), NN)
    dq = dot(jnp.transpose(k), ds.astype(jnp.bfloat16), NN) * HD**-0.5
    for j in range(per_group):
        rows = slice(j * window, (j + 1) * window)
        send_ref[:, j * HD : (j + 1) * HD] = jnp.transpose(out[:, rows]).astype(jnp.bfloat16)
        send_ref[:, width + j * HD : width + (j + 1) * HD] = jnp.transpose(dq[:, rows]).astype(jnp.bfloat16)


def last_rows_call(q, do, k, v, seg, groups):
    length, row_width = q.shape
    window = length // 4
    width = row_width // groups
    per_group = width // HD
    row_spec = pl.BlockSpec((window, width), lambda g: (3, g))
    key_spec = pl.BlockSpec((2 * window, HD), lambda g: (1, g))
    return pl.pallas_call(
        functools.partial(last_rows_kernel, per_group),
        grid=(groups,),
        in_specs=[row_spec, row_spec, key_spec, key_spec, pl.BlockSpec((1, 2 * window), lambda g: (0, 1))],
        out_specs=pl.BlockSpec((window, 2 * width), lambda g: (0, g)),
        out_shape=jax.ShapeDtypeStruct((window, 2 * row_width), jnp.bfloat16),
        scratch_shapes=[pltpu.VMEM((2 * window, per_group * window), jnp.float32)],
        cost_estimate=attention_cost(window, 2 * window, per_group * groups),
        name="last_rows",
    )(q, do, k, v, seg)


def attend_group(q_ref, do_ref, k, v, bias_ref, live, per_group, emit):
    k_t = jnp.transpose(k)
    v_t = jnp.transpose(v)
    dk = None
    dv = None
    for j in range(per_group):
        q = heads_of(q_ref, j)
        do = heads_of(do_ref, j)
        w, ds = head_scores(q, do, k, v, bias_ref, live)
        w = w.astype(jnp.bfloat16)
        ds = ds.astype(jnp.bfloat16)
        emit(j, *row_outputs(w, ds, k_t, v_t))
        dv_j = dot(w, do, NN)
        dk_j = dot(ds, q, NN)
        dv = dv_j if dv is None else dv + dv_j
        dk = dk_j if dk is None else dk + dk_j
    return dk * HD**-0.5, dv


def tail_kernel(split, per_group, handed_ref, position_ref, side_ref, q_ref, do_ref, k_ref, v_ref, seg_ref, out_ref, dq_ref, give_tail, give_head, keep_tail, keep_head, bias_ref):
    length = k_ref.shape[0]
    half = length // 2

    @pl.when(pl.program_id(0) == 0)
    def _():
        fill_bias(seg_ref[...], seg_ref[:, half:], bias_ref, half)

    live = seg_ref[:, half:] >= 0
    limit = length - handed_ref[position_ref[0]]
    keep = lax.broadcasted_iota(jnp.int32, (half, HD), 0) + half < limit

    def emit(j, out, dq):
        zero = jnp.zeros_like(out)
        out_ref[:, j * HD : (j + 1) * HD] = jnp.where(keep, out, zero)
        dq_ref[:, j * HD : (j + 1) * HD] = jnp.where(keep, dq, zero)

    dk, dv = attend_group(q_ref, do_ref, k_ref[...], v_ref[...], bias_ref, live, per_group, emit)

    def store(head_ref, tail_ref):
        head_ref[0] = dk[:half]
        head_ref[1] = dv[:half]
        tail_ref[0] = dk[half:]
        tail_ref[1] = dv[half:]

    pl.when(pl.program_id(0) < split)(lambda: store(give_head, give_tail))
    pl.when(pl.program_id(0) >= split)(lambda: store(keep_head, keep_tail))


def head_kernel(split, per_group, side_ref, q_ref, do_ref, k_ref, v_ref, seg_ref, give_part, keep_part, old_out, old_dq, out_ref, dq_ref, give_ref, keep_ref, bias_ref):
    @pl.when(pl.program_id(0) == 0)
    def _():
        fill_bias(seg_ref[...], seg_ref[...], bias_ref, 0)

    live = seg_ref[...] >= 0

    def emit(j, out, dq):
        out_ref[:, j * HD : (j + 1) * HD] = out
        dq_ref[:, j * HD : (j + 1) * HD] = dq

    dk, dv = attend_group(q_ref, do_ref, k_ref[...], v_ref[...], bias_ref, live, per_group, emit)

    def store(ref, part_ref):
        ref[0] = part_ref[0] + dk
        ref[1] = part_ref[1] + dv

    pl.when(pl.program_id(0) < split)(lambda: store(give_ref, give_part))
    pl.when(pl.program_id(0) >= split)(lambda: store(keep_ref, keep_part))


def key_places(split):
    def group(t, side_ref):
        return ((t // split) ^ (1 - side_ref[0])) * split + t % split

    def give(t):
        return jnp.minimum(t, split - 1)

    def keep(t):
        return jnp.maximum(t - split, 0)

    return group, give, keep


def tail_call(handed, position, side, q, do, k, v, seg, groups):
    length, row_width = q.shape
    half = length // 2
    width = row_width // groups
    per_group = width // HD
    split = groups // 2
    group, give, keep = key_places(split)
    row_spec = pl.BlockSpec((half, width), lambda t, h, p, s: (1, group(t, s)))
    key_spec = pl.BlockSpec((length, HD), lambda t, h, p, s: (0, group(t, s)))
    give_spec = pl.BlockSpec((2, half, HD), lambda t, *_: (0, 0, give(t)))
    keep_spec = pl.BlockSpec((2, half, HD), lambda t, *_: (0, 0, keep(t)))
    part_shape = jax.ShapeDtypeStruct((2, half, split * HD), jnp.float32)
    grid_spec = pltpu.PrefetchScalarGridSpec(
        num_scalar_prefetch=3,
        grid=(groups,),
        in_specs=[row_spec, row_spec, key_spec, key_spec, pl.BlockSpec((1, length), lambda t, *_: (0, 0))],
        out_specs=[row_spec, row_spec, give_spec, give_spec, keep_spec, keep_spec],
        scratch_shapes=[pltpu.VMEM((length, half), jnp.float32)],
    )
    return pl.pallas_call(
        functools.partial(tail_kernel, split, per_group),
        grid_spec=grid_spec,
        out_shape=[jax.ShapeDtypeStruct(q.shape, jnp.bfloat16)] * 2 + [part_shape] * 4,
        cost_estimate=attention_cost(half, length, per_group * groups),
        name="tail_rows",
    )(handed, position, side, q, do, k, v, seg)


def head_call(side, q, do, k, v, seg, groups, give_part, keep_part, out, dq):
    length, row_width = q.shape
    half = length // 2
    width = row_width // groups
    per_group = width // HD
    split = groups // 2
    group, give, keep = key_places(split)
    row_spec = pl.BlockSpec((half, width), lambda t, s: (0, group(t, s)))
    key_spec = pl.BlockSpec((half, HD), lambda t, s: (0, group(t, s)))
    give_spec = pl.BlockSpec((2, half, HD), lambda t, *_: (0, 0, give(t)))
    keep_spec = pl.BlockSpec((2, half, HD), lambda t, *_: (0, 0, keep(t)))
    grid_spec = pltpu.PrefetchScalarGridSpec(
        num_scalar_prefetch=1,
        grid=(groups,),
        in_specs=[row_spec, row_spec, key_spec, key_spec, pl.BlockSpec((1, half), lambda t, *_: (0, 0)), give_spec, keep_spec]
        + [any_spec()] * 2,
        out_specs=[row_spec, row_spec, give_spec, keep_spec],
        scratch_shapes=[pltpu.VMEM((half, half), jnp.float32)],
    )
    return pl.pallas_call(
        functools.partial(head_kernel, split, per_group),
        grid_spec=grid_spec,
        out_shape=[jax.ShapeDtypeStruct(q.shape, jnp.bfloat16)] * 2 + [jax.ShapeDtypeStruct(give_part.shape, jnp.float32)] * 2,
        input_output_aliases={8: 0, 9: 1},
        cost_estimate=attention_cost(half, half, per_group * groups),
        name="head_rows",
    )(side, q, do, k, v, seg, give_part, keep_part, out, dq)


def sum_kernel(own_ref, other_ref, out_ref):
    width = own_ref.shape[-1]
    for part in range(2):
        out_ref[:, part * width : (part + 1) * width] = (own_ref[part] + other_ref[part]).astype(jnp.bfloat16)


def sum_call(own, other):
    parts, rows, width = own.shape
    return pl.pallas_call(
        sum_kernel,
        in_specs=[pl.BlockSpec(memory_space=pltpu.VMEM)] * 2,
        out_specs=pl.BlockSpec(memory_space=pltpu.VMEM),
        out_shape=jax.ShapeDtypeStruct((rows, parts * width), jnp.bfloat16),
        name="sum_keys",
    )(own, other)


ACTIVE, START, FIRST, SKIP = range(4)
PACKED, LAST, KEYS, BRANCH = 0, 4, 8, 11
SETS = 4
SIZES = 3


def sender_sets(halfway):
    return [[i for i in range(halfway) if i * SETS // halfway == part] for part in range(SETS)]


def numbers_kernel(halfway, window, handed_ref, position_ref, seg_ref, place_ref):
    position = position_ref[0]
    receiver = position >= halfway
    moved = handed_ref[jnp.maximum(position - halfway, 0)]
    added = jnp.where(receiver, moved, 0)
    live = jnp.sum(jnp.where(seg_ref[...] >= 0, 1.0, 0.0)).astype(jnp.int32)
    offset = packed_offset(moved, window)
    top = 4 * window - window - PAD
    late = live + added - window + offset
    place_ref[PACKED + ACTIVE] = receiver.astype(jnp.int32)
    place_ref[PACKED + START] = jnp.minimum(live, top) // PAD
    place_ref[PACKED + FIRST] = live
    place_ref[PACKED + SKIP] = 2 * window - moved - offset
    place_ref[LAST + ACTIVE] = (receiver & (added > window)).astype(jnp.int32)
    place_ref[LAST + START] = jnp.minimum(late, top) // PAD
    place_ref[LAST + FIRST] = late
    place_ref[LAST + SKIP] = offset
    place_ref[KEYS] = live
    place_ref[KEYS + 1] = added
    place_ref[KEYS + 2] = 4 * window - handed_ref[position]
    branch = 0
    for part in sender_sets(halfway)[1:]:
        most = handed_ref[part[0]]
        for i in part[1:]:
            most = jnp.maximum(most, handed_ref[i])
        size = (most > window).astype(jnp.int32) + (most > window + window // 2).astype(jnp.int32)
        branch = branch * SIZES + size
    place_ref[BRANCH] = branch
    for i in range(BRANCH + 1, 16):
        place_ref[i] = 0


def numbers_call(handed, position, seg, halfway):
    smem = pl.BlockSpec(memory_space=pltpu.SMEM)
    return pl.pallas_call(
        functools.partial(numbers_kernel, halfway, seg.shape[1] // 4),
        in_specs=[smem, smem, pl.BlockSpec(memory_space=pltpu.VMEM)],
        out_specs=smem,
        out_shape=jax.ShapeDtypeStruct((16,), jnp.int32),
        name="place_numbers",
    )(handed, position, seg)


def pick_matrix(place_ref, base, rows, window, lead=0):
    row = lax.broadcasted_iota(jnp.int32, (rows, window), 0)
    source = lax.broadcasted_iota(jnp.int32, (rows, window), 1)
    skip = place_ref[base + SKIP] - lead
    offset = place_ref[base + FIRST] - place_ref[base + START] * PAD - skip
    chosen = (row - source == offset) & (source >= skip)
    return jnp.where(chosen, 1.0, 0.0).astype(jnp.bfloat16)


def with_rows(place_ref, base, refs, bufs, sems, rows, add):
    @pl.when(place_ref[base + ACTIVE] == 1)
    def _():
        begin = pl.multiple_of(place_ref[base + START] * PAD, PAD)
        reads = [
            pltpu.make_async_copy(ref.at[pl.ds(begin, rows), :], buf, sems.at[i]) for i, (ref, buf) in enumerate(zip(refs, bufs))
        ]
        for copy in reads:
            copy.start()
        for copy in reads:
            copy.wait()
        add()
        writes = [
            pltpu.make_async_copy(buf, ref.at[pl.ds(begin, rows), :], sems.at[i]) for i, (ref, buf) in enumerate(zip(refs, bufs))
        ]
        for copy in writes:
            copy.start()
        for copy in writes:
            copy.wait()


def place_packed_kernel(groups, per_group, place_ref, side_ref, pack_ref, mine_ref, other_ref, old_out, old_dq, out_ref, dq_ref, out_buf, dq_buf, sems):
    window = pack_ref.shape[0]
    rows = out_buf.shape[0]

    def add():
        pick = pick_matrix(place_ref, PACKED, rows, window)
        first = lax.broadcasted_iota(jnp.int32, (window, window), 0)
        second = lax.broadcasted_iota(jnp.int32, (window, window), 1)
        for g in range(groups):
            mine = heads_of(mine_ref, g)
            other = heads_of(other_ref, g)
            k = jnp.where(side_ref[0] == 0, mine, other)
            v = jnp.where(side_ref[0] == 0, other, mine)
            k_f = k.astype(jnp.float32)
            v_t = jnp.transpose(v)
            for j in range(per_group):
                head = g * per_group + j
                packed = pack_ref[:, head * window : (head + 1) * window].astype(jnp.float32)
                w = jnp.where(first <= second, packed, 0.0).astype(jnp.bfloat16)
                ds = jnp.where(first > second, packed, 0.0)
                out = jnp.transpose(dot(v_t, w, NN)).astype(jnp.bfloat16)
                total = jnp.sum(ds, axis=1, keepdims=True)
                dq = (dot(ds.astype(jnp.bfloat16), k, NN) - total * k_f) * HD**-0.5
                columns = slice(head * HD, (head + 1) * HD)
                out_buf[:, columns] += dot(pick, out, NN).astype(jnp.bfloat16)
                dq_buf[:, columns] += dot(pick, dq.astype(jnp.bfloat16), NN).astype(jnp.bfloat16)

    with_rows(place_ref, PACKED, (out_ref, dq_ref), (out_buf, dq_buf), sems, rows, add)


def place_last_kernel(groups, width, halfway, place_ref, position_ref, first_ref, short_ref, full_ref, old_out, old_dq, out_ref, dq_ref, out_buf, dq_buf, sems):
    window = first_ref.shape[0]
    rows = out_buf.shape[0]
    in_first = position_ref[0] < halfway + len(sender_sets(halfway)[0])
    short = place_ref[LAST + SKIP] >= window - short_ref.shape[0]

    def add_from(ref):
        size = ref.shape[0]
        pick = pick_matrix(place_ref, LAST, rows, size, window - size)
        for g in range(groups):
            columns = slice(g * width, (g + 1) * width)
            moved = dot(pick, ref[:, 2 * g * width : 2 * (g + 1) * width], NN).astype(jnp.bfloat16)
            out_buf[:, columns] += moved[:, :width]
            dq_buf[:, columns] += moved[:, width:]

    def add():
        pl.when(in_first)(lambda: add_from(first_ref))
        pl.when(jnp.logical_not(in_first) & short)(lambda: add_from(short_ref))
        pl.when(jnp.logical_not(in_first) & jnp.logical_not(short))(lambda: add_from(full_ref))

    with_rows(place_ref, LAST, (out_ref, dq_ref), (out_buf, dq_buf), sems, rows, add)


def place_call(kernel, scalars, arrays, out, dq):
    window = arrays[0].shape[0]
    rows = window + PAD
    count = len(scalars) + len(arrays)
    return pl.pallas_call(
        kernel,
        in_specs=[pl.BlockSpec(memory_space=pltpu.SMEM)] * len(scalars)
        + [pl.BlockSpec(memory_space=pltpu.VMEM)] * len(arrays)
        + [any_spec()] * 2,
        out_specs=[any_spec()] * 2,
        out_shape=[jax.ShapeDtypeStruct(out.shape, out.dtype)] * 2,
        scratch_shapes=[pltpu.VMEM((rows, out.shape[1]), jnp.bfloat16)] * 2 + [pltpu.SemaphoreType.DMA((2,))],
        input_output_aliases={count: 0, count + 1: 1},
        cost_estimate=pl.CostEstimate(
            flops=8 * rows * window * out.shape[1], transcendentals=0, bytes_accessed=12 * rows * out.shape[1]
        ),
    )(*scalars, *arrays, out, dq)


def place_keys_kernel(base, place_ref, arrived_ref, keep_ref, other_ref, tail_ref, dk_ref, dv_ref):
    length, width = dk_ref.shape
    half = length // 2
    kept = place_ref[base]
    added = place_ref[base + 1]
    limit = place_ref[base + 2]
    row = lax.broadcasted_iota(jnp.int32, (length, half), 0)
    source = lax.broadcasted_iota(jnp.int32, (length, half), 1)
    chosen = (row - source == kept - half + added) & (source >= half - added)
    pick = jnp.where(chosen, 1.0, 0.0).astype(jnp.bfloat16)
    moved = dot(pick, arrived_ref[...], NN).astype(jnp.bfloat16)
    own_row = lax.broadcasted_iota(jnp.int32, (half, width), 0) + half
    for part, ref in ((0, dk_ref), (1, dv_ref)):
        columns = slice(part * width, (part + 1) * width)
        ref[:half] = (keep_ref[part] + other_ref[part]).astype(jnp.bfloat16) + moved[:half, columns]
        tail = tail_ref[:, columns]
        ref[half:] = jnp.where(own_row < limit, tail, jnp.zeros_like(tail)) + moved[half:, columns]


def place_keys_call(base, place, arrived, keep, other, tail):
    half, width = tail.shape
    shape = jax.ShapeDtypeStruct((2 * half, width // 2), jnp.bfloat16)
    return pl.pallas_call(
        functools.partial(place_keys_kernel, base),
        in_specs=[pl.BlockSpec(memory_space=pltpu.SMEM)] + [pl.BlockSpec(memory_space=pltpu.VMEM)] * 4,
        out_specs=[pl.BlockSpec(memory_space=pltpu.VMEM)] * 2,
        out_shape=[shape, shape],
        name="place_keys",
    )(place, arrived, keep, other, tail)


def program(queries, key_states, value_states, out_grad, seg_ids, handed):
    length = seg_ids.shape[0]
    groups = key_states.shape[1] // HD
    q = queries[0]
    do = out_grad[0]
    width = q.shape[1] // groups
    per_group = width // HD
    index = lax.axis_index("dp").astype(jnp.int32)
    devices = lax.axis_size("dp")
    halfway = devices // 2
    seg = seg_ids.reshape(1, length)
    position = index.reshape(1)
    side = lax.axis_index("sub").astype(jnp.int32).reshape(1)
    onward = [(i, i + halfway) for i in range(halfway)]
    across = [(0, 1), (1, 0)]

    def moved(block, axis, route):
        return lax.ppermute(block, axis, route)

    own = (q, do, key_states, value_states, seg, groups)
    packed, window_keys = packed_call(handed, position, side, *own)
    packed_in = moved(packed, "dp", onward)
    mine = moved(window_keys, "dp", onward)
    last = last_rows_call(*own)
    sets = sender_sets(halfway)

    def route_of(parts):
        return [(i, i + halfway) for part in parts for i in part]

    first_in = moved(last, "dp", route_of(sets[:1]))
    place = numbers_call(handed, position, seg, halfway)

    out, dq, give_tail, give_head, keep_tail, keep_head = tail_call(handed, position, side, *own)
    other_tail = moved(give_tail, "sub", across)
    other = moved(mine, "sub", across)
    out, dq, give_head, keep_head = head_call(side, *own, give_head, keep_head, out, dq)
    other_head = moved(give_head, "sub", across)
    tail_sum = sum_call(keep_tail, other_tail)
    keys_in = moved(tail_sum, "dp", onward)
    out, dq = place_call(
        functools.partial(place_packed_kernel, groups, per_group), (place, side), (packed_in, mine, other), out, dq
    )

    window = last.shape[0]

    def branch(sizes):
        def run(block):
            arrived = []
            for size, rows in ((1, window // 2), (2, window)):
                parts = [part for part, own_size in zip(sets[1:], sizes) if own_size == size]
                if parts:
                    arrived.append(lax.ppermute(block[window - rows :], "dp", route_of(parts)))
                else:
                    arrived.append(jnp.zeros((rows, block.shape[1]), block.dtype))
            return tuple(arrived)

        return run

    branches = [branch(sizes) for sizes in itertools.product(range(SIZES), repeat=SETS - 1)]
    short_in, full_in = lax.switch(place[BRANCH], branches, last)
    dk, dv = place_keys_call(KEYS, place, keys_in, keep_head, other_head, tail_sum)
    out, dq = place_call(
        functools.partial(place_last_kernel, groups, width, halfway), (place, position), (first_in, short_in, full_in), out, dq
    )
    return out[None], dq[None], dk, dv


def solution(mesh):
    return jax.shard_map(
        program,
        mesh=mesh,
        in_specs=(
            P("sub", "dp", "head"),
            P("dp", "head"),
            P("dp", "head"),
            P("sub", "dp", "head"),
            P("dp"),
            P(),
        ),
        out_specs=(
            P("sub", "dp", "head"),
            P("sub", "dp", "head"),
            P("dp", ("head", "sub")),
            P("dp", ("head", "sub")),
        ),
        check_vma=False,
    )
```

```python
import functools
import itertools

import jax
import jax.numpy as jnp
from jax import lax
from jax.experimental import pallas as pl
from jax.experimental.pallas import tpu as pltpu
from jax.sharding import PartitionSpec as P


HD = 128
PAD = 16
LOG2E = 1.4426950408889634
MASKED = -1e30
NT = (((1,), (1,)), ((), ()))
NN = (((1,), (0,)), ((), ()))


def dot(a, b, dims):
    return lax.dot_general(a, b, dims, preferred_element_type=jnp.float32)


def any_spec():
    return pl.BlockSpec(memory_space=pl.ANY)


def attention_cost(rows, keys, heads):
    return pl.CostEstimate(
        flops=12 * rows * keys * HD * heads,
        transcendentals=rows * keys * heads,
        bytes_accessed=heads * (rows + keys) * HD * 8,
    )


def fill_bias(key_seg, row_seg, bias_ref, row_offset):
    keys = key_seg.shape[1]
    rows = row_seg.shape[1]
    column = jnp.transpose(jnp.broadcast_to(key_seg.astype(jnp.float32), (HD, keys)))
    for begin in range(0, rows, HD):
        row = row_seg[:, begin : begin + HD].astype(jnp.float32)
        key_index = lax.broadcasted_iota(jnp.int32, (keys, HD), 0)
        row_index = lax.broadcasted_iota(jnp.int32, (keys, HD), 1) + (row_offset + begin)
        allowed = (column == row) & (key_index <= row_index) & (row >= 0)
        bias_ref[:, begin : begin + HD] = jnp.where(allowed, 0.0, MASKED)


def head_scores(q, do, k, v, bias_ref, live):
    scale = HD**-0.5
    x = dot(k, q, NT) * (scale * LOG2E) + bias_ref[...]
    p = jnp.exp2(x - jnp.max(x, axis=0, keepdims=True))
    inverse = jnp.where(live, 1.0 / jnp.sum(p, axis=0, keepdims=True), 0.0)
    w = p * inverse
    dp = dot(v, do, NT)
    delta = jnp.sum(w * dp, axis=0, keepdims=True)
    return w, w * (dp - delta)


def heads_of(ref, j):
    return ref[:, j * HD : (j + 1) * HD]


def packed_offset(moved, window):
    return jnp.minimum((2 * window - moved) // PAD, window // PAD) * PAD


def stacked(block, per_group):
    return jnp.concatenate([block[:, j * HD : (j + 1) * HD] for j in range(per_group)], axis=0)


def packed_kernel(per_group, handed_ref, position_ref, side_ref, q_ref, do_ref, k_ref, v_ref, seg_ref, pack_ref, key_ref, bias_ref, live_ref):
    window = q_ref.shape[0] // 2
    offset = pl.multiple_of(packed_offset(handed_ref[position_ref[0]], window), PAD)
    slots = pl.ds(offset, window)

    @pl.when(pl.program_id(0) == 0)
    def _():
        seg = jnp.broadcast_to(seg_ref[...].astype(jnp.float32), (8, 2 * window))
        seg = pltpu.roll(seg, 2 * window - offset, 1)[0:1, :window]
        fill_bias(seg, seg, bias_ref, 0)
        live_ref[...] = jnp.broadcast_to(seg, (8, window))
        for j in range(1, per_group):
            bias_ref[:, j * window : (j + 1) * window] = bias_ref[:, :window]

    live = jnp.concatenate([live_ref[0:1, :]] * per_group, axis=1) >= 0
    k = k_ref[slots, :]
    v = v_ref[slots, :]
    q = stacked(q_ref[slots, :], per_group)
    do = stacked(do_ref[slots, :], per_group)
    w, ds = head_scores(q, do, k, v, bias_ref, live)
    key_index = lax.broadcasted_iota(jnp.int32, (window, window), 0)
    row_index = lax.broadcasted_iota(jnp.int32, (window, window), 1)
    for j in range(per_group):
        columns = slice(j * window, (j + 1) * window)
        packed = jnp.where(key_index <= row_index, w[:, columns], jnp.transpose(ds[:, columns]))
        pack_ref[:, columns] = packed.astype(jnp.bfloat16)
    key_ref[...] = jnp.where(side_ref[0] == 0, k, v)


def packed_call(handed, position, side, q, do, k, v, seg, groups):
    length, row_width = q.shape
    half = length // 2
    window = half // 2
    width = row_width // groups
    per_group = width // HD
    row_spec = pl.BlockSpec((half, width), lambda g, *_: (1, g))
    key_spec = pl.BlockSpec((half, HD), lambda g, *_: (1, g))
    grid_spec = pltpu.PrefetchScalarGridSpec(
        num_scalar_prefetch=3,
        grid=(groups,),
        in_specs=[row_spec, row_spec, key_spec, key_spec, pl.BlockSpec((1, half), lambda g, *_: (0, 1))],
        out_specs=[
            pl.BlockSpec((window, per_group * window), lambda g, *_: (0, g)),
            pl.BlockSpec((window, HD), lambda g, *_: (0, g)),
        ],
        scratch_shapes=[pltpu.VMEM((window, per_group * window), jnp.float32), pltpu.VMEM((8, window), jnp.float32)],
    )
    return pl.pallas_call(
        functools.partial(packed_kernel, per_group),
        grid_spec=grid_spec,
        out_shape=[
            jax.ShapeDtypeStruct((window, groups * per_group * window), jnp.bfloat16),
            jax.ShapeDtypeStruct((window, groups * HD), jnp.bfloat16),
        ],
        cost_estimate=attention_cost(window, window, per_group * groups),
        name="packed_window",
    )(handed, position, side, q, do, k, v, seg)


def last_rows_kernel(per_group, q_ref, do_ref, k_ref, v_ref, seg_ref, send_ref, bias_ref):
    window, width = q_ref.shape

    @pl.when(pl.program_id(0) == 0)
    def _():
        fill_bias(seg_ref[...], seg_ref[:, window:], bias_ref, window)
        for j in range(1, per_group):
            bias_ref[:, j * window : (j + 1) * window] = bias_ref[:, :window]

    live = jnp.concatenate([seg_ref[:, window:]] * per_group, axis=1) >= 0
    k = k_ref[...]
    v = v_ref[...]
    q = stacked(q_ref[...], per_group)
    do = stacked(do_ref[...], per_group)
    w, ds = head_scores(q, do, k, v, bias_ref, live)
    out = dot(jnp.transpose(v), w.astype(jnp.bfloat16), NN)
    dq = dot(jnp.transpose(k), ds.astype(jnp.bfloat16), NN) * HD**-0.5
    for j in range(per_group):
        rows = slice(j * window, (j + 1) * window)
        send_ref[:, j * HD : (j + 1) * HD] = jnp.transpose(out[:, rows]).astype(jnp.bfloat16)
        send_ref[:, width + j * HD : width + (j + 1) * HD] = jnp.transpose(dq[:, rows]).astype(jnp.bfloat16)


def last_rows_call(q, do, k, v, seg, groups):
    length, row_width = q.shape
    window = length // 4
    width = row_width // groups
    per_group = width // HD
    row_spec = pl.BlockSpec((window, width), lambda g: (3, g))
    key_spec = pl.BlockSpec((2 * window, HD), lambda g: (1, g))
    return pl.pallas_call(
        functools.partial(last_rows_kernel, per_group),
        grid=(groups,),
        in_specs=[row_spec, row_spec, key_spec, key_spec, pl.BlockSpec((1, 2 * window), lambda g: (0, 1))],
        out_specs=pl.BlockSpec((window, 2 * width), lambda g: (0, g)),
        out_shape=jax.ShapeDtypeStruct((window, 2 * row_width), jnp.bfloat16),
        scratch_shapes=[pltpu.VMEM((2 * window, per_group * window), jnp.float32)],
        cost_estimate=attention_cost(window, 2 * window, per_group * groups),
        name="last_rows",
    )(q, do, k, v, seg)


def own_kernel(split, per_group, handed_ref, position_ref, side_ref, place_ref, q_ref, do_ref, k_ref, v_ref, seg_ref, out_ref, dq_ref, give_tail, give_head, keep_tail, keep_head, bias_ref, dk_ref, dv_ref):
    length = k_ref.shape[0]
    half = length // 2
    window = half // 2
    blocks = length // window

    @pl.when(pl.program_id(0) == 0)
    def _():
        for block in range(blocks):
            rows = slice(block * window, (block + 1) * window)
            fill_bias(seg_ref[...], seg_ref[:, rows], bias_ref.at[block], block * window)

    limit = length - handed_ref[position_ref[0]]
    dk_ref[...] = jnp.zeros_like(dk_ref)
    dv_ref[...] = jnp.zeros_like(dv_ref)

    def row_block(block, carry):
        count = place_ref[COUNTS + block]
        rows = pl.ds(pl.multiple_of(block * window, window), window)
        keep = lax.broadcasted_iota(jnp.int32, (window, HD), 0) + block * window < limit

        def run(size):
            keys = pl.ds(pl.multiple_of((block + 1 - size) * window, window), size * window)
            q = stacked(q_ref[rows, :], per_group)
            do = stacked(do_ref[rows, :], per_group)
            k = k_ref[keys, :]
            v = v_ref[keys, :]
            scale = HD**-0.5
            bias = jnp.concatenate([bias_ref[block, keys, :]] * per_group, axis=1)
            x = dot(k, q, NT) * (scale * LOG2E) + bias
            top = jnp.max(x, axis=0, keepdims=True)
            p = jnp.exp2(x - top)
            live = top > 0.5 * MASKED
            w = p * jnp.where(live, 1.0 / jnp.sum(p, axis=0, keepdims=True), 0.0)
            wb = w.astype(jnp.bfloat16)
            dp = dot(v, do, NT)
            delta = jnp.sum(w * dp, axis=0, keepdims=True)
            ds = (w * (dp - delta)).astype(jnp.bfloat16)
            out = dot(jnp.transpose(v), wb, NN)
            dq = dot(jnp.transpose(k), ds, NN) * scale
            dv_ref[keys, :] += dot(wb, do, NN)
            dk_ref[keys, :] += dot(ds, q, NN)
            for j in range(per_group):
                columns = slice(j * HD, (j + 1) * HD)
                lanes = slice(j * window, (j + 1) * window)
                out_ref[rows, columns] = jnp.where(keep, jnp.transpose(out[:, lanes]), 0.0).astype(jnp.bfloat16)
                dq_ref[rows, columns] = jnp.where(keep, jnp.transpose(dq[:, lanes]), 0.0).astype(jnp.bfloat16)

        for size in range(1, blocks + 1):
            pl.when(count == size)(functools.partial(run, size))

        @pl.when(count == 0)
        def _():
            out_ref[rows, :] = jnp.zeros((window, per_group * HD), jnp.bfloat16)
            dq_ref[rows, :] = jnp.zeros((window, per_group * HD), jnp.bfloat16)

        return carry

    lax.fori_loop(0, blocks, row_block, 0)

    def store(head_ref, tail_ref):
        dk = (dk_ref[...] * HD**-0.5).astype(head_ref.dtype)
        dv = dv_ref[...].astype(head_ref.dtype)
        head_ref[0] = dk[:half]
        head_ref[1] = dv[:half]
        tail_ref[0] = dk[half:]
        tail_ref[1] = dv[half:]

    pl.when(pl.program_id(0) < split)(lambda: store(give_head, give_tail))
    pl.when(pl.program_id(0) >= split)(lambda: store(keep_head, keep_tail))


def key_places(split):
    def group(t, side_ref):
        return ((t // split) ^ (1 - side_ref[0])) * split + t % split

    def give(t):
        return jnp.minimum(t, split - 1)

    def keep(t):
        return jnp.maximum(t - split, 0)

    return group, give, keep


def own_call(handed, position, side, place, q, do, k, v, seg, groups):
    length, row_width = q.shape
    half = length // 2
    width = row_width // groups
    per_group = width // HD
    split = groups // 2
    group, give, keep = key_places(split)
    row_spec = pl.BlockSpec((length, width), lambda t, h, p, s, n: (0, group(t, s)))
    key_spec = pl.BlockSpec((length, HD), lambda t, h, p, s, n: (0, group(t, s)))
    give_spec = pl.BlockSpec((2, half, HD), lambda t, *_: (0, 0, give(t)))
    keep_spec = pl.BlockSpec((2, half, HD), lambda t, *_: (0, 0, keep(t)))
    grid_spec = pltpu.PrefetchScalarGridSpec(
        num_scalar_prefetch=4,
        grid=(groups,),
        in_specs=[row_spec, row_spec, key_spec, key_spec, pl.BlockSpec((1, length), lambda t, *_: (0, 0))],
        out_specs=[row_spec, row_spec, give_spec, give_spec, keep_spec, keep_spec],
        scratch_shapes=[
            pltpu.VMEM((4, length, length // 4), jnp.float32),
            pltpu.VMEM((length, HD), jnp.float32),
            pltpu.VMEM((length, HD), jnp.float32),
        ],
    )
    part = (2, half, split * HD)
    return pl.pallas_call(
        functools.partial(own_kernel, split, per_group),
        grid_spec=grid_spec,
        out_shape=[jax.ShapeDtypeStruct(q.shape, jnp.bfloat16)] * 2
        + [jax.ShapeDtypeStruct(part, jnp.bfloat16)] * 2
        + [jax.ShapeDtypeStruct(part, jnp.float32)] * 2,
        cost_estimate=attention_cost(length, half, per_group * groups),
        name="own_rows",
    )(handed, position, side, place, q, do, k, v, seg)


def sum_kernel(own_ref, other_ref, out_ref):
    width = own_ref.shape[-1]
    for part in range(2):
        out_ref[:, part * width : (part + 1) * width] = (own_ref[part] + other_ref[part]).astype(jnp.bfloat16)


def sum_call(own, other):
    parts, rows, width = own.shape
    return pl.pallas_call(
        sum_kernel,
        in_specs=[pl.BlockSpec(memory_space=pltpu.VMEM)] * 2,
        out_specs=pl.BlockSpec(memory_space=pltpu.VMEM),
        out_shape=jax.ShapeDtypeStruct((rows, parts * width), jnp.bfloat16),
        name="sum_keys",
    )(own, other)


ACTIVE, START, FIRST, SKIP = range(4)
PACKED, LAST, KEYS, BRANCH, COUNTS = 0, 4, 8, 11, 12
SETS = 4
SIZES = 3


def sender_sets(halfway):
    return [[i for i in range(halfway) if i * SETS // halfway == part] for part in range(SETS)]


def numbers_kernel(halfway, window, handed_ref, position_ref, seg_ref, place_ref):
    position = position_ref[0]
    receiver = position >= halfway
    moved = handed_ref[jnp.maximum(position - halfway, 0)]
    added = jnp.where(receiver, moved, 0)
    live = jnp.sum(jnp.where(seg_ref[...] >= 0, 1.0, 0.0)).astype(jnp.int32)
    offset = packed_offset(moved, window)
    top = 4 * window - window - PAD
    late = live + added - window + offset
    place_ref[PACKED + ACTIVE] = receiver.astype(jnp.int32)
    place_ref[PACKED + START] = jnp.minimum(live, top) // PAD
    place_ref[PACKED + FIRST] = live
    place_ref[PACKED + SKIP] = 2 * window - moved - offset
    place_ref[LAST + ACTIVE] = (receiver & (added > window)).astype(jnp.int32)
    place_ref[LAST + START] = jnp.minimum(late, top) // PAD
    place_ref[LAST + FIRST] = late
    place_ref[LAST + SKIP] = offset
    place_ref[KEYS] = live
    place_ref[KEYS + 1] = added
    place_ref[KEYS + 2] = 4 * window - handed_ref[position]
    branch = 0
    for part in sender_sets(halfway)[1:]:
        most = handed_ref[part[0]]
        for i in part[1:]:
            most = jnp.maximum(most, handed_ref[i])
        size = (most > window).astype(jnp.int32) + (most > window + window // 2).astype(jnp.int32)
        branch = branch * SIZES + size
    place_ref[BRANCH] = branch
    seg = seg_ref[...].astype(jnp.float32)
    slot = lax.broadcasted_iota(jnp.int32, seg.shape, 1)
    for block in range(4):
        number = jnp.sum(jnp.where(slot == block * window, seg, 0.0))
        begin = jnp.sum(jnp.where((seg >= 0) & (seg < number), 1.0, 0.0)).astype(jnp.int32)
        place_ref[COUNTS + block] = jnp.where(number >= 0, block + 1 - begin // window, 0)


def numbers_call(handed, position, seg, halfway):
    smem = pl.BlockSpec(memory_space=pltpu.SMEM)
    return pl.pallas_call(
        functools.partial(numbers_kernel, halfway, seg.shape[1] // 4),
        in_specs=[smem, smem, pl.BlockSpec(memory_space=pltpu.VMEM)],
        out_specs=smem,
        out_shape=jax.ShapeDtypeStruct((16,), jnp.int32),
        name="place_numbers",
    )(handed, position, seg)


def pick_matrix(place_ref, base, rows, window, lead=0):
    row = lax.broadcasted_iota(jnp.int32, (rows, window), 0)
    source = lax.broadcasted_iota(jnp.int32, (rows, window), 1)
    skip = place_ref[base + SKIP] - lead
    offset = place_ref[base + FIRST] - place_ref[base + START] * PAD - skip
    chosen = (row - source == offset) & (source >= skip)
    return jnp.where(chosen, 1.0, 0.0).astype(jnp.bfloat16)


def with_rows(place_ref, base, refs, bufs, sems, rows, add):
    @pl.when(place_ref[base + ACTIVE] == 1)
    def _():
        begin = pl.multiple_of(place_ref[base + START] * PAD, PAD)
        reads = [
            pltpu.make_async_copy(ref.at[pl.ds(begin, rows), :], buf, sems.at[i]) for i, (ref, buf) in enumerate(zip(refs, bufs))
        ]
        for copy in reads:
            copy.start()
        for copy in reads:
            copy.wait()
        add()
        writes = [
            pltpu.make_async_copy(buf, ref.at[pl.ds(begin, rows), :], sems.at[i]) for i, (ref, buf) in enumerate(zip(refs, bufs))
        ]
        for copy in writes:
            copy.start()
        for copy in writes:
            copy.wait()


def place_packed_kernel(groups, per_group, place_ref, side_ref, pack_ref, mine_ref, other_ref, old_out, old_dq, out_ref, dq_ref, out_buf, dq_buf, sems):
    window = pack_ref.shape[0]
    rows = out_buf.shape[0]

    def add():
        pick = pick_matrix(place_ref, PACKED, rows, window)
        first = lax.broadcasted_iota(jnp.int32, (window, window), 0)
        second = lax.broadcasted_iota(jnp.int32, (window, window), 1)
        for g in range(groups):
            mine = heads_of(mine_ref, g)
            other = heads_of(other_ref, g)
            k = jnp.where(side_ref[0] == 0, mine, other)
            v = jnp.where(side_ref[0] == 0, other, mine)
            k_f = k.astype(jnp.float32)
            v_t = jnp.transpose(v)
            for j in range(per_group):
                head = g * per_group + j
                packed = pack_ref[:, head * window : (head + 1) * window].astype(jnp.float32)
                w = jnp.where(first <= second, packed, 0.0).astype(jnp.bfloat16)
                ds = jnp.where(first > second, packed, 0.0)
                out = jnp.transpose(dot(v_t, w, NN)).astype(jnp.bfloat16)
                total = jnp.sum(ds, axis=1, keepdims=True)
                dq = (dot(ds.astype(jnp.bfloat16), k, NN) - total * k_f) * HD**-0.5
                columns = slice(head * HD, (head + 1) * HD)
                out_buf[:, columns] += dot(pick, out, NN).astype(jnp.bfloat16)
                dq_buf[:, columns] += dot(pick, dq.astype(jnp.bfloat16), NN).astype(jnp.bfloat16)

    with_rows(place_ref, PACKED, (out_ref, dq_ref), (out_buf, dq_buf), sems, rows, add)


def place_last_kernel(width, halfway, place_ref, position_ref, first_ref, detour_ref, short_ref, full_ref, old_out, old_dq, out_ref, dq_ref, out_buf, dq_buf, sems):
    window = first_ref.shape[0]
    rows = out_buf.shape[0]
    in_first = position_ref[0] < halfway + len(sender_sets(halfway)[0])
    short = place_ref[LAST + SKIP] >= window - short_ref.shape[0]

    def add_from(*refs):
        size = refs[0].shape[0]
        pick = pick_matrix(place_ref, LAST, rows, size, window - size)
        blocks = [(ref, g) for ref in refs for g in range(ref.shape[1] // (2 * width))]
        for g, (ref, place) in enumerate(blocks):
            columns = slice(g * width, (g + 1) * width)
            moved = dot(pick, ref[:, 2 * place * width : 2 * (place + 1) * width], NN).astype(jnp.bfloat16)
            out_buf[:, columns] += moved[:, :width]
            dq_buf[:, columns] += moved[:, width:]

    def add():
        pl.when(in_first)(lambda: add_from(first_ref, detour_ref))
        pl.when(jnp.logical_not(in_first) & short)(lambda: add_from(short_ref))
        pl.when(jnp.logical_not(in_first) & jnp.logical_not(short))(lambda: add_from(full_ref))

    with_rows(place_ref, LAST, (out_ref, dq_ref), (out_buf, dq_buf), sems, rows, add)


def place_call(kernel, scalars, arrays, out, dq):
    window = arrays[0].shape[0]
    rows = window + PAD
    count = len(scalars) + len(arrays)
    return pl.pallas_call(
        kernel,
        in_specs=[pl.BlockSpec(memory_space=pltpu.SMEM)] * len(scalars)
        + [pl.BlockSpec(memory_space=pltpu.VMEM)] * len(arrays)
        + [any_spec()] * 2,
        out_specs=[any_spec()] * 2,
        out_shape=[jax.ShapeDtypeStruct(out.shape, out.dtype)] * 2,
        scratch_shapes=[pltpu.VMEM((rows, out.shape[1]), jnp.bfloat16)] * 2 + [pltpu.SemaphoreType.DMA((2,))],
        input_output_aliases={count: 0, count + 1: 1},
        cost_estimate=pl.CostEstimate(
            flops=8 * rows * window * out.shape[1], transcendentals=0, bytes_accessed=12 * rows * out.shape[1]
        ),
    )(*scalars, *arrays, out, dq)


def place_keys_kernel(base, place_ref, arrived_ref, keep_ref, other_ref, tail_ref, dk_ref, dv_ref):
    length, width = dk_ref.shape
    half = length // 2
    kept = place_ref[base]
    added = place_ref[base + 1]
    limit = place_ref[base + 2]
    row = lax.broadcasted_iota(jnp.int32, (length, half), 0)
    source = lax.broadcasted_iota(jnp.int32, (length, half), 1)
    chosen = (row - source == kept - half + added) & (source >= half - added)
    pick = jnp.where(chosen, 1.0, 0.0).astype(jnp.bfloat16)
    moved = dot(pick, arrived_ref[...], NN).astype(jnp.bfloat16)
    own_row = lax.broadcasted_iota(jnp.int32, (half, width), 0) + half
    for part, ref in ((0, dk_ref), (1, dv_ref)):
        columns = slice(part * width, (part + 1) * width)
        ref[:half] = (keep_ref[part] + other_ref[part]).astype(jnp.bfloat16) + moved[:half, columns]
        tail = tail_ref[:, columns]
        ref[half:] = jnp.where(own_row < limit, tail, jnp.zeros_like(tail)) + moved[half:, columns]


def place_keys_call(base, place, arrived, keep, other, tail):
    half, width = tail.shape
    shape = jax.ShapeDtypeStruct((2 * half, width // 2), jnp.bfloat16)
    return pl.pallas_call(
        functools.partial(place_keys_kernel, base),
        in_specs=[pl.BlockSpec(memory_space=pltpu.SMEM)] + [pl.BlockSpec(memory_space=pltpu.VMEM)] * 4,
        out_specs=[pl.BlockSpec(memory_space=pltpu.VMEM)] * 2,
        out_shape=[shape, shape],
        name="place_keys",
    )(place, arrived, keep, other, tail)


def program(queries, key_states, value_states, out_grad, seg_ids, handed):
    length = seg_ids.shape[0]
    groups = key_states.shape[1] // HD
    q = queries[0]
    do = out_grad[0]
    width = q.shape[1] // groups
    per_group = width // HD
    index = lax.axis_index("dp").astype(jnp.int32)
    devices = lax.axis_size("dp")
    halfway = devices // 2
    seg = seg_ids.reshape(1, length)
    position = index.reshape(1)
    side = lax.axis_index("sub").astype(jnp.int32).reshape(1)
    onward = [(i, i + halfway) for i in range(halfway)]
    across = [(0, 1), (1, 0)]

    def moved(block, axis, route):
        return lax.ppermute(block, axis, route)

    own = (q, do, key_states, value_states, seg, groups)
    packed, window_keys = packed_call(handed, position, side, *own)
    packed_in = moved(packed, "dp", onward)
    mine = moved(window_keys, "dp", onward)
    last = last_rows_call(*own)
    sets = sender_sets(halfway)

    def route_of(parts):
        return [(i, i + halfway) for part in parts for i in part]

    near = len(sets[0])
    direct = (groups - 1) * 2 * width
    detour = moved(last[:, direct:], "dp", [(i, i + near) for i in sets[0]])
    place = numbers_call(handed, position, seg, halfway)

    out, dq, give_tail, give_head, keep_tail, keep_head = own_call(handed, position, side, place, *own)
    other_tail = moved(give_tail, "sub", across)
    other_head = moved(give_head, "sub", across)
    other = moved(mine, "sub", across)
    first_in = moved(last[:, :direct], "dp", route_of(sets[:1]))
    detour_in = moved(detour, "dp", [(i + near, i + halfway) for i in sets[0]])
    tail_sum = sum_call(keep_tail, other_tail)
    keys_in = moved(tail_sum, "dp", onward)
    out, dq = place_call(
        functools.partial(place_packed_kernel, groups, per_group), (place, side), (packed_in, mine, other), out, dq
    )

    window = last.shape[0]

    def branch(sizes):
        def run(block):
            arrived = []
            for size, rows in ((1, window // 2), (2, window)):
                parts = [part for part, own_size in zip(sets[1:], sizes) if own_size == size]
                if parts:
                    arrived.append(lax.ppermute(block[window - rows :], "dp", route_of(parts)))
                else:
                    arrived.append(jnp.zeros((rows, block.shape[1]), block.dtype))
            return tuple(arrived)

        return run

    branches = [branch(sizes) for sizes in itertools.product(range(SIZES), repeat=SETS - 1)]
    short_in, full_in = lax.switch(place[BRANCH], branches, last)
    dk, dv = place_keys_call(KEYS, place, keys_in, keep_head, other_head, tail_sum)
    out, dq = place_call(
        functools.partial(place_last_kernel, width, halfway), (place, position), (first_in, detour_in, short_in, full_in), out, dq
    )
    return out[None], dq[None], dk, dv


def solution(mesh):
    return jax.shard_map(
        program,
        mesh=mesh,
        in_specs=(
            P("sub", "dp", "head"),
            P("dp", "head"),
            P("dp", "head"),
            P("sub", "dp", "head"),
            P("dp"),
            P(),
        ),
        out_specs=(
            P("sub", "dp", "head"),
            P("sub", "dp", "head"),
            P("dp", ("head", "sub")),
            P("dp", ("head", "sub")),
        ),
        check_vma=False,
    )
```

```python
import functools
import itertools

import jax
import jax.numpy as jnp
from jax import lax
from jax.experimental import pallas as pl
from jax.experimental.pallas import tpu as pltpu
from jax.sharding import PartitionSpec as P


HD = 128
PAD = 16
LOG2E = 1.4426950408889634
MASKED = -1e30
NT = (((1,), (1,)), ((), ()))
NN = (((1,), (0,)), ((), ()))


def dot(a, b, dims):
    return lax.dot_general(a, b, dims, preferred_element_type=jnp.float32)


def any_spec():
    return pl.BlockSpec(memory_space=pl.ANY)


def attention_cost(rows, keys, heads):
    return pl.CostEstimate(
        flops=12 * rows * keys * HD * heads,
        transcendentals=rows * keys * heads,
        bytes_accessed=heads * (rows + keys) * HD * 8,
    )


def fill_bias(key_seg, row_seg, bias_ref, row_offset):
    keys = key_seg.shape[1]
    rows = row_seg.shape[1]
    column = jnp.transpose(jnp.broadcast_to(key_seg.astype(jnp.float32), (HD, keys)))
    for begin in range(0, rows, HD):
        row = row_seg[:, begin : begin + HD].astype(jnp.float32)
        key_index = lax.broadcasted_iota(jnp.int32, (keys, HD), 0)
        row_index = lax.broadcasted_iota(jnp.int32, (keys, HD), 1) + (row_offset + begin)
        allowed = (column == row) & (key_index <= row_index) & (row >= 0)
        bias_ref[:, begin : begin + HD] = jnp.where(allowed, 0.0, MASKED)


def head_scores(q, do, k, v, bias_ref, live):
    scale = HD**-0.5
    x = dot(k, q, NT) * (scale * LOG2E) + bias_ref[...]
    p = jnp.exp2(x - jnp.max(x, axis=0, keepdims=True))
    inverse = jnp.where(live, 1.0 / jnp.sum(p, axis=0, keepdims=True), 0.0)
    w = p * inverse
    dp = dot(v, do, NT)
    delta = jnp.sum(w * dp, axis=0, keepdims=True)
    return w, w * (dp - delta)


def heads_of(ref, j):
    return ref[:, j * HD : (j + 1) * HD]


def packed_offset(moved, window):
    return jnp.minimum((2 * window - moved) // PAD, window // PAD) * PAD


def stacked(block, per_group):
    return jnp.concatenate([block[:, j * HD : (j + 1) * HD] for j in range(per_group)], axis=0)


def packed_kernel(per_group, handed_ref, position_ref, side_ref, q_ref, do_ref, k_ref, v_ref, seg_ref, pack_ref, key_ref, bias_ref, live_ref):
    window = q_ref.shape[0] // 2
    offset = pl.multiple_of(packed_offset(handed_ref[position_ref[0]], window), PAD)
    slots = pl.ds(offset, window)

    @pl.when(pl.program_id(0) == 0)
    def _():
        seg = jnp.broadcast_to(seg_ref[...].astype(jnp.float32), (8, 2 * window))
        seg = pltpu.roll(seg, 2 * window - offset, 1)[0:1, :window]
        fill_bias(seg, seg, bias_ref, 0)
        live_ref[...] = jnp.broadcast_to(seg, (8, window))
        for j in range(1, per_group):
            bias_ref[:, j * window : (j + 1) * window] = bias_ref[:, :window]

    live = jnp.concatenate([live_ref[0:1, :]] * per_group, axis=1) >= 0
    k = k_ref[slots, :]
    v = v_ref[slots, :]
    q = stacked(q_ref[slots, :], per_group)
    do = stacked(do_ref[slots, :], per_group)
    w, ds = head_scores(q, do, k, v, bias_ref, live)
    key_index = lax.broadcasted_iota(jnp.int32, (window, window), 0)
    row_index = lax.broadcasted_iota(jnp.int32, (window, window), 1)
    for j in range(per_group):
        columns = slice(j * window, (j + 1) * window)
        packed = jnp.where(key_index <= row_index, w[:, columns], jnp.transpose(ds[:, columns]))
        pack_ref[:, columns] = packed.astype(jnp.bfloat16)
    key_ref[...] = jnp.where(side_ref[0] == 0, k, v)


def packed_call(handed, position, side, q, do, k, v, seg, groups):
    length, row_width = q.shape
    half = length // 2
    window = half // 2
    width = row_width // groups
    per_group = width // HD
    row_spec = pl.BlockSpec((half, width), lambda g, *_: (1, g))
    key_spec = pl.BlockSpec((half, HD), lambda g, *_: (1, g))
    grid_spec = pltpu.PrefetchScalarGridSpec(
        num_scalar_prefetch=3,
        grid=(groups,),
        in_specs=[row_spec, row_spec, key_spec, key_spec, pl.BlockSpec((1, half), lambda g, *_: (0, 1))],
        out_specs=[
            pl.BlockSpec((window, per_group * window), lambda g, *_: (0, g)),
            pl.BlockSpec((window, HD), lambda g, *_: (0, g)),
        ],
        scratch_shapes=[pltpu.VMEM((window, per_group * window), jnp.float32), pltpu.VMEM((8, window), jnp.float32)],
    )
    return pl.pallas_call(
        functools.partial(packed_kernel, per_group),
        grid_spec=grid_spec,
        out_shape=[
            jax.ShapeDtypeStruct((window, groups * per_group * window), jnp.bfloat16),
            jax.ShapeDtypeStruct((window, groups * HD), jnp.bfloat16),
        ],
        cost_estimate=attention_cost(window, window, per_group * groups),
        name="packed_window",
    )(handed, position, side, q, do, k, v, seg)


def last_rows_kernel(per_group, q_ref, do_ref, k_ref, v_ref, seg_ref, send_ref, bias_ref):
    window, width = q_ref.shape

    @pl.when(pl.program_id(0) == 0)
    def _():
        fill_bias(seg_ref[...], seg_ref[:, window:], bias_ref, window)
        for j in range(1, per_group):
            bias_ref[:, j * window : (j + 1) * window] = bias_ref[:, :window]

    live = jnp.concatenate([seg_ref[:, window:]] * per_group, axis=1) >= 0
    k = k_ref[...]
    v = v_ref[...]
    q = stacked(q_ref[...], per_group)
    do = stacked(do_ref[...], per_group)
    w, ds = head_scores(q, do, k, v, bias_ref, live)
    out = dot(jnp.transpose(v), w.astype(jnp.bfloat16), NN)
    dq = dot(jnp.transpose(k), ds.astype(jnp.bfloat16), NN) * HD**-0.5
    for j in range(per_group):
        rows = slice(j * window, (j + 1) * window)
        send_ref[:, j * HD : (j + 1) * HD] = jnp.transpose(out[:, rows]).astype(jnp.bfloat16)
        send_ref[:, width + j * HD : width + (j + 1) * HD] = jnp.transpose(dq[:, rows]).astype(jnp.bfloat16)


def last_rows_call(q, do, k, v, seg, groups):
    length, row_width = q.shape
    window = length // 4
    width = row_width // groups
    per_group = width // HD
    row_spec = pl.BlockSpec((window, width), lambda g: (3, g))
    key_spec = pl.BlockSpec((2 * window, HD), lambda g: (1, g))
    return pl.pallas_call(
        functools.partial(last_rows_kernel, per_group),
        grid=(groups,),
        in_specs=[row_spec, row_spec, key_spec, key_spec, pl.BlockSpec((1, 2 * window), lambda g: (0, 1))],
        out_specs=pl.BlockSpec((window, 2 * width), lambda g: (0, g)),
        out_shape=jax.ShapeDtypeStruct((window, 2 * row_width), jnp.bfloat16),
        scratch_shapes=[pltpu.VMEM((2 * window, per_group * window), jnp.float32)],
        cost_estimate=attention_cost(window, 2 * window, per_group * groups),
        name="last_rows",
    )(q, do, k, v, seg)


def own_kernel(split, per_group, handed_ref, position_ref, side_ref, place_ref, q_ref, do_ref, k_ref, v_ref, seg_ref, out_ref, dq_ref, give_tail, give_head, keep_tail, keep_head, bias_ref, dk_ref, dv_ref):
    length = k_ref.shape[0]
    half = length // 2
    window = half // 2
    blocks = length // window

    @pl.when(pl.program_id(0) == 0)
    def _():
        for block in range(blocks):
            rows = slice(block * window, (block + 1) * window)
            fill_bias(seg_ref[...], seg_ref[:, rows], bias_ref.at[block], block * window)

    limit = length - handed_ref[position_ref[0]]
    dk_ref[...] = jnp.zeros_like(dk_ref)
    dv_ref[...] = jnp.zeros_like(dv_ref)

    def row_block(block, carry):
        count = place_ref[COUNTS + block]
        rows = pl.ds(pl.multiple_of(block * window, window), window)
        keep = lax.broadcasted_iota(jnp.int32, (window, HD), 0) + block * window < limit

        def run(size):
            keys = pl.ds(pl.multiple_of((block + 1 - size) * window, window), size * window)
            q = stacked(q_ref[rows, :], per_group)
            do = stacked(do_ref[rows, :], per_group)
            k = k_ref[keys, :]
            v = v_ref[keys, :]
            scale = HD**-0.5
            bias = jnp.concatenate([bias_ref[block, keys, :]] * per_group, axis=1)
            x = dot(k, q, NT) * (scale * LOG2E) + bias
            top = jnp.max(x, axis=0, keepdims=True)
            p = jnp.exp2(x - top)
            live = top > 0.5 * MASKED
            w = p * jnp.where(live, 1.0 / jnp.sum(p, axis=0, keepdims=True), 0.0)
            wb = w.astype(jnp.bfloat16)
            dp = dot(v, do, NT)
            delta = jnp.sum(w * dp, axis=0, keepdims=True)
            ds = (w * (dp - delta)).astype(jnp.bfloat16)
            out = dot(jnp.transpose(v), wb, NN)
            dq = dot(jnp.transpose(k), ds, NN) * scale
            dv_ref[keys, :] += dot(wb, do, NN)
            dk_ref[keys, :] += dot(ds, q, NN)
            for j in range(per_group):
                columns = slice(j * HD, (j + 1) * HD)
                lanes = slice(j * window, (j + 1) * window)
                out_ref[rows, columns] = jnp.where(keep, jnp.transpose(out[:, lanes]), 0.0).astype(jnp.bfloat16)
                dq_ref[rows, columns] = jnp.where(keep, jnp.transpose(dq[:, lanes]), 0.0).astype(jnp.bfloat16)

        for size in range(1, blocks + 1):
            pl.when(count == size)(functools.partial(run, size))

        @pl.when(count == 0)
        def _():
            out_ref[rows, :] = jnp.zeros((window, per_group * HD), jnp.bfloat16)
            dq_ref[rows, :] = jnp.zeros((window, per_group * HD), jnp.bfloat16)

        return carry

    lax.fori_loop(0, blocks, row_block, 0)

    def store(head_ref, tail_ref):
        dk = (dk_ref[...] * HD**-0.5).astype(head_ref.dtype)
        dv = dv_ref[...].astype(head_ref.dtype)
        head_ref[0] = dk[:half]
        head_ref[1] = dv[:half]
        tail_ref[0] = dk[half:]
        tail_ref[1] = dv[half:]

    pl.when(pl.program_id(0) < split)(lambda: store(give_head, give_tail))
    pl.when(pl.program_id(0) >= split)(lambda: store(keep_head, keep_tail))


def key_places(split):
    def group(t, side_ref):
        return ((t // split) ^ (1 - side_ref[0])) * split + t % split

    def give(t):
        return jnp.minimum(t, split - 1)

    def keep(t):
        return jnp.maximum(t - split, 0)

    return group, give, keep


def own_call(handed, position, side, place, q, do, k, v, seg, groups):
    length, row_width = q.shape
    half = length // 2
    width = row_width // groups
    per_group = width // HD
    split = groups // 2
    group, give, keep = key_places(split)
    row_spec = pl.BlockSpec((length, width), lambda t, h, p, s, n: (0, group(t, s)))
    key_spec = pl.BlockSpec((length, HD), lambda t, h, p, s, n: (0, group(t, s)))
    give_spec = pl.BlockSpec((2, half, HD), lambda t, *_: (0, 0, give(t)))
    keep_spec = pl.BlockSpec((2, half, HD), lambda t, *_: (0, 0, keep(t)))
    grid_spec = pltpu.PrefetchScalarGridSpec(
        num_scalar_prefetch=4,
        grid=(groups,),
        in_specs=[row_spec, row_spec, key_spec, key_spec, pl.BlockSpec((1, length), lambda t, *_: (0, 0))],
        out_specs=[row_spec, row_spec, give_spec, give_spec, keep_spec, keep_spec],
        scratch_shapes=[
            pltpu.VMEM((4, length, length // 4), jnp.float32),
            pltpu.VMEM((length, HD), jnp.float32),
            pltpu.VMEM((length, HD), jnp.float32),
        ],
    )
    part = (2, half, split * HD)
    return pl.pallas_call(
        functools.partial(own_kernel, split, per_group),
        grid_spec=grid_spec,
        out_shape=[jax.ShapeDtypeStruct(q.shape, jnp.bfloat16)] * 2
        + [jax.ShapeDtypeStruct(part, jnp.bfloat16)] * 2
        + [jax.ShapeDtypeStruct(part, jnp.float32)] * 2,
        cost_estimate=attention_cost(length, half, per_group * groups),
        name="own_rows",
    )(handed, position, side, place, q, do, k, v, seg)


def sum_kernel(own_ref, other_ref, out_ref):
    width = own_ref.shape[-1]
    for part in range(2):
        out_ref[:, part * width : (part + 1) * width] = (own_ref[part] + other_ref[part]).astype(jnp.bfloat16)


def sum_call(own, other):
    parts, rows, width = own.shape
    return pl.pallas_call(
        sum_kernel,
        in_specs=[pl.BlockSpec(memory_space=pltpu.VMEM)] * 2,
        out_specs=pl.BlockSpec(memory_space=pltpu.VMEM),
        out_shape=jax.ShapeDtypeStruct((rows, parts * width), jnp.bfloat16),
        name="sum_keys",
    )(own, other)


ACTIVE, START, FIRST, SKIP = range(4)
PACKED, LAST, KEYS, BRANCH, COUNTS = 0, 4, 8, 11, 12
SETS = 4
SIZES = 3


def sender_sets(halfway):
    return [[i for i in range(halfway) if i * SETS // halfway == part] for part in range(SETS)]


def numbers_kernel(halfway, window, handed_ref, position_ref, seg_ref, place_ref):
    position = position_ref[0]
    receiver = position >= halfway
    moved = handed_ref[jnp.maximum(position - halfway, 0)]
    added = jnp.where(receiver, moved, 0)
    live = jnp.sum(jnp.where(seg_ref[...] >= 0, 1.0, 0.0)).astype(jnp.int32)
    offset = packed_offset(moved, window)
    top = 4 * window - window - PAD
    late = live + added - window + offset
    place_ref[PACKED + ACTIVE] = receiver.astype(jnp.int32)
    place_ref[PACKED + START] = jnp.minimum(live, top) // PAD
    place_ref[PACKED + FIRST] = live
    place_ref[PACKED + SKIP] = 2 * window - moved - offset
    place_ref[LAST + ACTIVE] = (receiver & (added > window)).astype(jnp.int32)
    place_ref[LAST + START] = jnp.minimum(late, top) // PAD
    place_ref[LAST + FIRST] = late
    place_ref[LAST + SKIP] = offset
    place_ref[KEYS] = live
    place_ref[KEYS + 1] = added
    place_ref[KEYS + 2] = 4 * window - handed_ref[position]
    branch = 0
    for part in sender_sets(halfway)[1:]:
        most = handed_ref[part[0]]
        for i in part[1:]:
            most = jnp.maximum(most, handed_ref[i])
        size = (most > window).astype(jnp.int32) + (most > window + window // 2).astype(jnp.int32)
        branch = branch * SIZES + size
    place_ref[BRANCH] = branch
    seg = seg_ref[...].astype(jnp.float32)
    slot = lax.broadcasted_iota(jnp.int32, seg.shape, 1)
    for block in range(4):
        number = jnp.sum(jnp.where(slot == block * window, seg, 0.0))
        begin = jnp.sum(jnp.where((seg >= 0) & (seg < number), 1.0, 0.0)).astype(jnp.int32)
        place_ref[COUNTS + block] = jnp.where(number >= 0, block + 1 - begin // window, 0)


def numbers_call(handed, position, seg, halfway):
    smem = pl.BlockSpec(memory_space=pltpu.SMEM)
    return pl.pallas_call(
        functools.partial(numbers_kernel, halfway, seg.shape[1] // 4),
        in_specs=[smem, smem, pl.BlockSpec(memory_space=pltpu.VMEM)],
        out_specs=smem,
        out_shape=jax.ShapeDtypeStruct((16,), jnp.int32),
        name="place_numbers",
    )(handed, position, seg)


def pick_matrix(place_ref, base, rows, window):
    row = lax.broadcasted_iota(jnp.int32, (rows, window), 0)
    source = lax.broadcasted_iota(jnp.int32, (rows, window), 1)
    skip = place_ref[base + SKIP]
    offset = place_ref[base + FIRST] - place_ref[base + START] * PAD - skip
    chosen = (row - source == offset) & (source >= skip)
    return jnp.where(chosen, 1.0, 0.0).astype(jnp.bfloat16)


def row_copies(place_ref, base, pairs, sems, first_sem, rows, inward):
    begin = pl.multiple_of(place_ref[base + START] * PAD, PAD)
    copies = []
    for i, (ref, buf, columns) in enumerate(pairs):
        outer = ref.at[pl.ds(begin, rows), columns]
        inner = buf.at[:, columns]
        source, target = (outer, inner) if inward else (inner, outer)
        copies.append(pltpu.make_async_copy(source, target, sems.at[first_sem + i]))
    return copies


def start_all(copies):
    for copy in copies:
        copy.start()


def wait_all(copies):
    for copy in copies:
        copy.wait()


def place_packed_kernel(groups, per_group, place_ref, side_ref, pack_ref, mine_ref, other_ref, old_out, old_dq, out_ref, dq_ref, out_buf, dq_buf, sems):
    window = pack_ref.shape[0]
    rows = out_buf.shape[0]
    every = slice(0, out_buf.shape[1])

    @pl.when(place_ref[PACKED + ACTIVE] == 1)
    def _():
        reads = row_copies(place_ref, PACKED, [(out_ref, out_buf, every), (dq_ref, dq_buf, every)], sems, 0, rows, True)
        start_all(reads)
        pick = pick_matrix(place_ref, PACKED, rows, window)
        first = lax.broadcasted_iota(jnp.int32, (window, window), 0)
        second = lax.broadcasted_iota(jnp.int32, (window, window), 1)
        writes = []
        for g in range(groups):
            mine = heads_of(mine_ref, g)
            other = heads_of(other_ref, g)
            k = jnp.where(side_ref[0] == 0, mine, other)
            v = jnp.where(side_ref[0] == 0, other, mine)
            k_f = k.astype(jnp.float32)
            v_t = jnp.transpose(v)
            outs = []
            grads = []
            for j in range(per_group):
                head = g * per_group + j
                packed = pack_ref[:, head * window : (head + 1) * window].astype(jnp.float32)
                w = jnp.where(first <= second, packed, 0.0).astype(jnp.bfloat16)
                ds = jnp.where(first > second, packed, 0.0)
                outs.append(jnp.transpose(dot(v_t, w, NN)).astype(jnp.bfloat16))
                total = jnp.sum(ds, axis=1, keepdims=True)
                dq = (dot(ds.astype(jnp.bfloat16), k, NN) - total * k_f) * HD**-0.5
                grads.append(dq.astype(jnp.bfloat16))
            moved_out = dot(pick, jnp.concatenate(outs, axis=1), NN).astype(jnp.bfloat16)
            moved_dq = dot(pick, jnp.concatenate(grads, axis=1), NN).astype(jnp.bfloat16)
            if g == 0:
                wait_all(reads)
            columns = slice(g * per_group * HD, (g + 1) * per_group * HD)
            out_buf[:, columns] += moved_out
            dq_buf[:, columns] += moved_dq
            writes += row_copies(
                place_ref, PACKED, [(out_ref, out_buf, columns), (dq_ref, dq_buf, columns)], sems, 2 + 2 * g, rows, False
            )
            start_all(writes[-2:])
        wait_all(writes)


def place_packed_call(place, side, arrays, out, dq, groups):
    window = arrays[0].shape[0]
    rows = window + PAD
    per_group = out.shape[1] // (groups * HD)
    return pl.pallas_call(
        functools.partial(place_packed_kernel, groups, per_group),
        in_specs=[pl.BlockSpec(memory_space=pltpu.SMEM)] * 2
        + [pl.BlockSpec(memory_space=pltpu.VMEM)] * len(arrays)
        + [any_spec()] * 2,
        out_specs=[any_spec()] * 2,
        out_shape=[jax.ShapeDtypeStruct(out.shape, out.dtype)] * 2,
        scratch_shapes=[pltpu.VMEM((rows, out.shape[1]), jnp.bfloat16)] * 2 + [pltpu.SemaphoreType.DMA((2 + 2 * groups,))],
        input_output_aliases={5: 0, 6: 1},
        cost_estimate=pl.CostEstimate(
            flops=8 * rows * window * out.shape[1], transcendentals=0, bytes_accessed=12 * rows * out.shape[1]
        ),
        name="place_packed",
    )(place, side, *arrays, out, dq)


def finish_kernel(groups, halfway, place_ref, position_ref, first_ref, detour_ref, short_ref, full_ref, arrived_keys_ref, keep_ref, other_ref, tail_ref, old_out, old_dq, out_ref, dq_ref, dk_ref, dv_ref, out_buf, dq_buf, rows_buf, keys_buf, arrived_buf, keep_buf, other_buf, tail_buf, sems):
    window = rows_buf.shape[0]
    rows = out_buf.shape[0]
    width = out_buf.shape[1] // groups
    half, both = tail_buf.shape
    part = both // 2
    direct = first_ref.shape[1]
    size = short_ref.shape[0]
    in_first = position_ref[0] < halfway + len(sender_sets(halfway)[0])
    short = jnp.logical_not(in_first) & (place_ref[LAST + SKIP] >= window - size)
    full = jnp.logical_not(in_first) & jnp.logical_not(short)
    active = place_ref[LAST + ACTIVE] == 1
    receiver = place_ref[PACKED + ACTIVE] == 1
    every = slice(0, out_buf.shape[1])

    reads = row_copies(place_ref, LAST, [(out_ref, out_buf, every), (dq_ref, dq_buf, every)], sems, 0, rows, True)
    first_copy = pltpu.make_async_copy(first_ref, rows_buf.at[:, :direct], sems.at[2])
    detour_copy = pltpu.make_async_copy(detour_ref, rows_buf.at[:, direct:], sems.at[3])
    short_copy = pltpu.make_async_copy(short_ref, rows_buf.at[window - size :, :], sems.at[2])
    full_copy = pltpu.make_async_copy(full_ref, rows_buf, sems.at[2])
    key_copies = [
        pltpu.make_async_copy(keep_ref, keep_buf, sems.at[4]),
        pltpu.make_async_copy(other_ref, other_buf, sems.at[5]),
        pltpu.make_async_copy(tail_ref, tail_buf, sems.at[6]),
        pltpu.make_async_copy(arrived_keys_ref, arrived_buf, sems.at[7]),
    ]
    start_all(key_copies)

    @pl.when(active)
    def _():
        start_all(reads)

        @pl.when(in_first)
        def _():
            first_copy.start()
            detour_copy.start()

        @pl.when(short)
        def _():
            rows_buf[: window - size, :] = jnp.zeros((window - size, rows_buf.shape[1]), rows_buf.dtype)
            short_copy.start()

        @pl.when(full)
        def _():
            full_copy.start()

    wait_all(key_copies)
    limit = place_ref[KEYS + 2]
    own_row = lax.broadcasted_iota(jnp.int32, (half, both), 0) + half
    tail = tail_buf[...]
    keys_buf[half:, :] = jnp.where(own_row < limit, tail, jnp.zeros_like(tail))
    for i in range(2):
        columns = slice(i * part, (i + 1) * part)
        keys_buf[:half, columns] = (keep_buf[i] + other_buf[i]).astype(keys_buf.dtype)

    @pl.when(receiver)
    def _():
        length = 2 * half
        row = lax.broadcasted_iota(jnp.int32, (length, half), 0)
        source = lax.broadcasted_iota(jnp.int32, (length, half), 1)
        missing = half - place_ref[KEYS + 1]
        chosen = (row - source == place_ref[KEYS] - missing) & (source >= missing)
        pick = jnp.where(chosen, 1.0, 0.0).astype(jnp.bfloat16)
        keys_buf[...] += dot(pick, arrived_buf[...], NN).astype(keys_buf.dtype)

    key_writes = [
        pltpu.make_async_copy(keys_buf.at[:, :part], dk_ref, sems.at[4]),
        pltpu.make_async_copy(keys_buf.at[:, part:], dv_ref, sems.at[5]),
    ]
    start_all(key_writes)

    @pl.when(active)
    def _():
        @pl.when(in_first)
        def _():
            first_copy.wait()
            detour_copy.wait()

        pl.when(short)(lambda: short_copy.wait())
        pl.when(full)(lambda: full_copy.wait())
        wait_all(reads)
        pick = pick_matrix(place_ref, LAST, rows, window)
        writes = []
        for g in range(groups):
            columns = slice(g * width, (g + 1) * width)
            moved = dot(pick, rows_buf[:, 2 * g * width : 2 * (g + 1) * width], NN).astype(jnp.bfloat16)
            out_buf[:, columns] += moved[:, :width]
            dq_buf[:, columns] += moved[:, width:]
            writes += row_copies(
                place_ref, LAST, [(out_ref, out_buf, columns), (dq_ref, dq_buf, columns)], sems, 8 + 2 * g, rows, False
            )
            start_all(writes[-2:])
        wait_all(writes)

    wait_all(key_writes)


def finish_call(place, position, arrived, keys, out, dq, groups, halfway):
    length, row_width = out.shape
    half = length // 2
    window = half // 2
    rows = window + PAD
    both = keys[-1].shape[1]
    keys_shape = jax.ShapeDtypeStruct((length, both // 2), jnp.bfloat16)
    return pl.pallas_call(
        functools.partial(finish_kernel, groups, halfway),
        in_specs=[pl.BlockSpec(memory_space=pltpu.SMEM)] * 2 + [any_spec()] * 10,
        out_specs=[any_spec()] * 4,
        out_shape=[jax.ShapeDtypeStruct(out.shape, out.dtype)] * 2 + [keys_shape] * 2,
        scratch_shapes=[pltpu.VMEM((rows, row_width), jnp.bfloat16)] * 2
        + [
            pltpu.VMEM((window, 2 * row_width), jnp.bfloat16),
            pltpu.VMEM((length, both), jnp.bfloat16),
            pltpu.VMEM((half, both), jnp.bfloat16),
            pltpu.VMEM((2, half, both // 2), jnp.float32),
            pltpu.VMEM((2, half, both // 2), jnp.bfloat16),
            pltpu.VMEM((half, both), jnp.bfloat16),
            pltpu.SemaphoreType.DMA((8 + 2 * groups,)),
        ],
        input_output_aliases={10: 0, 11: 1},
        name="finish",
    )(place, position, *arrived, *keys, out, dq)


def program(queries, key_states, value_states, out_grad, seg_ids, handed):
    length = seg_ids.shape[0]
    groups = key_states.shape[1] // HD
    q = queries[0]
    do = out_grad[0]
    width = q.shape[1] // groups
    index = lax.axis_index("dp").astype(jnp.int32)
    devices = lax.axis_size("dp")
    halfway = devices // 2
    seg = seg_ids.reshape(1, length)
    position = index.reshape(1)
    side = lax.axis_index("sub").astype(jnp.int32).reshape(1)
    onward = [(i, i + halfway) for i in range(halfway)]
    across = [(0, 1), (1, 0)]

    def moved(block, axis, route):
        return lax.ppermute(block, axis, route)

    own = (q, do, key_states, value_states, seg, groups)
    packed, window_keys = packed_call(handed, position, side, *own)
    packed_in = moved(packed, "dp", onward)
    mine = moved(window_keys, "dp", onward)
    last = last_rows_call(*own)
    sets = sender_sets(halfway)

    def route_of(parts):
        return [(i, i + halfway) for part in parts for i in part]

    near = len(sets[0])
    direct = (groups - 1) * 2 * width
    detour = moved(last[:, direct:], "dp", [(i, i + near) for i in sets[0]])
    place = numbers_call(handed, position, seg, halfway)

    out, dq, give_tail, give_head, keep_tail, keep_head = own_call(handed, position, side, place, *own)
    other_tail = moved(give_tail, "sub", across)
    other_head = moved(give_head, "sub", across)
    other = moved(mine, "sub", across)
    first_in = moved(last[:, :direct], "dp", route_of(sets[:1]))
    detour_in = moved(detour, "dp", [(i + near, i + halfway) for i in sets[0]])
    tail_sum = sum_call(keep_tail, other_tail)
    keys_in = moved(tail_sum, "dp", onward)
    out, dq = place_packed_call(place, side, (packed_in, mine, other), out, dq, groups)

    window = last.shape[0]

    def branch(sizes):
        def run(block):
            arrived = []
            for size, rows in ((1, window // 2), (2, window)):
                parts = [part for part, own_size in zip(sets[1:], sizes) if own_size == size]
                if parts:
                    arrived.append(lax.ppermute(block[window - rows :], "dp", route_of(parts)))
                else:
                    arrived.append(jnp.zeros((rows, block.shape[1]), block.dtype))
            return tuple(arrived)

        return run

    branches = [branch(sizes) for sizes in itertools.product(range(SIZES), repeat=SETS - 1)]
    short_in, full_in = lax.switch(place[BRANCH], branches, last)
    out, dq, dk, dv = finish_call(
        place,
        position,
        (first_in, detour_in, short_in, full_in),
        (keys_in, keep_head, other_head, tail_sum),
        out,
        dq,
        groups,
        halfway,
    )
    return out[None], dq[None], dk, dv


def solution(mesh):
    return jax.shard_map(
        program,
        mesh=mesh,
        in_specs=(
            P("sub", "dp", "head"),
            P("dp", "head"),
            P("dp", "head"),
            P("sub", "dp", "head"),
            P("dp"),
            P(),
        ),
        out_specs=(
            P("sub", "dp", "head"),
            P("sub", "dp", "head"),
            P("dp", ("head", "sub")),
            P("dp", ("head", "sub")),
        ),
        check_vma=False,
    )
```

```python
import functools
import itertools

import jax
import jax.numpy as jnp
from jax import lax
from jax.experimental import pallas as pl
from jax.experimental.pallas import tpu as pltpu
from jax.sharding import PartitionSpec as P


HD = 128
PAD = 16
LOG2E = 1.4426950408889634
MASKED = -1e30
NT = (((1,), (1,)), ((), ()))
NN = (((1,), (0,)), ((), ()))


def dot(a, b, dims):
    return lax.dot_general(a, b, dims, preferred_element_type=jnp.float32)


def any_spec():
    return pl.BlockSpec(memory_space=pl.ANY)


def attention_cost(rows, keys, heads):
    return pl.CostEstimate(
        flops=12 * rows * keys * HD * heads,
        transcendentals=rows * keys * heads,
        bytes_accessed=heads * (rows + keys) * HD * 8,
    )


def fill_bias(key_seg, row_seg, bias_ref, row_offset):
    keys = key_seg.shape[1]
    rows = row_seg.shape[1]
    column = jnp.transpose(jnp.broadcast_to(key_seg.astype(jnp.float32), (HD, keys)))
    for begin in range(0, rows, HD):
        row = row_seg[:, begin : begin + HD].astype(jnp.float32)
        key_index = lax.broadcasted_iota(jnp.int32, (keys, HD), 0)
        row_index = lax.broadcasted_iota(jnp.int32, (keys, HD), 1) + (row_offset + begin)
        allowed = (column == row) & (key_index <= row_index) & (row >= 0)
        bias_ref[:, begin : begin + HD] = jnp.where(allowed, 0.0, MASKED)


def head_scores(q, do, k, v, bias_ref, live):
    scale = HD**-0.5
    x = dot(k, q, NT) * (scale * LOG2E) + bias_ref[...]
    p = jnp.exp2(x - jnp.max(x, axis=0, keepdims=True))
    inverse = jnp.where(live, 1.0 / jnp.sum(p, axis=0, keepdims=True), 0.0)
    w = p * inverse
    dp = dot(v, do, NT)
    delta = jnp.sum(w * dp, axis=0, keepdims=True)
    return w, w * (dp - delta)


def heads_of(ref, j):
    return ref[:, j * HD : (j + 1) * HD]


def packed_offset(moved, window):
    return jnp.minimum((2 * window - moved) // PAD, window // PAD) * PAD


def stacked(block, per_group):
    return jnp.concatenate([block[:, j * HD : (j + 1) * HD] for j in range(per_group)], axis=0)


def packed_kernel(per_group, handed_ref, position_ref, side_ref, q_ref, do_ref, k_ref, v_ref, seg_ref, pack_ref, key_ref, bias_ref, live_ref):
    window = q_ref.shape[0] // 2
    offset = pl.multiple_of(packed_offset(handed_ref[position_ref[0]], window), PAD)
    slots = pl.ds(offset, window)

    @pl.when(pl.program_id(0) == 0)
    def _():
        seg = jnp.broadcast_to(seg_ref[...].astype(jnp.float32), (8, 2 * window))
        seg = pltpu.roll(seg, 2 * window - offset, 1)[0:1, :window]
        fill_bias(seg, seg, bias_ref, 0)
        live_ref[...] = jnp.broadcast_to(seg, (8, window))
        for j in range(1, per_group):
            bias_ref[:, j * window : (j + 1) * window] = bias_ref[:, :window]

    live = jnp.concatenate([live_ref[0:1, :]] * per_group, axis=1) >= 0
    k = k_ref[slots, :]
    v = v_ref[slots, :]
    q = stacked(q_ref[slots, :], per_group)
    do = stacked(do_ref[slots, :], per_group)
    w, ds = head_scores(q, do, k, v, bias_ref, live)
    key_index = lax.broadcasted_iota(jnp.int32, (window, window), 0)
    row_index = lax.broadcasted_iota(jnp.int32, (window, window), 1)
    for j in range(per_group):
        columns = slice(j * window, (j + 1) * window)
        packed = jnp.where(key_index <= row_index, w[:, columns], jnp.transpose(ds[:, columns]))
        pack_ref[:, columns] = packed.astype(jnp.bfloat16)
    key_ref[...] = jnp.where(side_ref[0] == 0, k, v)


def packed_call(handed, position, side, q, do, k, v, seg, groups):
    length, row_width = q.shape
    half = length // 2
    window = half // 2
    width = row_width // groups
    per_group = width // HD
    row_spec = pl.BlockSpec((half, width), lambda g, *_: (1, g))
    key_spec = pl.BlockSpec((half, HD), lambda g, *_: (1, g))
    grid_spec = pltpu.PrefetchScalarGridSpec(
        num_scalar_prefetch=3,
        grid=(groups,),
        in_specs=[row_spec, row_spec, key_spec, key_spec, pl.BlockSpec((1, half), lambda g, *_: (0, 1))],
        out_specs=[
            pl.BlockSpec((window, per_group * window), lambda g, *_: (0, g)),
            pl.BlockSpec((window, HD), lambda g, *_: (0, g)),
        ],
        scratch_shapes=[pltpu.VMEM((window, per_group * window), jnp.float32), pltpu.VMEM((8, window), jnp.float32)],
    )
    return pl.pallas_call(
        functools.partial(packed_kernel, per_group),
        grid_spec=grid_spec,
        out_shape=[
            jax.ShapeDtypeStruct((window, groups * per_group * window), jnp.bfloat16),
            jax.ShapeDtypeStruct((window, groups * HD), jnp.bfloat16),
        ],
        cost_estimate=attention_cost(window, window, per_group * groups),
        name="packed_window",
    )(handed, position, side, q, do, k, v, seg)


def last_rows_kernel(per_group, q_ref, do_ref, k_ref, v_ref, seg_ref, send_ref, bias_ref):
    window, width = q_ref.shape

    @pl.when(pl.program_id(0) == 0)
    def _():
        fill_bias(seg_ref[...], seg_ref[:, window:], bias_ref, window)
        for j in range(1, per_group):
            bias_ref[:, j * window : (j + 1) * window] = bias_ref[:, :window]

    live = jnp.concatenate([seg_ref[:, window:]] * per_group, axis=1) >= 0
    k = k_ref[...]
    v = v_ref[...]
    q = stacked(q_ref[...], per_group)
    do = stacked(do_ref[...], per_group)
    w, ds = head_scores(q, do, k, v, bias_ref, live)
    out = dot(jnp.transpose(v), w.astype(jnp.bfloat16), NN)
    dq = dot(jnp.transpose(k), ds.astype(jnp.bfloat16), NN) * HD**-0.5
    for j in range(per_group):
        rows = slice(j * window, (j + 1) * window)
        send_ref[:, j * HD : (j + 1) * HD] = jnp.transpose(out[:, rows]).astype(jnp.bfloat16)
        send_ref[:, width + j * HD : width + (j + 1) * HD] = jnp.transpose(dq[:, rows]).astype(jnp.bfloat16)


def last_rows_call(q, do, k, v, seg, groups):
    length, row_width = q.shape
    window = length // 4
    width = row_width // groups
    per_group = width // HD
    row_spec = pl.BlockSpec((window, width), lambda g: (3, g))
    key_spec = pl.BlockSpec((2 * window, HD), lambda g: (1, g))
    return pl.pallas_call(
        functools.partial(last_rows_kernel, per_group),
        grid=(groups,),
        in_specs=[row_spec, row_spec, key_spec, key_spec, pl.BlockSpec((1, 2 * window), lambda g: (0, 1))],
        out_specs=pl.BlockSpec((window, 2 * width), lambda g: (0, g)),
        out_shape=jax.ShapeDtypeStruct((window, 2 * row_width), jnp.bfloat16),
        scratch_shapes=[pltpu.VMEM((2 * window, per_group * window), jnp.float32)],
        cost_estimate=attention_cost(window, 2 * window, per_group * groups),
        name="last_rows",
    )(q, do, k, v, seg)


def own_kernel(split, per_group, handed_ref, position_ref, side_ref, place_ref, q_ref, do_ref, k_ref, v_ref, seg_ref, out_ref, dq_ref, give_tail, give_head, keep_tail, keep_head, bias_ref, dk_ref, dv_ref):
    length = k_ref.shape[0]
    half = length // 2
    window = half // 2
    blocks = length // window

    @pl.when(pl.program_id(0) == 0)
    def _():
        for block in range(blocks):
            rows = slice(block * window, (block + 1) * window)
            fill_bias(seg_ref[...], seg_ref[:, rows], bias_ref.at[block], block * window)

    limit = length - handed_ref[position_ref[0]]
    dk_ref[...] = jnp.zeros_like(dk_ref)
    dv_ref[...] = jnp.zeros_like(dv_ref)

    def row_block(block, carry):
        count = place_ref[COUNTS + block]
        rows = pl.ds(pl.multiple_of(block * window, window), window)
        keep = lax.broadcasted_iota(jnp.int32, (window, HD), 0) + block * window < limit

        def run(size):
            keys = pl.ds(pl.multiple_of((block + 1 - size) * window, window), size * window)
            q = stacked(q_ref[rows, :], per_group)
            do = stacked(do_ref[rows, :], per_group)
            k = k_ref[keys, :]
            v = v_ref[keys, :]
            scale = HD**-0.5
            bias = jnp.concatenate([bias_ref[block, keys, :]] * per_group, axis=1)
            x = dot(k, q, NT) * (scale * LOG2E) + bias
            top = jnp.max(x, axis=0, keepdims=True)
            p = jnp.exp2(x - top)
            live = top > 0.5 * MASKED
            w = p * jnp.where(live, 1.0 / jnp.sum(p, axis=0, keepdims=True), 0.0)
            wb = w.astype(jnp.bfloat16)
            dp = dot(v, do, NT)
            delta = jnp.sum(w * dp, axis=0, keepdims=True)
            ds = (w * (dp - delta)).astype(jnp.bfloat16)
            out = dot(jnp.transpose(v), wb, NN)
            dq = dot(jnp.transpose(k), ds, NN) * scale
            dv_ref[keys, :] += dot(wb, do, NN)
            dk_ref[keys, :] += dot(ds, q, NN)
            for j in range(per_group):
                columns = slice(j * HD, (j + 1) * HD)
                lanes = slice(j * window, (j + 1) * window)
                out_ref[rows, columns] = jnp.where(keep, jnp.transpose(out[:, lanes]), 0.0).astype(jnp.bfloat16)
                dq_ref[rows, columns] = jnp.where(keep, jnp.transpose(dq[:, lanes]), 0.0).astype(jnp.bfloat16)

        for size in range(1, blocks + 1):
            pl.when(count == size)(functools.partial(run, size))

        @pl.when(count == 0)
        def _():
            out_ref[rows, :] = jnp.zeros((window, per_group * HD), jnp.bfloat16)
            dq_ref[rows, :] = jnp.zeros((window, per_group * HD), jnp.bfloat16)

        return carry

    lax.fori_loop(0, blocks, row_block, 0)

    def store(head_ref, tail_ref):
        dk = (dk_ref[...] * HD**-0.5).astype(head_ref.dtype)
        dv = dv_ref[...].astype(head_ref.dtype)
        head_ref[0] = dk[:half]
        head_ref[1] = dv[:half]
        tail_ref[0] = dk[half:]
        tail_ref[1] = dv[half:]

    pl.when(pl.program_id(0) < split)(lambda: store(give_head, give_tail))
    pl.when(pl.program_id(0) >= split)(lambda: store(keep_head, keep_tail))


def key_places(split):
    def group(t, side_ref):
        return ((t // split) ^ (1 - side_ref[0])) * split + t % split

    def give(t):
        return jnp.minimum(t, split - 1)

    def keep(t):
        return jnp.maximum(t - split, 0)

    return group, give, keep


def own_call(handed, position, side, place, q, do, k, v, seg, groups):
    length, row_width = q.shape
    half = length // 2
    width = row_width // groups
    per_group = width // HD
    split = groups // 2
    group, give, keep = key_places(split)
    row_spec = pl.BlockSpec((length, width), lambda t, h, p, s, n: (0, group(t, s)))
    key_spec = pl.BlockSpec((length, HD), lambda t, h, p, s, n: (0, group(t, s)))
    give_spec = pl.BlockSpec((2, half, HD), lambda t, *_: (0, 0, give(t)))
    keep_spec = pl.BlockSpec((2, half, HD), lambda t, *_: (0, 0, keep(t)))
    grid_spec = pltpu.PrefetchScalarGridSpec(
        num_scalar_prefetch=4,
        grid=(groups,),
        in_specs=[row_spec, row_spec, key_spec, key_spec, pl.BlockSpec((1, length), lambda t, *_: (0, 0))],
        out_specs=[row_spec, row_spec, give_spec, give_spec, keep_spec, keep_spec],
        scratch_shapes=[
            pltpu.VMEM((4, length, length // 4), jnp.float32),
            pltpu.VMEM((length, HD), jnp.float32),
            pltpu.VMEM((length, HD), jnp.float32),
        ],
    )
    part = (2, half, split * HD)
    return pl.pallas_call(
        functools.partial(own_kernel, split, per_group),
        grid_spec=grid_spec,
        out_shape=[jax.ShapeDtypeStruct(q.shape, jnp.bfloat16)] * 2
        + [jax.ShapeDtypeStruct(part, jnp.bfloat16)] * 2
        + [jax.ShapeDtypeStruct(part, jnp.float32)] * 2,
        cost_estimate=attention_cost(length, half, per_group * groups),
        name="own_rows",
    )(handed, position, side, place, q, do, k, v, seg)


def sum_kernel(own_ref, other_ref, out_ref):
    width = own_ref.shape[-1]
    for part in range(2):
        out_ref[:, part * width : (part + 1) * width] = (own_ref[part] + other_ref[part]).astype(jnp.bfloat16)


def sum_call(own, other):
    parts, rows, width = own.shape
    return pl.pallas_call(
        sum_kernel,
        in_specs=[pl.BlockSpec(memory_space=pltpu.VMEM)] * 2,
        out_specs=pl.BlockSpec(memory_space=pltpu.VMEM),
        out_shape=jax.ShapeDtypeStruct((rows, parts * width), jnp.bfloat16),
        name="sum_keys",
    )(own, other)


ACTIVE, START, FIRST, SKIP = range(4)
PACKED, LAST, KEYS, BRANCH, COUNTS, PART, SIZE, NUMBERS = 0, 4, 8, 11, 12, 16, 17, 24
SETS = 4
SIZES = 3


def sender_sets(halfway):
    return [[i for i in range(halfway) if i * SETS // halfway == part] for part in range(SETS)]


def numbers_kernel(halfway, window, handed_ref, position_ref, seg_ref, place_ref):
    position = position_ref[0]
    receiver = position >= halfway
    moved = handed_ref[jnp.maximum(position - halfway, 0)]
    added = jnp.where(receiver, moved, 0)
    live = jnp.sum(jnp.where(seg_ref[...] >= 0, 1.0, 0.0)).astype(jnp.int32)
    offset = packed_offset(moved, window)
    top = 4 * window - window - PAD
    late = live + added - window + offset
    place_ref[PACKED + ACTIVE] = receiver.astype(jnp.int32)
    place_ref[PACKED + START] = jnp.minimum(live, top) // PAD
    place_ref[PACKED + FIRST] = live
    place_ref[PACKED + SKIP] = 2 * window - moved - offset
    place_ref[LAST + ACTIVE] = (receiver & (added > window)).astype(jnp.int32)
    place_ref[LAST + START] = jnp.minimum(late, top) // PAD
    place_ref[LAST + FIRST] = late
    place_ref[LAST + SKIP] = offset
    place_ref[KEYS] = live
    place_ref[KEYS + 1] = added
    place_ref[KEYS + 2] = 4 * window - handed_ref[position]
    branch = 0
    partner = jnp.maximum(position - halfway, 0)
    place_ref[PART] = partner * SETS // halfway
    own_size = 0
    for index, part in enumerate(sender_sets(halfway)):
        most = handed_ref[part[0]]
        for i in part[1:]:
            most = jnp.maximum(most, handed_ref[i])
        size = (most > window).astype(jnp.int32) + (most > window + window // 2).astype(jnp.int32)
        own_size = jnp.where((partner >= part[0]) & (partner <= part[-1]), size, own_size)
        if index > 0:
            branch = branch * SIZES + size
    place_ref[SIZE] = own_size
    place_ref[BRANCH] = branch
    seg = seg_ref[...].astype(jnp.float32)
    slot = lax.broadcasted_iota(jnp.int32, seg.shape, 1)
    for block in range(4):
        number = jnp.sum(jnp.where(slot == block * window, seg, 0.0))
        begin = jnp.sum(jnp.where((seg >= 0) & (seg < number), 1.0, 0.0)).astype(jnp.int32)
        place_ref[COUNTS + block] = jnp.where(number >= 0, block + 1 - begin // window, 0)


def numbers_call(handed, position, seg, halfway):
    smem = pl.BlockSpec(memory_space=pltpu.SMEM)
    return pl.pallas_call(
        functools.partial(numbers_kernel, halfway, seg.shape[1] // 4),
        in_specs=[smem, smem, pl.BlockSpec(memory_space=pltpu.VMEM)],
        out_specs=smem,
        out_shape=jax.ShapeDtypeStruct((NUMBERS,), jnp.int32),
        name="place_numbers",
    )(handed, position, seg)


def pick_matrix(place_ref, base, rows, window):
    row = lax.broadcasted_iota(jnp.int32, (rows, window), 0)
    source = lax.broadcasted_iota(jnp.int32, (rows, window), 1)
    skip = place_ref[base + SKIP]
    offset = place_ref[base + FIRST] - place_ref[base + START] * PAD - skip
    chosen = (row - source == offset) & (source >= skip)
    return jnp.where(chosen, 1.0, 0.0).astype(jnp.bfloat16)


def row_copies(place_ref, base, pairs, sems, first_sem, rows, inward):
    begin = pl.multiple_of(place_ref[base + START] * PAD, PAD)
    copies = []
    for i, (ref, buf, columns) in enumerate(pairs):
        outer = ref.at[pl.ds(begin, rows), columns]
        inner = buf.at[:, columns]
        source, target = (outer, inner) if inward else (inner, outer)
        copies.append(pltpu.make_async_copy(source, target, sems.at[first_sem + i]))
    return copies


def start_all(copies):
    for copy in copies:
        copy.start()


def wait_all(copies):
    for copy in copies:
        copy.wait()


def place_packed_kernel(groups, per_group, place_ref, side_ref, pack_ref, mine_ref, other_ref, old_out, old_dq, out_ref, dq_ref, out_buf, dq_buf, sems):
    window = pack_ref.shape[0]
    rows = out_buf.shape[0]
    every = slice(0, out_buf.shape[1])

    @pl.when(place_ref[PACKED + ACTIVE] == 1)
    def _():
        reads = row_copies(place_ref, PACKED, [(out_ref, out_buf, every), (dq_ref, dq_buf, every)], sems, 0, rows, True)
        start_all(reads)
        pick = pick_matrix(place_ref, PACKED, rows, window)
        first = lax.broadcasted_iota(jnp.int32, (window, window), 0)
        second = lax.broadcasted_iota(jnp.int32, (window, window), 1)
        writes = []
        for g in range(groups):
            mine = heads_of(mine_ref, g)
            other = heads_of(other_ref, g)
            k = jnp.where(side_ref[0] == 0, mine, other)
            v = jnp.where(side_ref[0] == 0, other, mine)
            k_f = k.astype(jnp.float32)
            v_t = jnp.transpose(v)
            outs = []
            grads = []
            for j in range(per_group):
                head = g * per_group + j
                packed = pack_ref[:, head * window : (head + 1) * window].astype(jnp.float32)
                w = jnp.where(first <= second, packed, 0.0).astype(jnp.bfloat16)
                ds = jnp.where(first > second, packed, 0.0)
                outs.append(jnp.transpose(dot(v_t, w, NN)).astype(jnp.bfloat16))
                total = jnp.sum(ds, axis=1, keepdims=True)
                dq = (dot(ds.astype(jnp.bfloat16), k, NN) - total * k_f) * HD**-0.5
                grads.append(dq.astype(jnp.bfloat16))
            moved_out = dot(pick, jnp.concatenate(outs, axis=1), NN).astype(jnp.bfloat16)
            moved_dq = dot(pick, jnp.concatenate(grads, axis=1), NN).astype(jnp.bfloat16)
            if g == 0:
                wait_all(reads)
            columns = slice(g * per_group * HD, (g + 1) * per_group * HD)
            out_buf[:, columns] += moved_out
            dq_buf[:, columns] += moved_dq
            writes += row_copies(
                place_ref, PACKED, [(out_ref, out_buf, columns), (dq_ref, dq_buf, columns)], sems, 2 + 2 * g, rows, False
            )
            start_all(writes[-2:])
        wait_all(writes)


def place_packed_call(place, side, arrays, out, dq, groups):
    window = arrays[0].shape[0]
    rows = window + PAD
    per_group = out.shape[1] // (groups * HD)
    return pl.pallas_call(
        functools.partial(place_packed_kernel, groups, per_group),
        in_specs=[pl.BlockSpec(memory_space=pltpu.SMEM)] * 2
        + [pl.BlockSpec(memory_space=pltpu.VMEM)] * len(arrays)
        + [any_spec()] * 2,
        out_specs=[any_spec()] * 2,
        out_shape=[jax.ShapeDtypeStruct(out.shape, out.dtype)] * 2,
        scratch_shapes=[pltpu.VMEM((rows, out.shape[1]), jnp.bfloat16)] * 2 + [pltpu.SemaphoreType.DMA((2 + 2 * groups,))],
        input_output_aliases={5: 0, 6: 1},
        cost_estimate=pl.CostEstimate(
            flops=8 * rows * window * out.shape[1], transcendentals=0, bytes_accessed=12 * rows * out.shape[1]
        ),
        name="place_packed",
    )(place, side, *arrays, out, dq)


def finish_kernel(groups, place_ref, first_ref, part_ref, detour_ref, short_ref, full_ref, long_keys_ref, short_keys_ref, keep_ref, other_ref, tail_ref, old_out, old_dq, out_ref, dq_ref, dk_ref, dv_ref, out_buf, dq_buf, rows_buf, keys_buf, arrived_buf, keep_buf, other_buf, tail_buf, sems):
    window = rows_buf.shape[0]
    rows = out_buf.shape[0]
    width = out_buf.shape[1] // groups
    half, both = tail_buf.shape
    part = both // 2
    direct = first_ref.shape[1]
    aside = direct + part_ref.shape[1]
    size = short_ref.shape[0]
    few = short_keys_ref.shape[0]
    in_first = place_ref[PART] == 0
    short = jnp.logical_not(in_first) & (place_ref[SIZE] == 1)
    full = jnp.logical_not(in_first) & (place_ref[SIZE] == 2)
    many = in_first | (place_ref[SIZE] > 0)
    active = place_ref[LAST + ACTIVE] == 1
    receiver = place_ref[PACKED + ACTIVE] == 1
    every = slice(0, out_buf.shape[1])

    reads = row_copies(place_ref, LAST, [(out_ref, out_buf, every), (dq_ref, dq_buf, every)], sems, 0, rows, True)
    part_copies = [
        pltpu.make_async_copy(first_ref, rows_buf.at[:, :direct], sems.at[2]),
        pltpu.make_async_copy(part_ref, rows_buf.at[:, direct:aside], sems.at[3]),
        pltpu.make_async_copy(detour_ref, rows_buf.at[:, aside:], sems.at[6]),
    ]
    short_copy = pltpu.make_async_copy(short_ref, rows_buf.at[window - size :, :], sems.at[2])
    full_copy = pltpu.make_async_copy(full_ref, rows_buf, sems.at[2])
    many_copy = pltpu.make_async_copy(long_keys_ref, arrived_buf, sems.at[7])
    few_copy = pltpu.make_async_copy(short_keys_ref, arrived_buf.at[half - few :, :], sems.at[7])
    key_copies = [
        pltpu.make_async_copy(keep_ref, keep_buf, sems.at[4]),
        pltpu.make_async_copy(other_ref, other_buf, sems.at[5]),
        pltpu.make_async_copy(tail_ref, tail_buf, sems.at[8]),
    ]
    start_all(key_copies)

    @pl.when(receiver)
    def _():
        pl.when(many)(lambda: many_copy.start())

        @pl.when(jnp.logical_not(many))
        def _():
            arrived_buf[: half - few, :] = jnp.zeros((half - few, both), arrived_buf.dtype)
            few_copy.start()

    @pl.when(active)
    def _():
        start_all(reads)

        pl.when(in_first)(lambda: start_all(part_copies))

        @pl.when(short)
        def _():
            rows_buf[: window - size, :] = jnp.zeros((window - size, rows_buf.shape[1]), rows_buf.dtype)
            short_copy.start()

        @pl.when(full)
        def _():
            full_copy.start()

    wait_all(key_copies)
    limit = place_ref[KEYS + 2]
    own_row = lax.broadcasted_iota(jnp.int32, (half, both), 0) + half
    tail = tail_buf[...]
    keys_buf[half:, :] = jnp.where(own_row < limit, tail, jnp.zeros_like(tail))
    for i in range(2):
        columns = slice(i * part, (i + 1) * part)
        keys_buf[:half, columns] = (keep_buf[i] + other_buf[i]).astype(keys_buf.dtype)

    @pl.when(receiver)
    def _():
        pl.when(many)(lambda: many_copy.wait())
        pl.when(jnp.logical_not(many))(lambda: few_copy.wait())
        length = 2 * half
        row = lax.broadcasted_iota(jnp.int32, (length, half), 0)
        source = lax.broadcasted_iota(jnp.int32, (length, half), 1)
        missing = half - place_ref[KEYS + 1]
        chosen = (row - source == place_ref[KEYS] - missing) & (source >= missing)
        pick = jnp.where(chosen, 1.0, 0.0).astype(jnp.bfloat16)
        keys_buf[...] += dot(pick, arrived_buf[...], NN).astype(keys_buf.dtype)

    key_writes = [
        pltpu.make_async_copy(keys_buf.at[:, :part], dk_ref, sems.at[4]),
        pltpu.make_async_copy(keys_buf.at[:, part:], dv_ref, sems.at[5]),
    ]
    start_all(key_writes)

    @pl.when(active)
    def _():
        pl.when(in_first)(lambda: wait_all(part_copies))
        pl.when(short)(lambda: short_copy.wait())
        pl.when(full)(lambda: full_copy.wait())
        wait_all(reads)
        pick = pick_matrix(place_ref, LAST, rows, window)
        writes = []
        for g in range(groups):
            columns = slice(g * width, (g + 1) * width)
            moved = dot(pick, rows_buf[:, 2 * g * width : 2 * (g + 1) * width], NN).astype(jnp.bfloat16)
            out_buf[:, columns] += moved[:, :width]
            dq_buf[:, columns] += moved[:, width:]
            writes += row_copies(
                place_ref, LAST, [(out_ref, out_buf, columns), (dq_ref, dq_buf, columns)], sems, 9 + 2 * g, rows, False
            )
            start_all(writes[-2:])
        wait_all(writes)

    wait_all(key_writes)


def finish_call(place, arrived, keys, out, dq, groups):
    length, row_width = out.shape
    half = length // 2
    window = half // 2
    rows = window + PAD
    both = keys[-1].shape[1]
    keys_shape = jax.ShapeDtypeStruct((length, both // 2), jnp.bfloat16)
    count = 1 + len(arrived) + len(keys)
    return pl.pallas_call(
        functools.partial(finish_kernel, groups),
        in_specs=[pl.BlockSpec(memory_space=pltpu.SMEM)] + [any_spec()] * (count + 1),
        out_specs=[any_spec()] * 4,
        out_shape=[jax.ShapeDtypeStruct(out.shape, out.dtype)] * 2 + [keys_shape] * 2,
        scratch_shapes=[pltpu.VMEM((rows, row_width), jnp.bfloat16)] * 2
        + [
            pltpu.VMEM((window, 2 * row_width), jnp.bfloat16),
            pltpu.VMEM((length, both), jnp.bfloat16),
            pltpu.VMEM((half, both), jnp.bfloat16),
            pltpu.VMEM((2, half, both // 2), jnp.float32),
            pltpu.VMEM((2, half, both // 2), jnp.bfloat16),
            pltpu.VMEM((half, both), jnp.bfloat16),
            pltpu.SemaphoreType.DMA((9 + 2 * groups,)),
        ],
        input_output_aliases={count: 0, count + 1: 1},
        name="finish",
    )(place, *arrived, *keys, out, dq)


def unfilled(shape, dtype):
    return pl.pallas_call(
        lambda ref: None, out_specs=any_spec(), out_shape=jax.ShapeDtypeStruct(shape, dtype), name="unfilled"
    )()


def aside_choice(sizes):
    def keys(size):
        return 1 if size == 0 else 2

    first, second, third = sizes

    def longest(aside):
        own = 2 * (1 - aside) + 4 * second + 2 + keys(second)
        other = 2 * aside + 4 * (first + third) + keys(first) + keys(third)
        return max(own, other)

    return int(longest(1) < longest(0))


def program(queries, key_states, value_states, out_grad, seg_ids, handed):
    length = seg_ids.shape[0]
    groups = key_states.shape[1] // HD
    q = queries[0]
    do = out_grad[0]
    index = lax.axis_index("dp").astype(jnp.int32)
    devices = lax.axis_size("dp")
    halfway = devices // 2
    seg = seg_ids.reshape(1, length)
    position = index.reshape(1)
    side = lax.axis_index("sub").astype(jnp.int32).reshape(1)
    onward = [(i, i + halfway) for i in range(halfway)]
    across = [(0, 1), (1, 0)]

    def moved(block, axis, route):
        return lax.ppermute(block, axis, route)

    own = (q, do, key_states, value_states, seg, groups)
    packed, window_keys = packed_call(handed, position, side, *own)
    packed_in = moved(packed, "dp", onward)
    mine = moved(window_keys, "dp", onward)
    last = last_rows_call(*own)
    sets = sender_sets(halfway)

    def route_of(parts):
        return [(i, i + halfway) for part in parts for i in part]

    near = len(sets[0])
    quarter = last.shape[1] // 4
    aside = moved(last[:, 2 * quarter :], "dp", [(i, i + near) for i in sets[0]])
    around = [(i + near, i + halfway) for i in sets[0]]
    place = numbers_call(handed, position, seg, halfway)

    out, dq, give_tail, give_head, keep_tail, keep_head = own_call(handed, position, side, place, *own)
    other_tail = moved(give_tail, "sub", across)
    other_head = moved(give_head, "sub", across)
    other = moved(mine, "sub", across)
    first_in = moved(last[:, : 2 * quarter], "dp", route_of(sets[:1]))
    detour_in = moved(aside[:, quarter:], "dp", around)
    tail_sum = sum_call(keep_tail, other_tail)
    out, dq = place_packed_call(place, side, (packed_in, mine, other), out, dq, groups)

    window = last.shape[0]

    def branch(sizes):
        def sent(block, parts):
            if parts:
                return lax.ppermute(block, "dp", route_of(parts))
            return unfilled(block.shape, block.dtype)

        def of_size(*wanted):
            return [part for part, size in zip(sets[1:], sizes) if size in wanted]

        def run(rows, other_rows, grads):
            full = sent(rows, of_size(2))
            short = sent(rows[window // 2 :], of_size(1))
            if aside_choice(sizes):
                part = lax.ppermute(other_rows[:, :quarter], "dp", around)
            else:
                part = sent(rows[:, 2 * quarter : 3 * quarter], sets[:1])
            long_keys = sent(grads, sets[:1] + of_size(1, 2))
            short_keys = sent(grads[window:], of_size(0))
            return part, short, full, long_keys, short_keys

        return run

    branches = [branch(sizes) for sizes in itertools.product(range(SIZES), repeat=SETS - 1)]
    part_in, *others_in = lax.switch(place[BRANCH], branches, last, aside, tail_sum)
    short_in, full_in, *keys_in = others_in
    out, dq, dk, dv = finish_call(
        place, (first_in, part_in, detour_in, short_in, full_in), (*keys_in, keep_head, other_head, tail_sum), out, dq, groups
    )
    return out[None], dq[None], dk, dv


def solution(mesh):
    return jax.shard_map(
        program,
        mesh=mesh,
        in_specs=(
            P("sub", "dp", "head"),
            P("dp", "head"),
            P("dp", "head"),
            P("sub", "dp", "head"),
            P("dp"),
            P(),
        ),
        out_specs=(
            P("sub", "dp", "head"),
            P("sub", "dp", "head"),
            P("dp", ("head", "sub")),
            P("dp", ("head", "sub")),
        ),
        check_vma=False,
    )
```

```python
import functools
import itertools

import jax
import jax.numpy as jnp
from jax import lax
from jax.experimental import pallas as pl
from jax.experimental.pallas import tpu as pltpu
from jax.sharding import PartitionSpec as P


HD = 128
PAD = 16
GRANT = 24 * 1024 * 1024
LOG2E = 1.4426950408889634
MASKED = -1e30
NT = (((1,), (1,)), ((), ()))
NN = (((1,), (0,)), ((), ()))


def dot(a, b, dims):
    return lax.dot_general(a, b, dims, preferred_element_type=jnp.float32)


def any_spec():
    return pl.BlockSpec(memory_space=pl.ANY)


def start_all(copies):
    for copy in copies:
        copy.start()


def wait_all(copies):
    for copy in copies:
        copy.wait()


def attention_cost(rows, keys, heads):
    return pl.CostEstimate(
        flops=12 * rows * keys * HD * heads,
        transcendentals=rows * keys * heads,
        bytes_accessed=heads * (rows + keys) * HD * 8,
    )


def fill_bias(key_seg, row_seg, bias_ref, row_offset):
    keys = key_seg.shape[1]
    rows = row_seg.shape[1]
    column = jnp.transpose(jnp.broadcast_to(key_seg.astype(jnp.float32), (HD, keys)))
    for begin in range(0, rows, HD):
        row = row_seg[:, begin : begin + HD].astype(jnp.float32)
        key_index = lax.broadcasted_iota(jnp.int32, (keys, HD), 0)
        row_index = lax.broadcasted_iota(jnp.int32, (keys, HD), 1) + (row_offset + begin)
        allowed = (column == row) & (key_index <= row_index) & (row >= 0)
        bias_ref[:, begin : begin + HD] = jnp.where(allowed, 0.0, MASKED)


def head_scores(q, do, k, v, bias_ref, live):
    scale = HD**-0.5
    x = dot(k, q, NT) * (scale * LOG2E) + bias_ref[...]
    p = jnp.exp2(x - jnp.max(x, axis=0, keepdims=True))
    inverse = jnp.where(live, 1.0 / jnp.sum(p, axis=0, keepdims=True), 0.0)
    w = p * inverse
    dp = dot(v, do, NT)
    delta = jnp.sum(w * dp, axis=0, keepdims=True)
    return w, w * (dp - delta)


def heads_of(ref, j):
    return ref[:, j * HD : (j + 1) * HD]


def packed_offset(moved, window):
    return jnp.minimum((2 * window - moved) // PAD, window // PAD) * PAD


def stacked(block, per_group):
    return jnp.concatenate([block[:, j * HD : (j + 1) * HD] for j in range(per_group)], axis=0)


def packed_kernel(halfway, groups, handed_ref, position_ref, side_ref, q_ref, do_ref, k_ref, v_ref, seg_ref, pack_ref, key_ref, q_buf, do_buf, k_buf, v_buf, pack_buf, bias_ref, sems):
    window, row_width = q_buf.shape
    width = row_width // groups
    per_group = width // HD
    half = 2 * window
    position = position_ref[0]

    @pl.when(position < halfway)
    def _():
        offset = packed_offset(handed_ref[position], window)
        slots = pl.ds(pl.multiple_of(half + offset, PAD), window)
        key_reads = [
            pltpu.make_async_copy(k_ref.at[slots, :], k_buf, sems.at[0]),
            pltpu.make_async_copy(v_ref.at[slots, :], v_buf, sems.at[1]),
        ]
        start_all(key_reads)
        row_reads = []
        for g in range(groups):
            columns = slice(g * width, (g + 1) * width)
            row_reads.append(
                [
                    pltpu.make_async_copy(ref.at[slots, columns], buf.at[:, columns], sems.at[2 + 2 * g + i])
                    for i, (ref, buf) in enumerate(((q_ref, q_buf), (do_ref, do_buf)))
                ]
            )
            start_all(row_reads[-1])
        seg = jnp.broadcast_to(seg_ref[:, half:].astype(jnp.float32), (8, half))
        seg = pltpu.roll(seg, half - offset, 1)[0:1, :window]
        fill_bias(seg, seg, bias_ref, 0)
        for j in range(1, per_group):
            bias_ref[:, j * window : (j + 1) * window] = bias_ref[:, :window]
        live = jnp.concatenate([seg] * per_group, axis=1) >= 0
        key_index = lax.broadcasted_iota(jnp.int32, (window, window), 0)
        row_index = lax.broadcasted_iota(jnp.int32, (window, window), 1)
        wait_all(key_reads)
        k_write = pltpu.make_async_copy(k_buf, key_ref, sems.at[0])
        v_write = pltpu.make_async_copy(v_buf, key_ref, sems.at[0])
        pl.when(side_ref[0] == 0)(lambda: k_write.start())
        pl.when(side_ref[0] != 0)(lambda: v_write.start())
        writes = []
        for g in range(groups):
            wait_all(row_reads[g])
            columns = slice(g * width, (g + 1) * width)
            q = stacked(q_buf[:, columns], per_group)
            do = stacked(do_buf[:, columns], per_group)
            w, ds = head_scores(q, do, heads_of(k_buf, g), heads_of(v_buf, g), bias_ref, live)
            begin = g * per_group * window
            for j in range(per_group):
                lanes = slice(j * window, (j + 1) * window)
                packed = jnp.where(key_index <= row_index, w[:, lanes], jnp.transpose(ds[:, lanes]))
                pack_buf[:, begin + j * window : begin + (j + 1) * window] = packed.astype(jnp.bfloat16)
            part = slice(begin, begin + per_group * window)
            writes.append(pltpu.make_async_copy(pack_buf.at[:, part], pack_ref.at[:, part], sems.at[2 + 2 * g]))
            writes[-1].start()
        pl.when(side_ref[0] == 0)(lambda: k_write.wait())
        pl.when(side_ref[0] != 0)(lambda: v_write.wait())
        wait_all(writes)


def packed_call(handed, position, side, q, do, k, v, seg, groups):
    length, row_width = q.shape
    window = length // 4
    per_group = row_width // (groups * HD)
    smem = pl.BlockSpec(memory_space=pltpu.SMEM)
    pack_width = groups * per_group * window
    return pl.pallas_call(
        functools.partial(packed_kernel, lax.axis_size("dp") // 2, groups),
        in_specs=[smem] * 3 + [any_spec()] * 4 + [pl.BlockSpec(memory_space=pltpu.VMEM)],
        out_specs=[any_spec()] * 2,
        out_shape=[
            jax.ShapeDtypeStruct((window, pack_width), jnp.bfloat16),
            jax.ShapeDtypeStruct((window, groups * HD), jnp.bfloat16),
        ],
        scratch_shapes=[pltpu.VMEM((window, row_width), jnp.bfloat16)] * 2
        + [pltpu.VMEM((window, groups * HD), jnp.bfloat16)] * 2
        + [
            pltpu.VMEM((window, pack_width), jnp.bfloat16),
            pltpu.VMEM((window, per_group * window), jnp.float32),
            pltpu.SemaphoreType.DMA((2 + 2 * groups,)),
        ],
        cost_estimate=attention_cost(window, window, per_group * groups),
        name="packed_window",
    )(handed, position, side, q, do, k, v, seg)


def last_rows_kernel(halfway, per_group, position_ref, q_ref, do_ref, k_ref, v_ref, seg_ref, send_ref, bias_ref):
    window, width = q_ref.shape

    sender = position_ref[0] < halfway

    @pl.when((pl.program_id(0) == 0) & sender)
    def _():
        fill_bias(seg_ref[...], seg_ref[:, window:], bias_ref, window)
        for j in range(1, per_group):
            bias_ref[:, j * window : (j + 1) * window] = bias_ref[:, :window]

    @pl.when(sender)
    def _():
        live = jnp.concatenate([seg_ref[:, window:]] * per_group, axis=1) >= 0
        k = k_ref[...]
        v = v_ref[...]
        q = stacked(q_ref[...], per_group)
        do = stacked(do_ref[...], per_group)
        w, ds = head_scores(q, do, k, v, bias_ref, live)
        out = dot(jnp.transpose(v), w.astype(jnp.bfloat16), NN)
        dq = dot(jnp.transpose(k), ds.astype(jnp.bfloat16), NN) * HD**-0.5
        for j in range(per_group):
            rows = slice(j * window, (j + 1) * window)
            send_ref[:, j * HD : (j + 1) * HD] = jnp.transpose(out[:, rows]).astype(jnp.bfloat16)
            send_ref[:, width + j * HD : width + (j + 1) * HD] = jnp.transpose(dq[:, rows]).astype(jnp.bfloat16)


def last_rows_call(position, q, do, k, v, seg, groups):
    length, row_width = q.shape
    window = length // 4
    width = row_width // groups
    per_group = width // HD
    row_spec = pl.BlockSpec((window, width), lambda g, *_: (3, g))
    key_spec = pl.BlockSpec((2 * window, HD), lambda g, *_: (1, g))
    grid_spec = pltpu.PrefetchScalarGridSpec(
        num_scalar_prefetch=1,
        grid=(groups,),
        in_specs=[row_spec, row_spec, key_spec, key_spec, pl.BlockSpec((1, 2 * window), lambda g, *_: (0, 1))],
        out_specs=pl.BlockSpec((window, 2 * width), lambda g, *_: (0, g)),
        scratch_shapes=[pltpu.VMEM((2 * window, per_group * window), jnp.float32)],
    )
    return pl.pallas_call(
        functools.partial(last_rows_kernel, lax.axis_size("dp") // 2, per_group),
        grid_spec=grid_spec,
        out_shape=jax.ShapeDtypeStruct((window, 2 * row_width), jnp.bfloat16),
        cost_estimate=attention_cost(window, 2 * window, per_group * groups),
        name="last_rows",
    )(position, q, do, k, v, seg)


def own_rows(base, per_group, limit, place_ref, q_ref, do_ref, k_ref, v_ref, bias_ref, out_ref, dq_ref, dk_ref, dv_ref):
    window = q_ref.shape[0] // 2

    def row_block(index, carry):
        block = base + index
        count = place_ref[COUNTS + block]
        rows = pl.ds(pl.multiple_of(index * window, window), window)

        def run(size):
            keys = pl.ds(pl.multiple_of((block + 1 - size) * window, window), size * window)
            q = stacked(q_ref[rows, :], per_group)
            do = stacked(do_ref[rows, :], per_group)
            k = k_ref[keys, :]
            v = v_ref[keys, :]
            scale = HD**-0.5
            bias = jnp.concatenate([bias_ref[index, keys, :]] * per_group, axis=1)
            x = dot(k, q, NT) * (scale * LOG2E) + bias
            top = jnp.max(x, axis=0, keepdims=True)
            p = jnp.exp2(x - top)
            live = top > 0.5 * MASKED
            w = p * jnp.where(live, 1.0 / jnp.sum(p, axis=0, keepdims=True), 0.0)
            wb = w.astype(jnp.bfloat16)
            dp = dot(v, do, NT)
            delta = jnp.sum(w * dp, axis=0, keepdims=True)
            ds = (w * (dp - delta)).astype(jnp.bfloat16)
            out = dot(jnp.transpose(v), wb, NN)
            dq = dot(jnp.transpose(k), ds, NN) * scale
            dv_ref[keys, :] += dot(wb, do, NN)
            dk_ref[keys, :] += dot(ds, q, NN)
            keep = None
            if limit is not None:
                keep = lax.broadcasted_iota(jnp.int32, (window, HD), 0) + block * window < limit
            for j in range(per_group):
                columns = slice(j * HD, (j + 1) * HD)
                lanes = slice(j * window, (j + 1) * window)
                for ref, value in ((out_ref, out), (dq_ref, dq)):
                    value = jnp.transpose(value[:, lanes])
                    if keep is not None:
                        value = jnp.where(keep, value, 0.0)
                    ref[rows, columns] = value.astype(jnp.bfloat16)

        for size in range(1, base + 3):
            pl.when(count == size)(functools.partial(run, size))

        @pl.when(count == 0)
        def _():
            out_ref[rows, :] = jnp.zeros((window, per_group * HD), jnp.bfloat16)
            dq_ref[rows, :] = jnp.zeros((window, per_group * HD), jnp.bfloat16)

        return carry

    lax.fori_loop(0, 2, row_block, 0)


def fill_biases(seg_ref, bias_ref, base, keys):
    window = bias_ref.shape[2]

    @pl.when(pl.program_id(0) == 0)
    def _():
        for index in range(2):
            begin = (base + index) * window
            fill_bias(seg_ref[:, :keys], seg_ref[:, begin : begin + window], bias_ref.at[index], begin)


def tail_kernel(split, per_group, handed_ref, position_ref, side_ref, place_ref, q_ref, do_ref, k_ref, v_ref, seg_ref, out_ref, dq_ref, give_ref, keep_ref, part_ref, bias_ref, dk_ref, dv_ref):
    length = k_ref.shape[0]
    half = length // 2
    fill_biases(seg_ref, bias_ref, 2, length)
    dk_ref[...] = jnp.zeros_like(dk_ref)
    dv_ref[...] = jnp.zeros_like(dv_ref)
    limit = length - handed_ref[position_ref[0]]
    own_rows(2, per_group, limit, place_ref, q_ref, do_ref, k_ref, v_ref, bias_ref, out_ref, dq_ref, dk_ref, dv_ref)
    part_ref[0] = dk_ref[:half, :]
    part_ref[1] = dv_ref[:half, :]

    def store(ref):
        ref[0] = (dk_ref[half:, :] * HD**-0.5).astype(ref.dtype)
        ref[1] = dv_ref[half:, :].astype(ref.dtype)

    pl.when(pl.program_id(0) < split)(lambda: store(give_ref))
    pl.when(pl.program_id(0) >= split)(lambda: store(keep_ref))


def head_kernel(split, per_group, side_ref, place_ref, q_ref, do_ref, k_ref, v_ref, seg_ref, part_ref, old_out, old_dq, out_ref, dq_ref, give_ref, keep_ref, bias_ref, dk_ref, dv_ref):
    half = k_ref.shape[0]
    fill_biases(seg_ref, bias_ref, 0, half)
    dk_ref[...] = part_ref[0]
    dv_ref[...] = part_ref[1]
    own_rows(0, per_group, None, place_ref, q_ref, do_ref, k_ref, v_ref, bias_ref, out_ref, dq_ref, dk_ref, dv_ref)

    def store(ref):
        ref[0] = (dk_ref[...] * HD**-0.5).astype(ref.dtype)
        ref[1] = dv_ref[...].astype(ref.dtype)

    pl.when(pl.program_id(0) < split)(lambda: store(give_ref))
    pl.when(pl.program_id(0) >= split)(lambda: store(keep_ref))


def key_places(split):
    def group(t, side_ref):
        return ((t // split) ^ (1 - side_ref[0])) * split + t % split

    def give(t):
        return jnp.minimum(t, split - 1)

    def keep(t):
        return jnp.maximum(t - split, 0)

    return group, give, keep


def tail_call(handed, position, side, place, q, do, k, v, seg, groups):
    length, row_width = q.shape
    half = length // 2
    width = row_width // groups
    per_group = width // HD
    split = groups // 2
    group, give, keep = key_places(split)
    row_spec = pl.BlockSpec((half, width), lambda t, h, p, s, n: (1, group(t, s)))
    key_spec = pl.BlockSpec((length, HD), lambda t, h, p, s, n: (0, group(t, s)))
    give_spec = pl.BlockSpec((2, half, HD), lambda t, *_: (0, 0, give(t)))
    keep_spec = pl.BlockSpec((2, half, HD), lambda t, *_: (0, 0, keep(t)))
    part_spec = pl.BlockSpec((2, half, HD), lambda t, *_: (0, 0, t))
    grid_spec = pltpu.PrefetchScalarGridSpec(
        num_scalar_prefetch=4,
        grid=(groups,),
        in_specs=[row_spec, row_spec, key_spec, key_spec, pl.BlockSpec((1, length), lambda t, *_: (0, 0))],
        out_specs=[row_spec, row_spec, give_spec, keep_spec, part_spec],
        scratch_shapes=[
            pltpu.VMEM((2, length, length // 4), jnp.float32),
            pltpu.VMEM((length, HD), jnp.float32),
            pltpu.VMEM((length, HD), jnp.float32),
        ],
    )
    part = (2, half, split * HD)
    return pl.pallas_call(
        functools.partial(tail_kernel, split, per_group),
        grid_spec=grid_spec,
        out_shape=[jax.ShapeDtypeStruct(q.shape, jnp.bfloat16)] * 2
        + [
            jax.ShapeDtypeStruct(part, jnp.bfloat16),
            jax.ShapeDtypeStruct(part, jnp.float32),
            jax.ShapeDtypeStruct((2, half, groups * HD), jnp.float32),
        ],
        cost_estimate=attention_cost(half, half, per_group * groups),
        name="tail_rows",
    )(handed, position, side, place, q, do, k, v, seg)


def head_call(side, place, q, do, k, v, seg, groups, part, out, dq):
    length, row_width = q.shape
    half = length // 2
    width = row_width // groups
    per_group = width // HD
    split = groups // 2
    group, give, keep = key_places(split)
    row_spec = pl.BlockSpec((half, width), lambda t, s, n: (0, group(t, s)))
    key_spec = pl.BlockSpec((half, HD), lambda t, s, n: (0, group(t, s)))
    give_spec = pl.BlockSpec((2, half, HD), lambda t, *_: (0, 0, give(t)))
    keep_spec = pl.BlockSpec((2, half, HD), lambda t, *_: (0, 0, keep(t)))
    part_spec = pl.BlockSpec((2, half, HD), lambda t, *_: (0, 0, t))
    grid_spec = pltpu.PrefetchScalarGridSpec(
        num_scalar_prefetch=2,
        grid=(groups,),
        in_specs=[row_spec, row_spec, key_spec, key_spec, pl.BlockSpec((1, half), lambda t, *_: (0, 0)), part_spec]
        + [any_spec()] * 2,
        out_specs=[row_spec, row_spec, give_spec, keep_spec],
        scratch_shapes=[
            pltpu.VMEM((2, half, half // 2), jnp.float32),
            pltpu.VMEM((half, HD), jnp.float32),
            pltpu.VMEM((half, HD), jnp.float32),
        ],
    )
    part_shape = (2, half, split * HD)
    return pl.pallas_call(
        functools.partial(head_kernel, split, per_group),
        grid_spec=grid_spec,
        out_shape=[jax.ShapeDtypeStruct(q.shape, jnp.bfloat16)] * 2
        + [jax.ShapeDtypeStruct(part_shape, jnp.bfloat16), jax.ShapeDtypeStruct(part_shape, jnp.float32)],
        input_output_aliases={8: 0, 9: 1},
        cost_estimate=attention_cost(half, half, per_group * groups),
        name="head_rows",
    )(side, place, q, do, k, v, seg, part, out, dq)


def sum_kernel(own_ref, other_ref, out_ref):
    width = own_ref.shape[-1]
    for part in range(2):
        out_ref[:, part * width : (part + 1) * width] = (own_ref[part] + other_ref[part]).astype(jnp.bfloat16)


def sum_call(own, other):
    parts, rows, width = own.shape
    return pl.pallas_call(
        sum_kernel,
        in_specs=[pl.BlockSpec(memory_space=pltpu.VMEM)] * 2,
        out_specs=pl.BlockSpec(memory_space=pltpu.VMEM),
        out_shape=jax.ShapeDtypeStruct((rows, parts * width), jnp.bfloat16),
        compiler_params=pltpu.CompilerParams(vmem_limit_bytes=GRANT),
        name="sum_keys",
    )(own, other)


ACTIVE, START, FIRST, SKIP = range(4)
PACKED, LAST, KEYS, COUNTS, PART, SIZE, NUMBERS = 0, 4, 8, 12, 16, 17, 24
SETS = 4
SIZES = 3


def sender_sets(halfway):
    return [[i for i in range(halfway) if i * SETS // halfway == part] for part in range(SETS)]


def column_loads(sizes, aside):
    def keys(size):
        return 1 if size == 0 else 2

    first, second, third = sizes
    own = 2 * (1 - aside) + 4 * second + 2 + keys(second)
    other = 2 * aside + 4 * (first + third) + keys(first) + keys(third)
    return max(own, other)


def aside_choice(sizes):
    return int(column_loads(sizes, 1) < column_loads(sizes, 0))


def branch_menu():
    choices = list(itertools.product(range(SIZES), repeat=SETS - 1))

    def longest(sizes):
        return min(column_loads(sizes, 0), column_loads(sizes, 1))

    def widened(sizes):
        able = [
            other
            for other in choices
            if all(x >= y for x, y in zip(other, sizes)) and longest(other) <= longest(sizes)
        ]
        return max(able, key=lambda other: (sum(other), other))

    menu = sorted({widened(sizes) for sizes in choices})
    return menu, [menu.index(widened(sizes)) for sizes in choices]


def numbers_kernel(halfway, window, handed_ref, position_ref, seg_ref, place_ref, branch_ref):
    position = position_ref[0]
    receiver = position >= halfway
    moved = handed_ref[jnp.maximum(position - halfway, 0)]
    added = jnp.where(receiver, moved, 0)
    live = jnp.sum(jnp.where(seg_ref[...] >= 0, 1.0, 0.0)).astype(jnp.int32)
    offset = packed_offset(moved, window)
    top = 4 * window - window - PAD
    late = live + added - window + offset
    place_ref[PACKED + ACTIVE] = receiver.astype(jnp.int32)
    place_ref[PACKED + START] = jnp.minimum(live, top) // PAD
    place_ref[PACKED + FIRST] = live
    place_ref[PACKED + SKIP] = 2 * window - moved - offset
    place_ref[LAST + ACTIVE] = (receiver & (added > window)).astype(jnp.int32)
    place_ref[LAST + START] = jnp.minimum(late, top) // PAD
    place_ref[LAST + FIRST] = late
    place_ref[LAST + SKIP] = offset
    place_ref[KEYS] = live
    place_ref[KEYS + 1] = added
    place_ref[KEYS + 2] = 4 * window - handed_ref[position]
    partner = jnp.maximum(position - halfway, 0)
    part = partner * SETS // halfway
    place_ref[PART] = part
    choice = 0
    for members in sender_sets(halfway)[1:]:
        most = handed_ref[members[0]]
        for i in members[1:]:
            most = jnp.maximum(most, handed_ref[i])
        size = (most > window).astype(jnp.int32) + (most > window + window // 2).astype(jnp.int32)
        choice = choice * SIZES + size
    menu, branch_of = branch_menu()
    branch = 0
    own_size = 0
    for number, index in enumerate(branch_of):
        branch = jnp.where(choice == number, index, branch)
    for index, sizes in enumerate(menu):
        for member, size in enumerate(sizes):
            own_size = jnp.where((branch == index) & (part == member + 1), size, own_size)
    branch_ref[0] = branch
    place_ref[SIZE] = own_size
    seg = seg_ref[...].astype(jnp.float32)
    slot = lax.broadcasted_iota(jnp.int32, seg.shape, 1)
    for block in range(4):
        number = jnp.sum(jnp.where(slot == block * window, seg, 0.0))
        begin = jnp.sum(jnp.where((seg >= 0) & (seg < number), 1.0, 0.0)).astype(jnp.int32)
        place_ref[COUNTS + block] = jnp.where(number >= 0, block + 1 - begin // window, 0)


def numbers_call(handed, position, seg, halfway):
    smem = pl.BlockSpec(memory_space=pltpu.SMEM)
    return pl.pallas_call(
        functools.partial(numbers_kernel, halfway, seg.shape[1] // 4),
        in_specs=[smem, smem, pl.BlockSpec(memory_space=pltpu.VMEM)],
        out_specs=[smem, smem],
        out_shape=[jax.ShapeDtypeStruct((NUMBERS,), jnp.int32), jax.ShapeDtypeStruct((1,), jnp.int32)],
        name="place_numbers",
    )(handed, position, seg)


def pick_matrix(place_ref, base, rows, window):
    row = lax.broadcasted_iota(jnp.int32, (rows, window), 0)
    source = lax.broadcasted_iota(jnp.int32, (rows, window), 1)
    skip = place_ref[base + SKIP]
    offset = place_ref[base + FIRST] - place_ref[base + START] * PAD - skip
    chosen = (row - source == offset) & (source >= skip)
    return jnp.where(chosen, 1.0, 0.0).astype(jnp.bfloat16)


def row_copies(place_ref, base, pairs, sems, first_sem, rows, inward):
    begin = pl.multiple_of(place_ref[base + START] * PAD, PAD)
    copies = []
    for i, (ref, buf, columns) in enumerate(pairs):
        outer = ref.at[pl.ds(begin, rows), columns]
        inner = buf.at[:, columns]
        source, target = (outer, inner) if inward else (inner, outer)
        copies.append(pltpu.make_async_copy(source, target, sems.at[first_sem + i]))
    return copies


def place_packed_kernel(groups, per_group, place_ref, side_ref, pack, mine, other, old_out, old_dq, out_ref, dq_ref, out_buf, dq_buf, pack_ref, mine_ref, other_ref, sems):
    window = pack_ref.shape[0]
    rows = out_buf.shape[0]
    every = slice(0, out_buf.shape[1])

    @pl.when(place_ref[PACKED + ACTIVE] == 1)
    def _():
        inputs = [
            pltpu.make_async_copy(mine, mine_ref, sems.at[2]),
            pltpu.make_async_copy(other, other_ref, sems.at[3]),
            pltpu.make_async_copy(pack, pack_ref, sems.at[4]),
        ]
        start_all(inputs)
        reads = row_copies(place_ref, PACKED, [(out_ref, out_buf, every), (dq_ref, dq_buf, every)], sems, 0, rows, True)
        start_all(reads)
        pick = pick_matrix(place_ref, PACKED, rows, window)
        wait_all(inputs)
        first = lax.broadcasted_iota(jnp.int32, (window, window), 0)
        second = lax.broadcasted_iota(jnp.int32, (window, window), 1)
        writes = []
        for g in range(groups):
            own = heads_of(mine_ref, g)
            swapped = heads_of(other_ref, g)
            k = jnp.where(side_ref[0] == 0, own, swapped)
            v = jnp.where(side_ref[0] == 0, swapped, own)
            k_f = k.astype(jnp.float32)
            v_t = jnp.transpose(v)
            outs = []
            grads = []
            for j in range(per_group):
                head = g * per_group + j
                packed = pack_ref[:, head * window : (head + 1) * window].astype(jnp.float32)
                w = jnp.where(first <= second, packed, 0.0).astype(jnp.bfloat16)
                ds = jnp.where(first > second, packed, 0.0)
                outs.append(jnp.transpose(dot(v_t, w, NN)).astype(jnp.bfloat16))
                total = jnp.sum(ds, axis=1, keepdims=True)
                dq = (dot(ds.astype(jnp.bfloat16), k, NN) - total * k_f) * HD**-0.5
                grads.append(dq.astype(jnp.bfloat16))
            moved_out = dot(pick, jnp.concatenate(outs, axis=1), NN).astype(jnp.bfloat16)
            moved_dq = dot(pick, jnp.concatenate(grads, axis=1), NN).astype(jnp.bfloat16)
            if g == 0:
                wait_all(reads)
            columns = slice(g * per_group * HD, (g + 1) * per_group * HD)
            out_buf[:, columns] += moved_out
            dq_buf[:, columns] += moved_dq
            writes += row_copies(
                place_ref, PACKED, [(out_ref, out_buf, columns), (dq_ref, dq_buf, columns)], sems, 5 + 2 * g, rows, False
            )
            start_all(writes[-2:])
        wait_all(writes)


def place_packed_call(place, side, arrays, out, dq, groups):
    window = arrays[0].shape[0]
    rows = window + PAD
    row_width = out.shape[1]
    per_group = row_width // (groups * HD)
    count = 2 + len(arrays)
    return pl.pallas_call(
        functools.partial(place_packed_kernel, groups, per_group),
        in_specs=[pl.BlockSpec(memory_space=pltpu.SMEM)] * 2 + [any_spec()] * (len(arrays) + 2),
        out_specs=[any_spec()] * 2,
        out_shape=[jax.ShapeDtypeStruct(out.shape, out.dtype)] * 2,
        scratch_shapes=[pltpu.VMEM((rows, row_width), jnp.bfloat16)] * 2
        + [
            pltpu.VMEM((window, groups * per_group * window), jnp.bfloat16),
            pltpu.VMEM((window, groups * HD), jnp.bfloat16),
            pltpu.VMEM((window, groups * HD), jnp.bfloat16),
            pltpu.SemaphoreType.DMA((5 + 2 * groups,)),
        ],
        input_output_aliases={count: 0, count + 1: 1},
        cost_estimate=pl.CostEstimate(
            flops=8 * rows * window * row_width, transcendentals=0, bytes_accessed=12 * rows * row_width
        ),
        compiler_params=pltpu.CompilerParams(vmem_limit_bytes=GRANT),
        name="place_packed",
    )(place, side, *arrays, out, dq)


def finish_kernel(groups, place_ref, first_ref, second_ref, part_ref, detour_ref, short_ref, full_ref, long_keys_ref, short_keys_ref, keep_ref, other_ref, tail_ref, old_out, old_dq, out_ref, dq_ref, dk_ref, dv_ref, out_buf, dq_buf, rows_buf, keys_buf, arrived_buf, keep_buf, other_buf, tail_buf, sems):
    window = rows_buf.shape[0]
    rows = out_buf.shape[0]
    width = out_buf.shape[1] // groups
    half, both = tail_buf.shape
    part = both // 2
    quarter = first_ref.shape[1]
    size = short_ref.shape[0]
    few = short_keys_ref.shape[0]
    in_first = place_ref[PART] == 0
    short = jnp.logical_not(in_first) & (place_ref[SIZE] == 1)
    full = jnp.logical_not(in_first) & (place_ref[SIZE] == 2)
    many = in_first | (place_ref[SIZE] > 0)
    active = place_ref[LAST + ACTIVE] == 1
    receiver = place_ref[PACKED + ACTIVE] == 1
    every = slice(0, out_buf.shape[1])

    reads = row_copies(place_ref, LAST, [(out_ref, out_buf, every), (dq_ref, dq_buf, every)], sems, 0, rows, True)
    part_copies = [
        pltpu.make_async_copy(ref, rows_buf.at[:, i * quarter : (i + 1) * quarter], sems.at[sem])
        for i, (ref, sem) in enumerate(((first_ref, 2), (second_ref, 3), (part_ref, 6), (detour_ref, 9 + 2 * groups)))
    ]
    short_copy = pltpu.make_async_copy(short_ref, rows_buf.at[window - size :, :], sems.at[2])
    full_copy = pltpu.make_async_copy(full_ref, rows_buf, sems.at[2])
    many_copy = pltpu.make_async_copy(long_keys_ref, arrived_buf, sems.at[7])
    few_copy = pltpu.make_async_copy(short_keys_ref, arrived_buf.at[half - few :, :], sems.at[7])
    key_copies = [
        pltpu.make_async_copy(keep_ref, keep_buf, sems.at[4]),
        pltpu.make_async_copy(other_ref, other_buf, sems.at[5]),
        pltpu.make_async_copy(tail_ref, tail_buf, sems.at[8]),
    ]
    start_all(key_copies)

    @pl.when(receiver)
    def _():
        pl.when(many)(lambda: many_copy.start())

        @pl.when(jnp.logical_not(many))
        def _():
            arrived_buf[: half - few, :] = jnp.zeros((half - few, both), arrived_buf.dtype)
            few_copy.start()

    @pl.when(active)
    def _():
        start_all(reads)

        pl.when(in_first)(lambda: start_all(part_copies))

        @pl.when(short)
        def _():
            rows_buf[: window - size, :] = jnp.zeros((window - size, rows_buf.shape[1]), rows_buf.dtype)
            short_copy.start()

        @pl.when(full)
        def _():
            full_copy.start()

    wait_all(key_copies)
    limit = place_ref[KEYS + 2]
    own_row = lax.broadcasted_iota(jnp.int32, (half, both), 0) + half
    tail = tail_buf[...]
    keys_buf[half:, :] = jnp.where(own_row < limit, tail, jnp.zeros_like(tail))
    for i in range(2):
        columns = slice(i * part, (i + 1) * part)
        keys_buf[:half, columns] = (keep_buf[i] + other_buf[i]).astype(keys_buf.dtype)

    @pl.when(receiver)
    def _():
        pl.when(many)(lambda: many_copy.wait())
        pl.when(jnp.logical_not(many))(lambda: few_copy.wait())
        length = 2 * half
        row = lax.broadcasted_iota(jnp.int32, (length, half), 0)
        source = lax.broadcasted_iota(jnp.int32, (length, half), 1)
        missing = half - place_ref[KEYS + 1]
        chosen = (row - source == place_ref[KEYS] - missing) & (source >= missing)
        pick = jnp.where(chosen, 1.0, 0.0).astype(jnp.bfloat16)
        keys_buf[...] += dot(pick, arrived_buf[...], NN).astype(keys_buf.dtype)

    key_writes = [
        pltpu.make_async_copy(keys_buf.at[:, :part], dk_ref, sems.at[4]),
        pltpu.make_async_copy(keys_buf.at[:, part:], dv_ref, sems.at[5]),
    ]
    start_all(key_writes)

    @pl.when(active)
    def _():
        pl.when(in_first)(lambda: wait_all(part_copies))
        pl.when(short)(lambda: short_copy.wait())
        pl.when(full)(lambda: full_copy.wait())
        wait_all(reads)
        pick = pick_matrix(place_ref, LAST, rows, window)
        writes = []
        for g in range(groups):
            columns = slice(g * width, (g + 1) * width)
            moved = dot(pick, rows_buf[:, 2 * g * width : 2 * (g + 1) * width], NN).astype(jnp.bfloat16)
            out_buf[:, columns] += moved[:, :width]
            dq_buf[:, columns] += moved[:, width:]
            writes += row_copies(
                place_ref, LAST, [(out_ref, out_buf, columns), (dq_ref, dq_buf, columns)], sems, 9 + 2 * g, rows, False
            )
            start_all(writes[-2:])
        wait_all(writes)

    wait_all(key_writes)


def finish_call(place, arrived, keys, out, dq, groups):
    length, row_width = out.shape
    half = length // 2
    window = half // 2
    rows = window + PAD
    both = keys[-1].shape[1]
    keys_shape = jax.ShapeDtypeStruct((length, both // 2), jnp.bfloat16)
    count = 1 + len(arrived) + len(keys)
    return pl.pallas_call(
        functools.partial(finish_kernel, groups),
        in_specs=[pl.BlockSpec(memory_space=pltpu.SMEM)] + [any_spec()] * (count + 1),
        out_specs=[any_spec()] * 4,
        out_shape=[jax.ShapeDtypeStruct(out.shape, out.dtype)] * 2 + [keys_shape] * 2,
        scratch_shapes=[pltpu.VMEM((rows, row_width), jnp.bfloat16)] * 2
        + [
            pltpu.VMEM((window, 2 * row_width), jnp.bfloat16),
            pltpu.VMEM((length, both), jnp.bfloat16),
            pltpu.VMEM((half, both), jnp.bfloat16),
            pltpu.VMEM((2, half, both // 2), jnp.float32),
            pltpu.VMEM((2, half, both // 2), jnp.bfloat16),
            pltpu.VMEM((half, both), jnp.bfloat16),
            pltpu.SemaphoreType.DMA((10 + 2 * groups,)),
        ],
        input_output_aliases={count: 0, count + 1: 1},
        compiler_params=pltpu.CompilerParams(vmem_limit_bytes=GRANT),
        name="finish",
    )(place, *arrived, *keys, out, dq)


def unfilled(shape, dtype):
    return pl.pallas_call(
        lambda ref: None, out_specs=any_spec(), out_shape=jax.ShapeDtypeStruct(shape, dtype), name="unfilled"
    )()


def program(queries, key_states, value_states, out_grad, seg_ids, handed):
    length = seg_ids.shape[0]
    groups = key_states.shape[1] // HD
    q = queries[0]
    do = out_grad[0]
    index = lax.axis_index("dp").astype(jnp.int32)
    devices = lax.axis_size("dp")
    halfway = devices // 2
    seg = seg_ids.reshape(1, length)
    position = index.reshape(1)
    side = lax.axis_index("sub").astype(jnp.int32).reshape(1)
    onward = [(i, i + halfway) for i in range(halfway)]
    across = [(0, 1), (1, 0)]

    def moved(block, axis, route):
        return lax.ppermute(block, axis, route)

    own = (q, do, key_states, value_states, seg, groups)
    packed, window_keys = packed_call(handed, position, side, *own)
    packed_in = moved(packed, "dp", onward)
    mine = moved(window_keys, "dp", onward)
    last = last_rows_call(position, *own)
    sets = sender_sets(halfway)

    def route_of(parts):
        return [(i, i + halfway) for part in parts for i in part]

    near = len(sets[0])
    quarter = last.shape[1] // 4
    aside = moved(last[:, 2 * quarter :], "dp", [(i, i + near) for i in sets[0]])
    around = [(i + near, i + halfway) for i in sets[0]]
    first_in = moved(last[:, :quarter], "dp", route_of(sets[:1]))
    place, branch_number = numbers_call(handed, position, seg, halfway)

    out, dq, give_tail, keep_tail, part = tail_call(handed, position, side, place, *own)
    other_tail = moved(give_tail, "sub", across)
    out, dq, give_head, keep_head = head_call(side, place, *own, part, out, dq)
    other_head = moved(give_head, "sub", across)
    other = moved(mine, "sub", across)
    second_in = moved(last[:, quarter : 2 * quarter], "dp", route_of(sets[:1]))
    detour_in = moved(aside[:, quarter:], "dp", around)
    tail_sum = sum_call(keep_tail, other_tail)
    out, dq = place_packed_call(place, side, (packed_in, mine, other), out, dq, groups)

    window = last.shape[0]

    def branch(sizes):
        def sent(block, parts):
            if parts:
                return lax.ppermute(block, "dp", route_of(parts))
            return unfilled(block.shape, block.dtype)

        def of_size(*wanted):
            return [part for part, size in zip(sets[1:], sizes) if size in wanted]

        def run(rows, other_rows, grads):
            full = sent(rows, of_size(2))
            short = sent(rows[window // 2 :], of_size(1))
            if aside_choice(sizes):
                part = lax.ppermute(other_rows[:, :quarter], "dp", around)
            else:
                part = sent(rows[:, 2 * quarter : 3 * quarter], sets[:1])
            long_keys = sent(grads, sets[:1] + of_size(1, 2))
            short_keys = sent(grads[window:], of_size(0))
            return part, short, full, long_keys, short_keys

        return run

    branches = [branch(sizes) for sizes in branch_menu()[0]]
    part_in, *others_in = lax.switch(branch_number[0], branches, last, aside, tail_sum)
    short_in, full_in, *keys_in = others_in
    out, dq, dk, dv = finish_call(
        place, (first_in, second_in, part_in, detour_in, short_in, full_in), (*keys_in, keep_head, other_head, tail_sum), out, dq, groups
    )
    return out[None], dq[None], dk, dv


def solution(mesh):
    return jax.shard_map(
        program,
        mesh=mesh,
        in_specs=(
            P("sub", "dp", "head"),
            P("dp", "head"),
            P("dp", "head"),
            P("sub", "dp", "head"),
            P("dp"),
            P(),
        ),
        out_specs=(
            P("sub", "dp", "head"),
            P("sub", "dp", "head"),
            P("dp", ("head", "sub")),
            P("dp", ("head", "sub")),
        ),
        check_vma=False,
    )
```

```python
import functools
import itertools

import jax
import jax.numpy as jnp
from jax import lax
from jax.experimental import pallas as pl
from jax.experimental.pallas import tpu as pltpu
from jax.sharding import PartitionSpec as P


HD = 128
PAD = 16
GRANT = 24 * 1024 * 1024
LOG2E = 1.4426950408889634
MASKED = -1e30
NT = (((1,), (1,)), ((), ()))
NN = (((1,), (0,)), ((), ()))


def dot(a, b, dims):
    return lax.dot_general(a, b, dims, preferred_element_type=jnp.float32)


def any_spec():
    return pl.BlockSpec(memory_space=pl.ANY)


def start_all(copies):
    for copy in copies:
        copy.start()


def wait_all(copies):
    for copy in copies:
        copy.wait()


def attention_cost(rows, keys, heads):
    return pl.CostEstimate(
        flops=12 * rows * keys * HD * heads,
        transcendentals=rows * keys * heads,
        bytes_accessed=heads * (rows + keys) * HD * 8,
    )


def fill_bias(key_seg, row_seg, bias_ref, row_offset):
    keys = key_seg.shape[1]
    rows = row_seg.shape[1]
    column = jnp.transpose(jnp.broadcast_to(key_seg.astype(jnp.float32), (HD, keys)))
    for begin in range(0, rows, HD):
        row = row_seg[:, begin : begin + HD].astype(jnp.float32)
        key_index = lax.broadcasted_iota(jnp.int32, (keys, HD), 0)
        row_index = lax.broadcasted_iota(jnp.int32, (keys, HD), 1) + (row_offset + begin)
        allowed = (column == row) & (key_index <= row_index) & (row >= 0)
        bias_ref[:, begin : begin + HD] = jnp.where(allowed, 0.0, MASKED)


def head_scores(q, do, k, v, bias_ref, live):
    scale = HD**-0.5
    x = dot(k, q, NT) * (scale * LOG2E) + bias_ref[...]
    p = jnp.exp2(x - jnp.max(x, axis=0, keepdims=True))
    inverse = jnp.where(live, 1.0 / jnp.sum(p, axis=0, keepdims=True), 0.0)
    w = p * inverse
    dp = dot(v, do, NT)
    delta = jnp.sum(w * dp, axis=0, keepdims=True)
    return w, w * (dp - delta)


def heads_of(ref, j):
    return ref[:, j * HD : (j + 1) * HD]


def packed_offset(moved, window):
    return jnp.minimum((2 * window - moved) // PAD, window // PAD) * PAD


def stacked(block, per_group):
    return jnp.concatenate([block[:, j * HD : (j + 1) * HD] for j in range(per_group)], axis=0)


def packed_kernel(halfway, groups, handed_ref, position_ref, side_ref, q_ref, do_ref, k_ref, v_ref, seg_ref, pack_ref, key_ref, q_buf, do_buf, k_buf, v_buf, pack_buf, bias_ref, sems):
    window, row_width = q_buf.shape
    width = row_width // groups
    per_group = width // HD
    half = 2 * window
    position = position_ref[0]

    @pl.when(position < halfway)
    def _():
        offset = packed_offset(handed_ref[position], window)
        slots = pl.ds(pl.multiple_of(half + offset, PAD), window)
        key_reads = [
            pltpu.make_async_copy(k_ref.at[slots, :], k_buf, sems.at[0]),
            pltpu.make_async_copy(v_ref.at[slots, :], v_buf, sems.at[1]),
        ]
        start_all(key_reads)
        row_reads = []
        for g in range(groups):
            columns = slice(g * width, (g + 1) * width)
            row_reads.append(
                [
                    pltpu.make_async_copy(ref.at[slots, columns], buf.at[:, columns], sems.at[2 + 2 * g + i])
                    for i, (ref, buf) in enumerate(((q_ref, q_buf), (do_ref, do_buf)))
                ]
            )
            start_all(row_reads[-1])
        seg = jnp.broadcast_to(seg_ref[:, half:].astype(jnp.float32), (8, half))
        seg = pltpu.roll(seg, half - offset, 1)[0:1, :window]
        fill_bias(seg, seg, bias_ref, 0)
        for j in range(1, per_group):
            bias_ref[:, j * window : (j + 1) * window] = bias_ref[:, :window]
        live = jnp.concatenate([seg] * per_group, axis=1) >= 0
        key_index = lax.broadcasted_iota(jnp.int32, (window, window), 0)
        row_index = lax.broadcasted_iota(jnp.int32, (window, window), 1)
        wait_all(key_reads)
        k_write = pltpu.make_async_copy(k_buf, key_ref, sems.at[0])
        v_write = pltpu.make_async_copy(v_buf, key_ref, sems.at[0])
        pl.when(side_ref[0] == 0)(lambda: k_write.start())
        pl.when(side_ref[0] != 0)(lambda: v_write.start())
        writes = []
        for g in range(groups):
            wait_all(row_reads[g])
            columns = slice(g * width, (g + 1) * width)
            q = stacked(q_buf[:, columns], per_group)
            do = stacked(do_buf[:, columns], per_group)
            w, ds = head_scores(q, do, heads_of(k_buf, g), heads_of(v_buf, g), bias_ref, live)
            begin = g * per_group * window
            for j in range(per_group):
                lanes = slice(j * window, (j + 1) * window)
                packed = jnp.where(key_index <= row_index, w[:, lanes], jnp.transpose(ds[:, lanes]))
                pack_buf[:, begin + j * window : begin + (j + 1) * window] = packed.astype(jnp.bfloat16)
            part = slice(begin, begin + per_group * window)
            writes.append(pltpu.make_async_copy(pack_buf.at[:, part], pack_ref.at[:, part], sems.at[2 + 2 * g]))
            writes[-1].start()
        pl.when(side_ref[0] == 0)(lambda: k_write.wait())
        pl.when(side_ref[0] != 0)(lambda: v_write.wait())
        wait_all(writes)


def packed_call(handed, position, side, q, do, k, v, seg, groups):
    length, row_width = q.shape
    window = length // 4
    per_group = row_width // (groups * HD)
    smem = pl.BlockSpec(memory_space=pltpu.SMEM)
    pack_width = groups * per_group * window
    return pl.pallas_call(
        functools.partial(packed_kernel, lax.axis_size("dp") // 2, groups),
        in_specs=[smem] * 3 + [any_spec()] * 4 + [pl.BlockSpec(memory_space=pltpu.VMEM)],
        out_specs=[any_spec()] * 2,
        out_shape=[
            jax.ShapeDtypeStruct((window, pack_width), jnp.bfloat16),
            jax.ShapeDtypeStruct((window, groups * HD), jnp.bfloat16),
        ],
        scratch_shapes=[pltpu.VMEM((window, row_width), jnp.bfloat16)] * 2
        + [pltpu.VMEM((window, groups * HD), jnp.bfloat16)] * 2
        + [
            pltpu.VMEM((window, pack_width), jnp.bfloat16),
            pltpu.VMEM((window, per_group * window), jnp.float32),
            pltpu.SemaphoreType.DMA((2 + 2 * groups,)),
        ],
        cost_estimate=attention_cost(window, window, per_group * groups),
        name="packed_window",
    )(handed, position, side, q, do, k, v, seg)


def last_rows_kernel(halfway, per_group, handed_ref, position_ref, q_ref, do_ref, k_ref, v_ref, seg_ref, send_ref, bias_ref):
    window, width = q_ref.shape

    sender = (position_ref[0] < halfway) & (handed_ref[position_ref[0]] > window)

    @pl.when((pl.program_id(0) == 0) & sender)
    def _():
        fill_bias(seg_ref[...], seg_ref[:, window:], bias_ref, window)
        for j in range(1, per_group):
            bias_ref[:, j * window : (j + 1) * window] = bias_ref[:, :window]

    @pl.when(sender)
    def _():
        live = jnp.concatenate([seg_ref[:, window:]] * per_group, axis=1) >= 0
        k = k_ref[...]
        v = v_ref[...]
        q = stacked(q_ref[...], per_group)
        do = stacked(do_ref[...], per_group)
        w, ds = head_scores(q, do, k, v, bias_ref, live)
        out = dot(jnp.transpose(v), w.astype(jnp.bfloat16), NN)
        dq = dot(jnp.transpose(k), ds.astype(jnp.bfloat16), NN) * HD**-0.5
        for j in range(per_group):
            rows = slice(j * window, (j + 1) * window)
            send_ref[:, j * HD : (j + 1) * HD] = jnp.transpose(out[:, rows]).astype(jnp.bfloat16)
            send_ref[:, width + j * HD : width + (j + 1) * HD] = jnp.transpose(dq[:, rows]).astype(jnp.bfloat16)


def last_rows_call(handed, position, q, do, k, v, seg, groups):
    length, row_width = q.shape
    window = length // 4
    width = row_width // groups
    per_group = width // HD
    row_spec = pl.BlockSpec((window, width), lambda g, *_: (3, g))
    key_spec = pl.BlockSpec((2 * window, HD), lambda g, *_: (1, g))
    grid_spec = pltpu.PrefetchScalarGridSpec(
        num_scalar_prefetch=2,
        grid=(groups,),
        in_specs=[row_spec, row_spec, key_spec, key_spec, pl.BlockSpec((1, 2 * window), lambda g, *_: (0, 1))],
        out_specs=pl.BlockSpec((window, 2 * width), lambda g, *_: (0, g)),
        scratch_shapes=[pltpu.VMEM((2 * window, per_group * window), jnp.float32)],
    )
    return pl.pallas_call(
        functools.partial(last_rows_kernel, lax.axis_size("dp") // 2, per_group),
        grid_spec=grid_spec,
        out_shape=jax.ShapeDtypeStruct((window, 2 * row_width), jnp.bfloat16),
        cost_estimate=attention_cost(window, 2 * window, per_group * groups),
        name="last_rows",
    )(handed, position, q, do, k, v, seg)


def own_rows(base, per_group, limit, place_ref, q_ref, do_ref, k_ref, v_ref, bias_ref, out_ref, dq_ref, dk_ref, dv_ref):
    window = q_ref.shape[0] // 2

    def row_block(index, carry):
        block = base + index
        count = place_ref[COUNTS + block]
        rows = pl.ds(pl.multiple_of(index * window, window), window)

        def run(size):
            keys = pl.ds(pl.multiple_of((block + 1 - size) * window, window), size * window)
            q = stacked(q_ref[rows, :], per_group)
            do = stacked(do_ref[rows, :], per_group)
            k = k_ref[keys, :]
            v = v_ref[keys, :]
            scale = HD**-0.5
            bias = jnp.concatenate([bias_ref[index, keys, :]] * per_group, axis=1)
            x = dot(k, q, NT) * (scale * LOG2E) + bias
            top = jnp.max(x, axis=0, keepdims=True)
            p = jnp.exp2(x - top)
            live = top > 0.5 * MASKED
            w = p * jnp.where(live, 1.0 / jnp.sum(p, axis=0, keepdims=True), 0.0)
            wb = w.astype(jnp.bfloat16)
            dp = dot(v, do, NT)
            delta = jnp.sum(w * dp, axis=0, keepdims=True)
            ds = (w * (dp - delta)).astype(jnp.bfloat16)
            out = dot(jnp.transpose(v), wb, NN)
            dq = dot(jnp.transpose(k), ds, NN) * scale
            dv_ref[keys, :] += dot(wb, do, NN)
            dk_ref[keys, :] += dot(ds, q, NN)
            keep = None
            if limit is not None:
                keep = lax.broadcasted_iota(jnp.int32, (window, HD), 0) + block * window < limit
            for j in range(per_group):
                columns = slice(j * HD, (j + 1) * HD)
                lanes = slice(j * window, (j + 1) * window)
                for ref, value in ((out_ref, out), (dq_ref, dq)):
                    value = jnp.transpose(value[:, lanes])
                    if keep is not None:
                        value = jnp.where(keep, value, 0.0)
                    ref[rows, columns] = value.astype(jnp.bfloat16)

        for size in range(1, base + 3):
            pl.when(count == size)(functools.partial(run, size))

        @pl.when(count == 0)
        def _():
            out_ref[rows, :] = jnp.zeros((window, per_group * HD), jnp.bfloat16)
            dq_ref[rows, :] = jnp.zeros((window, per_group * HD), jnp.bfloat16)

        return carry

    lax.fori_loop(0, 2, row_block, 0)


def fill_biases(seg_ref, bias_ref, base, keys):
    window = bias_ref.shape[2]

    @pl.when(pl.program_id(0) == 0)
    def _():
        for index in range(2):
            begin = (base + index) * window
            fill_bias(seg_ref[:, :keys], seg_ref[:, begin : begin + window], bias_ref.at[index], begin)


def tail_kernel(split, per_group, handed_ref, position_ref, side_ref, place_ref, q_ref, do_ref, k_ref, v_ref, seg_ref, out_ref, dq_ref, give_ref, keep_ref, part_ref, bias_ref, dk_ref, dv_ref):
    length = k_ref.shape[0]
    half = length // 2
    fill_biases(seg_ref, bias_ref, 2, length)
    dk_ref[...] = jnp.zeros_like(dk_ref)
    dv_ref[...] = jnp.zeros_like(dv_ref)
    limit = length - handed_ref[position_ref[0]]
    own_rows(2, per_group, limit, place_ref, q_ref, do_ref, k_ref, v_ref, bias_ref, out_ref, dq_ref, dk_ref, dv_ref)
    part_ref[0] = dk_ref[:half, :]
    part_ref[1] = dv_ref[:half, :]

    def store(ref):
        ref[0] = (dk_ref[half:, :] * HD**-0.5).astype(ref.dtype)
        ref[1] = dv_ref[half:, :].astype(ref.dtype)

    pl.when(pl.program_id(0) < split)(lambda: store(give_ref))
    pl.when(pl.program_id(0) >= split)(lambda: store(keep_ref))


def head_kernel(split, per_group, side_ref, place_ref, q_ref, do_ref, k_ref, v_ref, seg_ref, part_ref, old_out, old_dq, out_ref, dq_ref, give_ref, keep_ref, bias_ref, dk_ref, dv_ref):
    half = k_ref.shape[0]
    fill_biases(seg_ref, bias_ref, 0, half)
    dk_ref[...] = part_ref[0]
    dv_ref[...] = part_ref[1]
    own_rows(0, per_group, None, place_ref, q_ref, do_ref, k_ref, v_ref, bias_ref, out_ref, dq_ref, dk_ref, dv_ref)

    def store(ref):
        ref[0] = (dk_ref[...] * HD**-0.5).astype(ref.dtype)
        ref[1] = dv_ref[...].astype(ref.dtype)

    pl.when(pl.program_id(0) < split)(lambda: store(give_ref))
    pl.when(pl.program_id(0) >= split)(lambda: store(keep_ref))


def key_places(split):
    def group(t, side_ref):
        return ((t // split) ^ (1 - side_ref[0])) * split + t % split

    def give(t):
        return jnp.minimum(t, split - 1)

    def keep(t):
        return jnp.maximum(t - split, 0)

    return group, give, keep


def tail_call(handed, position, side, place, q, do, k, v, seg, groups):
    length, row_width = q.shape
    half = length // 2
    width = row_width // groups
    per_group = width // HD
    split = groups // 2
    group, give, keep = key_places(split)
    row_spec = pl.BlockSpec((half, width), lambda t, h, p, s, n: (1, group(t, s)))
    key_spec = pl.BlockSpec((length, HD), lambda t, h, p, s, n: (0, group(t, s)))
    give_spec = pl.BlockSpec((2, half, HD), lambda t, *_: (0, 0, give(t)))
    keep_spec = pl.BlockSpec((2, half, HD), lambda t, *_: (0, 0, keep(t)))
    part_spec = pl.BlockSpec((2, half, HD), lambda t, *_: (0, 0, t))
    grid_spec = pltpu.PrefetchScalarGridSpec(
        num_scalar_prefetch=4,
        grid=(groups,),
        in_specs=[row_spec, row_spec, key_spec, key_spec, pl.BlockSpec((1, length), lambda t, *_: (0, 0))],
        out_specs=[row_spec, row_spec, give_spec, keep_spec, part_spec],
        scratch_shapes=[
            pltpu.VMEM((2, length, length // 4), jnp.float32),
            pltpu.VMEM((length, HD), jnp.float32),
            pltpu.VMEM((length, HD), jnp.float32),
        ],
    )
    part = (2, half, split * HD)
    return pl.pallas_call(
        functools.partial(tail_kernel, split, per_group),
        grid_spec=grid_spec,
        out_shape=[jax.ShapeDtypeStruct(q.shape, jnp.bfloat16)] * 2
        + [
            jax.ShapeDtypeStruct(part, jnp.bfloat16),
            jax.ShapeDtypeStruct(part, jnp.float32),
            jax.ShapeDtypeStruct((2, half, groups * HD), jnp.float32),
        ],
        cost_estimate=attention_cost(half, half, per_group * groups),
        name="tail_rows",
    )(handed, position, side, place, q, do, k, v, seg)


def head_call(side, place, q, do, k, v, seg, groups, part, out, dq):
    length, row_width = q.shape
    half = length // 2
    width = row_width // groups
    per_group = width // HD
    split = groups // 2
    group, give, keep = key_places(split)
    row_spec = pl.BlockSpec((half, width), lambda t, s, n: (0, group(t, s)))
    key_spec = pl.BlockSpec((half, HD), lambda t, s, n: (0, group(t, s)))
    give_spec = pl.BlockSpec((2, half, HD), lambda t, *_: (0, 0, give(t)))
    keep_spec = pl.BlockSpec((2, half, HD), lambda t, *_: (0, 0, keep(t)))
    part_spec = pl.BlockSpec((2, half, HD), lambda t, *_: (0, 0, t))
    grid_spec = pltpu.PrefetchScalarGridSpec(
        num_scalar_prefetch=2,
        grid=(groups,),
        in_specs=[row_spec, row_spec, key_spec, key_spec, pl.BlockSpec((1, half), lambda t, *_: (0, 0)), part_spec]
        + [any_spec()] * 2,
        out_specs=[row_spec, row_spec, give_spec, keep_spec],
        scratch_shapes=[
            pltpu.VMEM((2, half, half // 2), jnp.float32),
            pltpu.VMEM((half, HD), jnp.float32),
            pltpu.VMEM((half, HD), jnp.float32),
        ],
    )
    part_shape = (2, half, split * HD)
    return pl.pallas_call(
        functools.partial(head_kernel, split, per_group),
        grid_spec=grid_spec,
        out_shape=[jax.ShapeDtypeStruct(q.shape, jnp.bfloat16)] * 2
        + [jax.ShapeDtypeStruct(part_shape, jnp.bfloat16), jax.ShapeDtypeStruct(part_shape, jnp.float32)],
        input_output_aliases={8: 0, 9: 1},
        cost_estimate=attention_cost(half, half, per_group * groups),
        name="head_rows",
    )(side, place, q, do, k, v, seg, part, out, dq)


def sum_kernel(own_ref, other_ref, out_ref):
    width = own_ref.shape[-1]
    for part in range(2):
        out_ref[:, part * width : (part + 1) * width] = (own_ref[part] + other_ref[part]).astype(jnp.bfloat16)


def sum_call(own, other):
    parts, rows, width = own.shape
    return pl.pallas_call(
        sum_kernel,
        in_specs=[pl.BlockSpec(memory_space=pltpu.VMEM)] * 2,
        out_specs=pl.BlockSpec(memory_space=pltpu.VMEM),
        out_shape=jax.ShapeDtypeStruct((rows, parts * width), jnp.bfloat16),
        compiler_params=pltpu.CompilerParams(vmem_limit_bytes=GRANT),
        name="sum_keys",
    )(own, other)


ACTIVE, START, FIRST, SKIP = range(4)
PACKED, LAST, KEYS, COUNTS, PART, SIZE, NUMBERS = 0, 4, 8, 12, 16, 17, 24
SETS = 4
SIZES = 3


def sender_sets(halfway):
    return [[i for i in range(halfway) if i * SETS // halfway == part] for part in range(SETS)]


def column_loads(sizes, aside):
    def keys(size):
        return 1 if size == 0 else 2

    first, second, third = sizes
    own = 2 * (1 - aside) + 4 * second + 2 + keys(second)
    other = 2 * aside + 4 * (first + third) + keys(first) + keys(third)
    return max(own, other)


def aside_choice(sizes):
    return int(column_loads(sizes, 1) < column_loads(sizes, 0))


def branch_menu():
    choices = list(itertools.product(range(SIZES), repeat=SETS - 1))

    def longest(sizes):
        return min(column_loads(sizes, 0), column_loads(sizes, 1))

    def widened(sizes):
        able = [
            other
            for other in choices
            if all(x >= y for x, y in zip(other, sizes)) and longest(other) <= longest(sizes)
        ]
        return max(able, key=lambda other: (sum(other), other))

    menu = sorted({widened(sizes) for sizes in choices})
    return menu, [menu.index(widened(sizes)) for sizes in choices]


def numbers_kernel(halfway, window, handed_ref, position_ref, seg_ref, place_ref, branch_ref):
    position = position_ref[0]
    receiver = position >= halfway
    moved = handed_ref[jnp.maximum(position - halfway, 0)]
    added = jnp.where(receiver, moved, 0)
    live = jnp.sum(jnp.where(seg_ref[...] >= 0, 1.0, 0.0)).astype(jnp.int32)
    offset = packed_offset(moved, window)
    top = 4 * window - window - PAD
    late = live + added - window + offset
    place_ref[PACKED + ACTIVE] = receiver.astype(jnp.int32)
    place_ref[PACKED + START] = jnp.minimum(live, top) // PAD
    place_ref[PACKED + FIRST] = live
    place_ref[PACKED + SKIP] = 2 * window - moved - offset
    place_ref[LAST + ACTIVE] = (receiver & (added > window)).astype(jnp.int32)
    place_ref[LAST + START] = jnp.minimum(late, top) // PAD
    place_ref[LAST + FIRST] = late
    place_ref[LAST + SKIP] = offset
    place_ref[KEYS] = live
    place_ref[KEYS + 1] = added
    place_ref[KEYS + 2] = 4 * window - handed_ref[position]
    partner = jnp.maximum(position - halfway, 0)
    part = partner * SETS // halfway
    place_ref[PART] = part
    choice = 0
    for members in sender_sets(halfway)[1:]:
        most = handed_ref[members[0]]
        for i in members[1:]:
            most = jnp.maximum(most, handed_ref[i])
        size = (most > window).astype(jnp.int32) + (most > window + window // 2).astype(jnp.int32)
        choice = choice * SIZES + size
    menu, branch_of = branch_menu()
    branch = 0
    own_size = 0
    for number, index in enumerate(branch_of):
        branch = jnp.where(choice == number, index, branch)
    for index, sizes in enumerate(menu):
        for member, size in enumerate(sizes):
            own_size = jnp.where((branch == index) & (part == member + 1), size, own_size)
    branch_ref[0] = branch
    place_ref[SIZE] = own_size
    seg = seg_ref[...].astype(jnp.float32)
    slot = lax.broadcasted_iota(jnp.int32, seg.shape, 1)
    for block in range(4):
        number = jnp.sum(jnp.where(slot == block * window, seg, 0.0))
        begin = jnp.sum(jnp.where((seg >= 0) & (seg < number), 1.0, 0.0)).astype(jnp.int32)
        place_ref[COUNTS + block] = jnp.where(number >= 0, block + 1 - begin // window, 0)


def numbers_call(handed, position, seg, halfway):
    smem = pl.BlockSpec(memory_space=pltpu.SMEM)
    return pl.pallas_call(
        functools.partial(numbers_kernel, halfway, seg.shape[1] // 4),
        in_specs=[smem, smem, pl.BlockSpec(memory_space=pltpu.VMEM)],
        out_specs=[smem, smem],
        out_shape=[jax.ShapeDtypeStruct((NUMBERS,), jnp.int32), jax.ShapeDtypeStruct((1,), jnp.int32)],
        name="place_numbers",
    )(handed, position, seg)


def pick_matrix(place_ref, base, rows, window):
    row = lax.broadcasted_iota(jnp.int32, (rows, window), 0)
    source = lax.broadcasted_iota(jnp.int32, (rows, window), 1)
    skip = place_ref[base + SKIP]
    offset = place_ref[base + FIRST] - place_ref[base + START] * PAD - skip
    chosen = (row - source == offset) & (source >= skip)
    return jnp.where(chosen, 1.0, 0.0).astype(jnp.bfloat16)


def row_copies(place_ref, base, pairs, sems, first_sem, rows, inward):
    begin = pl.multiple_of(place_ref[base + START] * PAD, PAD)
    copies = []
    for i, (ref, buf, columns) in enumerate(pairs):
        outer = ref.at[pl.ds(begin, rows), columns]
        inner = buf.at[:, columns]
        source, target = (outer, inner) if inward else (inner, outer)
        copies.append(pltpu.make_async_copy(source, target, sems.at[first_sem + i]))
    return copies


def place_packed_kernel(groups, per_group, place_ref, side_ref, pack, mine, other, old_out, old_dq, out_ref, dq_ref, out_buf, dq_buf, pack_ref, mine_ref, other_ref, sems):
    window = pack_ref.shape[0]
    rows = out_buf.shape[0]
    every = slice(0, out_buf.shape[1])

    @pl.when(place_ref[PACKED + ACTIVE] == 1)
    def _():
        inputs = [
            pltpu.make_async_copy(mine, mine_ref, sems.at[2]),
            pltpu.make_async_copy(other, other_ref, sems.at[3]),
            pltpu.make_async_copy(pack, pack_ref, sems.at[4]),
        ]
        start_all(inputs)
        reads = row_copies(place_ref, PACKED, [(out_ref, out_buf, every), (dq_ref, dq_buf, every)], sems, 0, rows, True)
        start_all(reads)
        pick = pick_matrix(place_ref, PACKED, rows, window)
        wait_all(inputs)
        first = lax.broadcasted_iota(jnp.int32, (window, window), 0)
        second = lax.broadcasted_iota(jnp.int32, (window, window), 1)
        writes = []
        for g in range(groups):
            own = heads_of(mine_ref, g)
            swapped = heads_of(other_ref, g)
            k = jnp.where(side_ref[0] == 0, own, swapped)
            v = jnp.where(side_ref[0] == 0, swapped, own)
            k_f = k.astype(jnp.float32)
            v_t = jnp.transpose(v)
            outs = []
            grads = []
            for j in range(per_group):
                head = g * per_group + j
                packed = pack_ref[:, head * window : (head + 1) * window].astype(jnp.float32)
                w = jnp.where(first <= second, packed, 0.0).astype(jnp.bfloat16)
                ds = jnp.where(first > second, packed, 0.0)
                outs.append(jnp.transpose(dot(v_t, w, NN)).astype(jnp.bfloat16))
                total = jnp.sum(ds, axis=1, keepdims=True)
                dq = (dot(ds.astype(jnp.bfloat16), k, NN) - total * k_f) * HD**-0.5
                grads.append(dq.astype(jnp.bfloat16))
            moved_out = dot(pick, jnp.concatenate(outs, axis=1), NN).astype(jnp.bfloat16)
            moved_dq = dot(pick, jnp.concatenate(grads, axis=1), NN).astype(jnp.bfloat16)
            if g == 0:
                wait_all(reads)
            columns = slice(g * per_group * HD, (g + 1) * per_group * HD)
            out_buf[:, columns] += moved_out
            dq_buf[:, columns] += moved_dq
            writes += row_copies(
                place_ref, PACKED, [(out_ref, out_buf, columns), (dq_ref, dq_buf, columns)], sems, 5 + 2 * g, rows, False
            )
            start_all(writes[-2:])
        wait_all(writes)


def place_packed_call(place, side, arrays, out, dq, groups):
    window = arrays[0].shape[0]
    rows = window + PAD
    row_width = out.shape[1]
    per_group = row_width // (groups * HD)
    count = 2 + len(arrays)
    return pl.pallas_call(
        functools.partial(place_packed_kernel, groups, per_group),
        in_specs=[pl.BlockSpec(memory_space=pltpu.SMEM)] * 2 + [any_spec()] * (len(arrays) + 2),
        out_specs=[any_spec()] * 2,
        out_shape=[jax.ShapeDtypeStruct(out.shape, out.dtype)] * 2,
        scratch_shapes=[pltpu.VMEM((rows, row_width), jnp.bfloat16)] * 2
        + [
            pltpu.VMEM((window, groups * per_group * window), jnp.bfloat16),
            pltpu.VMEM((window, groups * HD), jnp.bfloat16),
            pltpu.VMEM((window, groups * HD), jnp.bfloat16),
            pltpu.SemaphoreType.DMA((5 + 2 * groups,)),
        ],
        input_output_aliases={count: 0, count + 1: 1},
        cost_estimate=pl.CostEstimate(
            flops=8 * rows * window * row_width, transcendentals=0, bytes_accessed=12 * rows * row_width
        ),
        compiler_params=pltpu.CompilerParams(vmem_limit_bytes=GRANT),
        name="place_packed",
    )(place, side, *arrays, out, dq)


def finish_kernel(groups, place_ref, first_ref, second_ref, part_ref, detour_ref, short_ref, full_ref, long_keys_ref, short_keys_ref, keep_ref, other_ref, tail_ref, old_out, old_dq, out_ref, dq_ref, dk_ref, dv_ref, out_buf, dq_buf, rows_buf, keys_buf, arrived_buf, keep_buf, other_buf, tail_buf, sems):
    window = rows_buf.shape[0]
    rows = out_buf.shape[0]
    width = out_buf.shape[1] // groups
    half, both = tail_buf.shape
    part = both // 2
    quarter = first_ref.shape[1]
    size = short_ref.shape[0]
    few = short_keys_ref.shape[0]
    in_first = place_ref[PART] == 0
    short = jnp.logical_not(in_first) & (place_ref[SIZE] == 1)
    full = jnp.logical_not(in_first) & (place_ref[SIZE] == 2)
    many = in_first | (place_ref[SIZE] > 0)
    active = place_ref[LAST + ACTIVE] == 1
    receiver = place_ref[PACKED + ACTIVE] == 1
    every = slice(0, out_buf.shape[1])

    reads = row_copies(place_ref, LAST, [(out_ref, out_buf, every), (dq_ref, dq_buf, every)], sems, 0, rows, True)
    part_copies = [
        pltpu.make_async_copy(ref, rows_buf.at[:, i * quarter : (i + 1) * quarter], sems.at[sem])
        for i, (ref, sem) in enumerate(((first_ref, 2), (second_ref, 3), (part_ref, 6), (detour_ref, 9 + 2 * groups)))
    ]
    short_copy = pltpu.make_async_copy(short_ref, rows_buf.at[window - size :, :], sems.at[2])
    full_copy = pltpu.make_async_copy(full_ref, rows_buf, sems.at[2])
    many_copy = pltpu.make_async_copy(long_keys_ref, arrived_buf, sems.at[7])
    few_copy = pltpu.make_async_copy(short_keys_ref, arrived_buf.at[half - few :, :], sems.at[7])
    key_copies = [
        pltpu.make_async_copy(keep_ref, keep_buf, sems.at[4]),
        pltpu.make_async_copy(other_ref, other_buf, sems.at[5]),
        pltpu.make_async_copy(tail_ref, tail_buf, sems.at[8]),
    ]
    start_all(key_copies)

    @pl.when(receiver)
    def _():
        pl.when(many)(lambda: many_copy.start())

        @pl.when(jnp.logical_not(many))
        def _():
            arrived_buf[: half - few, :] = jnp.zeros((half - few, both), arrived_buf.dtype)
            few_copy.start()

    @pl.when(active)
    def _():
        start_all(reads)

        pl.when(in_first)(lambda: start_all(part_copies))

        @pl.when(short)
        def _():
            rows_buf[: window - size, :] = jnp.zeros((window - size, rows_buf.shape[1]), rows_buf.dtype)
            short_copy.start()

        @pl.when(full)
        def _():
            full_copy.start()

    wait_all(key_copies)
    limit = place_ref[KEYS + 2]
    own_row = lax.broadcasted_iota(jnp.int32, (half, both), 0) + half
    tail = tail_buf[...]
    keys_buf[half:, :] = jnp.where(own_row < limit, tail, jnp.zeros_like(tail))
    for i in range(2):
        columns = slice(i * part, (i + 1) * part)
        keys_buf[:half, columns] = (keep_buf[i] + other_buf[i]).astype(keys_buf.dtype)

    @pl.when(receiver)
    def _():
        pl.when(many)(lambda: many_copy.wait())
        pl.when(jnp.logical_not(many))(lambda: few_copy.wait())
        length = 2 * half
        row = lax.broadcasted_iota(jnp.int32, (length, half), 0)
        source = lax.broadcasted_iota(jnp.int32, (length, half), 1)
        missing = half - place_ref[KEYS + 1]
        chosen = (row - source == place_ref[KEYS] - missing) & (source >= missing)
        pick = jnp.where(chosen, 1.0, 0.0).astype(jnp.bfloat16)
        keys_buf[...] += dot(pick, arrived_buf[...], NN).astype(keys_buf.dtype)

    key_writes = [
        pltpu.make_async_copy(keys_buf.at[:, :part], dk_ref, sems.at[4]),
        pltpu.make_async_copy(keys_buf.at[:, part:], dv_ref, sems.at[5]),
    ]
    start_all(key_writes)

    @pl.when(active)
    def _():
        pl.when(in_first)(lambda: wait_all(part_copies))
        pl.when(short)(lambda: short_copy.wait())
        pl.when(full)(lambda: full_copy.wait())
        wait_all(reads)
        pick = pick_matrix(place_ref, LAST, rows, window)
        writes = []
        for g in range(groups):
            columns = slice(g * width, (g + 1) * width)
            moved = dot(pick, rows_buf[:, 2 * g * width : 2 * (g + 1) * width], NN).astype(jnp.bfloat16)
            out_buf[:, columns] += moved[:, :width]
            dq_buf[:, columns] += moved[:, width:]
            writes += row_copies(
                place_ref, LAST, [(out_ref, out_buf, columns), (dq_ref, dq_buf, columns)], sems, 9 + 2 * g, rows, False
            )
            start_all(writes[-2:])
        wait_all(writes)

    wait_all(key_writes)


def finish_call(place, arrived, keys, out, dq, groups):
    length, row_width = out.shape
    half = length // 2
    window = half // 2
    rows = window + PAD
    both = keys[-1].shape[1]
    keys_shape = jax.ShapeDtypeStruct((length, both // 2), jnp.bfloat16)
    count = 1 + len(arrived) + len(keys)
    return pl.pallas_call(
        functools.partial(finish_kernel, groups),
        in_specs=[pl.BlockSpec(memory_space=pltpu.SMEM)] + [any_spec()] * (count + 1),
        out_specs=[any_spec()] * 4,
        out_shape=[jax.ShapeDtypeStruct(out.shape, out.dtype)] * 2 + [keys_shape] * 2,
        scratch_shapes=[pltpu.VMEM((rows, row_width), jnp.bfloat16)] * 2
        + [
            pltpu.VMEM((window, 2 * row_width), jnp.bfloat16),
            pltpu.VMEM((length, both), jnp.bfloat16),
            pltpu.VMEM((half, both), jnp.bfloat16),
            pltpu.VMEM((2, half, both // 2), jnp.float32),
            pltpu.VMEM((2, half, both // 2), jnp.bfloat16),
            pltpu.VMEM((half, both), jnp.bfloat16),
            pltpu.SemaphoreType.DMA((10 + 2 * groups,)),
        ],
        input_output_aliases={count: 0, count + 1: 1},
        compiler_params=pltpu.CompilerParams(vmem_limit_bytes=GRANT),
        name="finish",
    )(place, *arrived, *keys, out, dq)


def unfilled(shape, dtype):
    return pl.pallas_call(
        lambda ref: None, out_specs=any_spec(), out_shape=jax.ShapeDtypeStruct(shape, dtype), name="unfilled"
    )()


def program(queries, key_states, value_states, out_grad, seg_ids, handed):
    length = seg_ids.shape[0]
    groups = key_states.shape[1] // HD
    q = queries[0]
    do = out_grad[0]
    index = lax.axis_index("dp").astype(jnp.int32)
    devices = lax.axis_size("dp")
    halfway = devices // 2
    seg = seg_ids.reshape(1, length)
    position = index.reshape(1)
    side = lax.axis_index("sub").astype(jnp.int32).reshape(1)
    onward = [(i, i + halfway) for i in range(halfway)]
    across = [(0, 1), (1, 0)]

    def moved(block, axis, route):
        return lax.ppermute(block, axis, route)

    own = (q, do, key_states, value_states, seg, groups)
    packed, window_keys = packed_call(handed, position, side, *own)
    packed_in = moved(packed, "dp", onward)
    mine = moved(window_keys, "dp", onward)
    last = last_rows_call(handed, position, *own)
    sets = sender_sets(halfway)

    def route_of(parts):
        return [(i, i + halfway) for part in parts for i in part]

    near = len(sets[0])
    quarter = last.shape[1] // 4
    aside = moved(last[:, 2 * quarter :], "dp", [(i, i + near) for i in sets[0]])
    around = [(i + near, i + halfway) for i in sets[0]]
    first_in = moved(last[:, :quarter], "dp", route_of(sets[:1]))
    place, branch_number = numbers_call(handed, position, seg, halfway)

    out, dq, give_tail, keep_tail, part = tail_call(handed, position, side, place, *own)
    other_tail = moved(give_tail, "sub", across)
    out, dq, give_head, keep_head = head_call(side, place, *own, part, out, dq)
    other_head = moved(give_head, "sub", across)
    other = moved(mine, "sub", across)
    second_in = moved(last[:, quarter : 2 * quarter], "dp", route_of(sets[:1]))
    detour_in = moved(aside[:, quarter:], "dp", around)
    tail_sum = sum_call(keep_tail, other_tail)
    out, dq = place_packed_call(place, side, (packed_in, mine, other), out, dq, groups)

    window = last.shape[0]

    def branch(sizes):
        def sent(block, parts):
            if parts:
                return lax.ppermute(block, "dp", route_of(parts))
            return unfilled(block.shape, block.dtype)

        def of_size(*wanted):
            return [part for part, size in zip(sets[1:], sizes) if size in wanted]

        def run(rows, other_rows, grads):
            full = sent(rows, of_size(2))
            short = sent(rows[window // 2 :], of_size(1))
            if aside_choice(sizes):
                part = lax.ppermute(other_rows[:, :quarter], "dp", around)
            else:
                part = sent(rows[:, 2 * quarter : 3 * quarter], sets[:1])
            long_keys = sent(grads, sets[:1] + of_size(1, 2))
            short_keys = sent(grads[window:], of_size(0))
            return part, short, full, long_keys, short_keys

        return run

    branches = [branch(sizes) for sizes in branch_menu()[0]]
    part_in, *others_in = lax.switch(branch_number[0], branches, last, aside, tail_sum)
    short_in, full_in, *keys_in = others_in
    out, dq, dk, dv = finish_call(
        place, (first_in, second_in, part_in, detour_in, short_in, full_in), (*keys_in, keep_head, other_head, tail_sum), out, dq, groups
    )
    return out[None], dq[None], dk, dv


def solution(mesh):
    return jax.shard_map(
        program,
        mesh=mesh,
        in_specs=(
            P("sub", "dp", "head"),
            P("dp", "head"),
            P("dp", "head"),
            P("sub", "dp", "head"),
            P("dp"),
            P(),
        ),
        out_specs=(
            P("sub", "dp", "head"),
            P("sub", "dp", "head"),
            P("dp", ("head", "sub")),
            P("dp", ("head", "sub")),
        ),
        check_vma=False,
    )
```
